256 devices in a mesh: dp: 4 (over z_hi, core), ctx: 16 (over z_lo, y), tp: 4 (over x).
Axes of the slice: x: 4, y: 4, z: 8 (z_hi: 2, z_lo: 4; z = z_hi * 4 + z_lo), core: 2. Of those that a mesh axis runs over, the one named last changes fastest.
Arguments:
- teacher_part: bfloat16 [4, 4, 4096, 8192], P('dp', 'tp', 'ctx'), may hold values from -8 to 8
- student_in: bfloat16 [4, 4096, 4096], P('dp', 'ctx'), may hold values from -24 to 24
- out_proj: bfloat16 [4096, 4096], P('ctx', 'tp'), may hold values from -0.09375 to 0.09375
- segment_ids: int32 [4, 4096], P('dp'), may hold values from 0 to 7, never falling along the last dimension, each value on 1 to 1024 neighbouring positions
- valid_count: int32 [4], P('dp'), may hold values from 256 to 4096, as said below
Outputs:
- doc_loss: float32 [4], P('dp')
- wo_grad: float32 [4096, 4096], P('ctx', 'tp')
- state_grad: float32 [4, 4096, 4096], P('dp', 'ctx', 'tp')
The draws below stay inside these ranges and needn't reach their ends.
Inputs may be any that keep to these rules, and one draw needn't show every extreme that they name: `valid_count`: one document in every draw is valid at all 4096 positions. `segment_ids`: segment numbers never fall along a document.
All inputs are finite; a program needn't handle non-finite values.
Results may differ from the reference program's by a relative error of at most 0.019.
The reference program's roundings to bfloat16 on the way (of `teacher_hidden`, `student_hidden`, `score_grad` and `hidden_grad`) count: a program that leaves them out, or rounds other values in their place, can miss the bound.
Values may be sent and summed in bfloat16 or wider, within the bound.
A program may use at most 64 MiB of HBM per device.

```python
import math
import jax
import jax.numpy as jnp
import numpy as np
from jax import lax

DT = 8192
DS = 4096
HEADS = 32
TOK_DEV = 256
SEQ = 4096
DOCS = 4
SEGS = 8
SEG_MOST = 1024
N_CTX = 16
N_TP = 4


def draw_teacher_part(key, part):
    key_base, key_scale = jax.random.split(key, 2)
    shape = (DOCS, N_TP, SEQ, DT)
    base = jnp.clip(jax.random.normal(key_base, shape, jnp.float32), -5.0, 5.0)
    row_scale = jnp.exp(jax.random.uniform(key_scale, (DOCS, 1, SEQ, 1), jnp.float32, math.log(0.4), math.log(4.0)))
    return (0.25 * base * row_scale).astype(jnp.bfloat16)


def draw_student_input(key, part):
    key_base, key_scale = jax.random.split(key, 2)
    shape = (DOCS, SEQ, DS)
    base = jnp.clip(jax.random.normal(key_base, shape, jnp.float32), -5.0, 5.0)
    row_scale = jnp.exp(jax.random.uniform(key_scale, (DOCS, SEQ, 1), jnp.float32, math.log(0.4), math.log(4.0)))
    return base * row_scale


def draw_student_in(key, part):
    return draw_student_input(key, part).astype(jnp.bfloat16)


def draw_valid_count(key, part):
    key_count, key_full = jax.random.split(key, 2)
    counts = jax.random.randint(key_count, (DOCS,), TOK_DEV, SEQ + 1)
    full_doc = jax.random.randint(key_full, (), 0, DOCS)
    return jnp.where(jnp.arange(DOCS, dtype=jnp.int32) == full_doc, SEQ, counts).astype(jnp.int32)


def levels(rng, extent, cuts, smallest, largest):
    factor_of, own = 1.0, jax.random.fold_in(rng, 6)
    for dim, shards_of in cuts:
        heights = jnp.exp(jax.random.uniform(jax.random.fold_in(own, dim), (shards_of,), jnp.float32, smallest / len(cuts), largest / len(cuts)))
        factor_of = factor_of * jnp.repeat(heights, extent[dim] // shards_of).reshape([-1 if axis == dim else 1 for axis in range(len(extent))])
    return factor_of


def split_up(count, total, limit, slope):
    portions = [(1 << 20) // math.isqrt(grade ** slope) + 1 for grade in range(2, count + 1)]
    spare, given = total - limit - (count - 1), [1] * (count - 1)
    while spare > 0:
        candidates = [i for i in range(count - 1) if given[i] < limit]
        whole, left = sum([portions[i] for i in candidates]), spare
        for i in candidates:
            more = min(limit - given[i], max(1, left * portions[i] // whole), spare)
            given[i] = given[i] + more
            spare = spare - more
    return np.array([limit] + given)


def ragged_sizes(key, amount, total, reach, skew):
    if amount == 2:
        one = jax.random.randint(key, (), max(1, total - reach), min(reach, total - 1) + 1)
        return jnp.stack([one, total - one])
    lengths = jnp.asarray(split_up(amount, total, reach, skew), jnp.int32)
    pairs = (amount - 1) // 2
    donor, taker = lengths[1:1 + 2 * pairs:2], lengths[2:2 + 2 * pairs:2]
    margin = jnp.minimum(donor - 1, reach - taker)
    passed = jax.random.randint(jax.random.fold_in(key, 1), (pairs,), 0, 1 << 20) % (margin + 1)
    lengths = lengths.at[1:1 + 2 * pairs:2].set(donor - passed).at[2:2 + 2 * pairs:2].set(taker + passed)
    return lengths[jax.random.permutation(jax.random.fold_in(key, 2), amount)]


def bell_draw(own_key, dims, scale, bound, cuts=(), kind=jnp.bfloat16):
    gain = levels(own_key, dims, cuts, -0.22, 0.18) if cuts else 1.0
    entries = jax.random.normal(own_key, dims, jnp.float32) * scale * gain
    return jnp.minimum(jnp.maximum(entries, -bound), bound).astype(kind)


def setup_inputs(seed: int = 0) -> dict:
    splits = jax.random.split(jax.random.key(seed), 6)
    teacher_part = draw_teacher_part(jax.random.fold_in(splits[5], 71), 0)
    student_in = draw_student_in(jax.random.fold_in(splits[5], 71), 0)
    out_proj = bell_draw(splits[2], (DS, DS), DS ** -0.5, 0.09375, ((0, 16), (1, 4)))
    segment_ids = jax.vmap(lambda own: jnp.searchsorted(jnp.cumsum(ragged_sizes(own, SEGS, SEQ, SEG_MOST, 1)), jnp.arange(SEQ), side="right"))(jax.random.split(splits[3], DOCS)).reshape((DOCS, SEQ)).astype(jnp.int32)
    valid_count = draw_valid_count(jax.random.fold_in(splits[5], 71), 0)
    return {"teacher_part": teacher_part, "student_in": student_in, "out_proj": out_proj, "segment_ids": segment_ids, "valid_count": valid_count}


masked_score = -1e+30

def log_probs(scores, allowed):
    scores = jnp.where(allowed[None, :, :], scores, masked_score)
    top = lax.optimization_barrier(jnp.max(scores, axis=-1, keepdims=True))
    shifted = scores - top
    return shifted - jnp.log(lax.optimization_barrier(jnp.sum(jnp.exp(shifted), axis=-1, keepdims=True)))

def window_terms(teacher_query, teacher_keys, student_query, student_keys, allowed, live):
    length = teacher_query.shape[0]
    teacher_qh = teacher_query.reshape(length, HEADS, -1).astype(jnp.float32)
    teacher_kh = teacher_keys.reshape(2 * length, HEADS, -1).astype(jnp.float32)
    student_qh = student_query.reshape(length, HEADS, -1).astype(jnp.float32)
    student_kh = student_keys.reshape(2 * length, HEADS, -1).astype(jnp.float32)
    teacher_scale = 1.0 / math.sqrt(teacher_qh.shape[-1])
    student_scale = 1.0 / math.sqrt(student_qh.shape[-1])
    teacher_scores = jnp.einsum('qhd,khd->hqk', teacher_qh, teacher_kh, precision=lax.Precision.HIGHEST) * teacher_scale
    student_scores = jnp.einsum('qhd,khd->hqk', student_qh, student_kh, precision=lax.Precision.HIGHEST) * student_scale
    teacher_logp = log_probs(teacher_scores, allowed)
    student_logp = log_probs(student_scores, allowed)
    teacher_prob = jnp.exp(teacher_logp)
    student_prob = jnp.exp(student_logp)
    divergence = lax.optimization_barrier(jnp.sum(teacher_prob * (teacher_logp - student_logp), axis=-1))
    loss_part = jnp.sum(divergence * live[None, :]) / HEADS
    grad_scale = live[None, :, None] * (student_scale / HEADS)
    score_grad = ((student_prob - teacher_prob) * grad_scale).astype(jnp.bfloat16).astype(jnp.float32)
    query_grad = jnp.einsum('hqk,khd->qhd', score_grad, student_kh, precision=lax.Precision.HIGHEST).reshape(length, -1)
    key_grad = jnp.einsum('hqk,qhd->khd', score_grad, student_qh, precision=lax.Precision.HIGHEST).reshape(2 * length, -1)
    return (loss_part, query_grad, key_grad)

def reference(teacher_part, student_in, out_proj, segment_ids, valid_count):
    unscale = HEADS * math.sqrt(DS // HEADS)

    def document_terms(index):
        teacher_doc = teacher_part[index]
        student_doc = student_in[index]
        segments = segment_ids[index]
        valid_limit = valid_count[index]
        teacher_hidden = lax.optimization_barrier(jnp.sum(teacher_doc.astype(jnp.float32), axis=0)).astype(jnp.bfloat16)
        student_hidden = jnp.dot(student_doc, out_proj, preferred_element_type=jnp.float32).astype(jnp.bfloat16)
        teacher_padded = jnp.concatenate([jnp.zeros((TOK_DEV, DT), jnp.bfloat16), teacher_hidden], 0)
        student_padded = jnp.concatenate([jnp.zeros((TOK_DEV, DS), jnp.bfloat16), student_hidden], 0)
        segment_padded = jnp.concatenate([jnp.full((TOK_DEV,), -1, jnp.int32), segments.astype(jnp.int32)], 0)

        def one_window(window):
            start = (window * TOK_DEV).astype(jnp.int32)
            teacher_query = lax.dynamic_slice_in_dim(teacher_hidden, start, TOK_DEV, 0)
            teacher_keys = lax.dynamic_slice_in_dim(teacher_padded, start, 2 * TOK_DEV, 0)
            student_query = lax.dynamic_slice_in_dim(student_hidden, start, TOK_DEV, 0)
            student_keys = lax.dynamic_slice_in_dim(student_padded, start, 2 * TOK_DEV, 0)
            query_segment = lax.dynamic_slice_in_dim(segments.astype(jnp.int32), start, TOK_DEV, 0)
            key_segment = lax.dynamic_slice_in_dim(segment_padded, start, 2 * TOK_DEV, 0)
            query_position = start + jnp.arange(TOK_DEV, dtype=jnp.int32)
            key_position = start - TOK_DEV + jnp.arange(2 * TOK_DEV, dtype=jnp.int32)
            allowed = (key_segment[None, :] == query_segment[:, None]) & (key_position[None, :] < valid_limit)
            live = jnp.where(query_position < valid_limit, 1.0, 0.0).astype(jnp.float32)
            return window_terms(teacher_query, teacher_keys, student_query, student_keys, allowed, live)
        losses, query_grads, key_grads = lax.map(one_window, jnp.arange(N_CTX, dtype=jnp.int32))
        own_grad = query_grads + key_grads[:, TOK_DEV:]
        from_next = jnp.concatenate([key_grads[1:, :TOK_DEV], jnp.zeros((1, TOK_DEV, DS), jnp.float32)], 0)
        hidden_grad = (own_grad + from_next).reshape(SEQ, DS).astype(jnp.bfloat16)
        doc_grad = jnp.dot(student_doc.T, hidden_grad, preferred_element_type=jnp.float32)
        scaled = hidden_grad.astype(jnp.float32) * unscale
        return (jnp.sum(losses), doc_grad, scaled)
    doc_loss, doc_grads, state_grad = lax.map(document_terms, jnp.arange(DOCS, dtype=jnp.int32))
    return (doc_loss, lax.optimization_barrier(jnp.sum(doc_grads, axis=0)), state_grad)
```

```python
import math

import jax
import jax.numpy as jnp
from jax import lax
from jax.experimental import pallas as pl
from jax.experimental.pallas import tpu as pltpu
from jax.sharding import PartitionSpec as P

DS = 4096
HEADS = 32
MESH = pl.DeviceIdType.MESH
F32 = jnp.float32
BF16 = jnp.bfloat16
NEG = -1e30
UNSCALE = HEADS * math.sqrt(DS // HEADS)
T_SCALE = 1.0 / math.sqrt(256)
S_SCALE = 1.0 / math.sqrt(128)
G_SCALE = S_SCALE / HEADS
N_SEM = 224


def dot_nn(a, b):
    return lax.dot_general(a, b, (((1,), (0,)), ((), ())), preferred_element_type=F32)


def dot_nt(a, b):
    return lax.dot_general(a, b, (((1,), (1,)), ((), ())), preferred_element_type=F32)


def turned(a):
    return jnp.transpose(a.astype(F32)).astype(BF16)


def kernel(
    tpart, xin, win, seg_ref, valid_ref,
    ht_out, gt_out, loss_out,
    xb, wb, acc,
    t_own, t_fp, t_fm, r1p, r1m, rdp, rdm, r2p, r2m, tt, tx,
    ss, so, sx, st, sxt,
    mo, mp, mn, zt, lt, zs, st_d, st_n, rs_d, rs_n,
    hacc, hsend, hrecv, ho,
    gb, p1p, p1m, pdp, pdm, p2p, p2m, qb, q1p, q1m, qdp, qdm, q2p, q2m, fin, fin_r, gf, gf_r,
    lx, ly, lz,
    send_sem, recv_sem, loc_sem,
):
    dp, ctx, x = lax.axis_index("dp"), lax.axis_index("ctx"), lax.axis_index("tp")
    core, zh, zl, y = dp % 2, dp // 2, ctx // 4, ctx % 4
    z = zh * 4 + zl
    other = 1 - core

    def dev(x_, y_, z_, c_):
        return ((z_ // 4) * 2 + c_, (z_ % 4) * 4 + y_, x_)

    def on_x(k):
        return dev((x + k) % 4, y, z, core)

    def on_y(k):
        return dev(x, (y + k) % 4, z, core)

    def on_z(k):
        return dev(x, y, (z + k) % 8, core)

    def on_zl(k):
        return dev(x, y, zh * 4 + (zl + k) % 4, core)

    mate = dev(x, y, z, other)
    nxt = dev(x, (y + 1) % 4, (z + (y + 1) // 4) % 8, core)
    prv = dev(x, (y + 3) % 4, (z + 7 + (y + 3) // 4) % 8, core)

    partners = [on_x(1), on_x(2), on_x(3), on_y(1), on_y(2), on_y(3), on_z(1), on_z(7), on_z(4)]
    partners += [on_zl(1), on_zl(2), on_zl(3), mate, nxt, prv]

    sems = [0]
    pending = []

    def remote(src, dst, where):
        k = sems[0]
        sems[0] += 1
        return pltpu.make_async_remote_copy(
            src_ref=src, dst_ref=dst, send_sem=send_sem.at[k], recv_sem=recv_sem.at[k],
            device_id=where, device_id_type=MESH,
        )

    def go(copy):
        copy.start()
        pending.append(copy)
        return copy

    locs = [0]

    def local(src, dst):
        k = locs[0]
        locs[0] += 1
        copy = pltpu.make_async_copy(src, dst, loc_sem.at[k])
        copy.start()
        return copy

    x_loc = local(xin, xb.at[core])
    col0 = pl.multiple_of(core * 512, 512)
    w_loc = local(win.at[:, pl.ds(col0, 512)], wb.at[ctx])

    def tcol(block, head):
        return tpart.at[:, pl.ds(pl.multiple_of(block * 2048 + head * 256, 256), 256)]

    fp_loc = [local(tcol((x + 1) % 4, i), t_fp.at[i]) for i in range(4)]
    fm_loc = [local(tcol((x + 3) % 4, 4 + i), t_fm.at[i]) for i in range(4)]
    own_loc = [local(tcol(x, i), t_own.at[i]) for i in range(8)]

    barrier = pltpu.get_barrier_semaphore()
    for where in partners:
        pl.semaphore_signal(barrier, inc=1, device_id=where, device_id_type=MESH)
    pl.semaphore_wait(barrier, len(partners))

    m_s1p = [remote(tcol((x + 2) % 4, i), r1p.at[i], on_x(1)) for i in range(4)]
    m_s1m = [remote(tcol((x + 2) % 4, 4 + i), r1m.at[i], on_x(3)) for i in range(4)]
    m_dp = [remote(tcol((x + 1) % 4, 4 + i), rdp.at[i], on_x(1)) for i in range(4)]
    m_dm = [remote(tcol((x + 3) % 4, i), rdm.at[i], on_x(3)) for i in range(4)]
    m_s2p = [remote(r1p.at[i], r2p.at[i], on_x(1)) for i in range(4)]
    m_s2m = [remote(r1m.at[i], r2m.at[i], on_x(3)) for i in range(4)]
    m_ta = [remote(tt.at[i], tx.at[0, i], nxt) for i in range(4)]
    m_tb = [remote(tt.at[4 + i], tx.at[1, i], prv) for i in range(4)]
    m_x = remote(xin, xb.at[core], mate)

    def block(dy, dz):
        return ((zl + dz) % 4) * 4 + (y + dy) % 4

    def gather_messages(kind):
        base = kind * 128

        def at(dp_, dq_):
            return block(dq_, dp_) if kind == 0 else block(dp_, dq_)

        def to(which, sign):
            on_z_axis = (kind == 0) == (which == "p")
            k = 1 if sign > 0 else -1
            return on_z(k % 8) if on_z_axis else on_y(k % 4)

        def piece(dp_, dq_, part):
            start, size = {"all": (0, 128), "lo": (0, 64), "hi": (64, 64)}[part]
            b = at(dp_, dq_)
            return wb.at[b, pl.ds(base + start, size)]

        def message(dp_, dq_, part, which, sign):
            ref = piece(dp_, dq_, part)
            return remote(ref, ref, to(which, sign))

        own = win.at[pl.ds(base, 128), pl.ds(col0, 512)]

        def first(which, sign):
            return remote(own, piece(0, 0, "all"), to(which, sign))

        return [
            first("p", 1), first("p", -1), first("q", 1), first("q", -1),
            message(-1, 0, "lo", "p", 1), message(1, 0, "hi", "p", -1),
            message(-1, 0, "all", "q", 1), message(-1, 0, "all", "q", -1),
            message(1, 0, "all", "q", 1), message(1, 0, "all", "q", -1),
            message(0, -1, "lo", "q", 1), message(0, 1, "hi", "q", -1),
            message(2, 0, "all", "q", 1), message(2, 0, "all", "q", -1),
            message(-1, -1, "lo", "q", 1), message(-1, 1, "hi", "q", -1),
            message(1, -1, "lo", "q", 1), message(1, 1, "hi", "q", -1),
            message(2, -1, "lo", "q", 1), message(2, 1, "hi", "q", -1),
        ]

    ag = [gather_messages(0), gather_messages(1)]

    def ag_start(*ids):
        for k in ids:
            for kind in (0, 1):
                go(ag[kind][k])

    def ag_wait(*ids):
        for k in ids:
            for kind in (0, 1):
                ag[kind][k].wait_recv()

    go(m_s1p[0]); go(m_s1m[0])
    ag_start(0, 1)
    go(m_s1p[1]); go(m_s1m[1]); go(m_dp[0]); go(m_dm[0])
    ag_start(2, 3)
    go(m_x)

    window = ctx
    valid = valid_ref[0]

    def seg_row(w):
        return seg_ref[:, pl.ds(pl.multiple_of(w * 256, 256), 256)].astype(F32)

    row_own = seg_row(window)
    row_next = seg_row((window + 1) % 16)
    col_own = jnp.transpose(jnp.broadcast_to(row_own, (256, 256)))
    col_prev = jnp.transpose(jnp.broadcast_to(seg_row((window + 15) % 16), (256, 256)))
    key_iota = lax.broadcasted_iota(jnp.int32, (256, 256), 0)
    query_iota = lax.broadcasted_iota(jnp.int32, (256, 256), 1)
    key_own = key_iota + window * 256
    key_prev = key_own - 256
    query_next = query_iota + (window + 1) * 256
    mo[...] = jnp.where((col_own == row_own) & (key_own < valid), 0.0, NEG)
    mp[...] = jnp.where((col_prev == row_own) & (key_prev >= 0) & (key_prev < valid), 0.0, NEG)
    mn[...] = jnp.where((col_own == row_next) & (key_own < valid) & (query_next < 4096), 0.0, NEG)
    lane = lax.broadcasted_iota(jnp.int32, (1, 256), 1)
    live_own = jnp.where(lane + window * 256 < valid, 1.0, 0.0).astype(F32)
    live_next = jnp.where(
        (lane + (window + 1) * 256 < valid) & (lane + (window + 1) * 256 < 4096), 1.0, 0.0
    ).astype(F32)

    acc[...] = jnp.zeros_like(acc)

    def feed(dy, dz):
        b = block(dy, dz)
        xs = xb[:, :, pl.ds(pl.multiple_of(b * 256, 256), 256)].reshape(512, 256)
        acc[...] += dot_nn(xs, wb[b])

    def relay(i):
        m_s1p[i].wait_recv()
        fp_loc[i].wait()
        r1p[i] = (r1p[i].astype(F32) + t_fp[i].astype(F32)).astype(BF16)
        go(m_s2p[i])
        m_s1m[i].wait_recv()
        fm_loc[i].wait()
        r1m[i] = (r1m[i].astype(F32) + t_fm[i].astype(F32)).astype(BF16)
        go(m_s2m[i])

    def settle(i):
        m_s2p[i].wait_recv()
        m_dm[i].wait_recv()
        own_loc[i].wait()
        tt[i] = (t_own[i].astype(F32) + r2p[i].astype(F32) + rdm[i].astype(F32)).astype(BF16)
        go(m_ta[i])
        m_s2m[i].wait_recv()
        m_dp[i].wait_recv()
        own_loc[4 + i].wait()
        tt[4 + i] = (
            t_own[4 + i].astype(F32) + r2m[i].astype(F32) + rdp[i].astype(F32)
        ).astype(BF16)
        go(m_tb[i])

    ag_wait(0, 1)
    ag_start(4, 5, 6, 7, 8, 9)
    relay(0)
    go(m_s1p[2]); go(m_s1m[2]); go(m_dp[1]); go(m_dm[1])
    ag_wait(2, 3)
    ag_start(10, 11)
    relay(1)
    go(m_s1p[3]); go(m_s1m[3]); go(m_dp[2]); go(m_dm[2])
    x_loc.wait()
    w_loc.wait()
    m_x.wait_recv()
    feed(0, 0)
    feed(1, 0)
    feed(-1, 0)
    feed(0, 1)
    feed(0, -1)
    ag_wait(4, 5)
    ag_start(12, 13)
    settle(0)
    ag_wait(6, 7, 8, 9)
    ag_start(14, 15, 16, 17)
    relay(2)
    go(m_dp[3]); go(m_dm[3])
    feed(1, 1)
    feed(-1, 1)
    feed(1, -1)
    feed(-1, -1)
    ag_wait(12, 13)
    ag_start(18, 19)
    settle(1)
    relay(3)
    ag_wait(10, 11)
    feed(2, 0)
    feed(0, 2)
    ag_wait(14, 15, 16, 17)
    feed(2, 1)
    feed(2, -1)
    feed(1, 2)
    feed(-1, 2)
    ag_wait(18, 19)
    feed(2, 2)

    m_so = remote(so, ss.at[pl.ds(core * 4, 4)], mate)

    def half_to(f):
        up = 1 - f
        y_ = (y + 1 + 2 * f) % 4
        z_ = (z + up * ((y + 1) // 4) + f * (7 + (y + 3) // 4)) % 8
        return dev(x, y_, z_, core)

    k_half = sems[0]
    sems[0] += 2

    def half_copy(f):
        return pltpu.make_async_remote_copy(
            src_ref=ss.at[pl.ds(f * 4, 4)], dst_ref=sx.at[f], send_sem=send_sem.at[k_half + f],
            recv_sem=recv_sem.at[k_half + f], device_id=half_to(f), device_id_type=MESH,
        )

    acc_own = acc[pl.ds(pl.multiple_of(core * 256, 256), 256), :].astype(BF16)
    acc_oth = acc[pl.ds(pl.multiple_of(other * 256, 256), 256), :].astype(BF16)
    for j in range(4):
        so[j] = acc_oth[:, j * 128:(j + 1) * 128]
    go(m_so)
    for j in range(4):
        ss[core * 4 + j] = acc_own[:, j * 128:(j + 1) * 128]
    go(half_copy(core))
    m_so.wait_recv()
    go(half_copy(other))

    def teacher_a(i):
        m_ta[i].wait_recv()
        q = tt[i]
        own = dot_nt(q, q) * T_SCALE + mo[...]
        off = dot_nt(tx[0, i], q) * T_SCALE + mp[...]
        top = jnp.maximum(jnp.max(own, 0, keepdims=True), jnp.max(off, 0, keepdims=True))
        own = own - top
        off = off - top
        zt[i, 0] = own
        zt[i, 1] = off
        total = jnp.sum(jnp.exp(own), 0, keepdims=True) + jnp.sum(jnp.exp(off), 0, keepdims=True)
        lt[i:i + 1] = jnp.log(total)

    def b_stats(own, off, row):
        top = jnp.max(own, 0, keepdims=True)
        own = own - top
        st_d[row:row + 1] = top
        st_d[row + 4:row + 5] = jnp.sum(jnp.exp(own), 0, keepdims=True)
        top = jnp.max(off, 0, keepdims=True)
        off = off - top
        st_n[row:row + 1] = top
        st_n[row + 4:row + 5] = jnp.sum(jnp.exp(off), 0, keepdims=True)
        return own, off

    def teacher_b(i):
        m_tb[i].wait_recv()
        k = tt[4 + i]
        own = dot_nt(k, k) * T_SCALE + mo[...]
        off = dot_nt(k, tx[1, i]) * T_SCALE + mn[...]
        zt[4 + i, 0], zt[4 + i, 1] = b_stats(own, off, i)

    settle(2)
    teacher_a(0)
    teacher_b(0)
    teacher_a(1)
    teacher_b(1)
    settle(3)
    for j in range(8):
        st[j] = turned(ss[j])
    teacher_a(2)
    teacher_b(2)
    for f in range(2):
        half_copy(f).wait_recv()
        for j in range(4):
            sxt[f, j] = turned(sx[f, j])

    for i in range(4):
        k = ss[4 + i]
        own = dot_nt(k, k) * S_SCALE + mo[...]
        off = dot_nt(k, sx[1, i]) * S_SCALE + mn[...]
        zs[i, 0], zs[i, 1] = b_stats(own, off, 8 + i)
    teacher_b(3)
    m_sd = go(remote(st_d, rs_d, prv))
    m_sn = go(remote(st_n, rs_n, nxt))
    teacher_a(3)

    gain_own = live_own * G_SCALE
    gain_next = live_next * G_SCALE

    def grads(t_log, s_log, live, gain):
        t_prob = jnp.exp(t_log)
        s_prob = jnp.exp(s_log)
        loss = jnp.sum(t_prob * (t_log - s_log), 0, keepdims=True) * live
        return loss, ((s_prob - t_prob) * gain).astype(BF16)

    m_h = [remote(hsend.at[i], hrecv.at[i], prv if i < 4 else nxt) for i in range(8)]
    losses = []

    def relate_a(i):
        q = ss[i]
        own = dot_nt(q, q) * S_SCALE + mo[...]
        off = dot_nt(sx[0, i], q) * S_SCALE + mp[...]
        top = jnp.maximum(jnp.max(own, 0, keepdims=True), jnp.max(off, 0, keepdims=True))
        own = own - top
        off = off - top
        total = jnp.sum(jnp.exp(own), 0, keepdims=True) + jnp.sum(jnp.exp(off), 0, keepdims=True)
        s_sum = jnp.log(total)
        t_sum = lt[i:i + 1]
        loss_o, g_own = grads(zt[i, 0] - t_sum, own - s_sum, live_own, gain_own)
        loss_p, g_off = grads(zt[i, 1] - t_sum, off - s_sum, live_own, gain_own)
        losses.append(loss_o + loss_p)
        turned_q = st[i]
        hsend[i] = dot_nt(turned_q, g_off).astype(BF16)
        go(m_h[i])
        hacc[i] = dot_nn(sxt[0, i], g_off) + dot_nn(turned_q, g_own) + dot_nt(turned_q, g_own)

    def shifts(m_here, l_here, m_there, l_there):
        top = jnp.maximum(m_here, m_there)
        total = l_here * jnp.exp(m_here - top) + l_there * jnp.exp(m_there - top)
        return (m_here - top) - jnp.log(total)

    def relate_b(i):
        def row(ref, r):
            return ref[r:r + 1]

        t_own = shifts(row(st_d, i), row(st_d, 4 + i), row(rs_n, i), row(rs_n, 4 + i))
        s_own = shifts(row(st_d, 8 + i), row(st_d, 12 + i), row(rs_n, 8 + i), row(rs_n, 12 + i))
        t_off = shifts(row(st_n, i), row(st_n, 4 + i), row(rs_d, i), row(rs_d, 4 + i))
        s_off = shifts(row(st_n, 8 + i), row(st_n, 12 + i), row(rs_d, 8 + i), row(rs_d, 12 + i))
        loss_o, g_own = grads(zt[4 + i, 0] + t_own, zs[i, 0] + s_own, live_own, gain_own)
        loss_n, g_off = grads(zt[4 + i, 1] + t_off, zs[i, 1] + s_off, live_next, gain_next)
        losses.append(loss_o + loss_n)
        turned_k = st[4 + i]
        hsend[4 + i] = dot_nn(turned_k, g_off).astype(BF16)
        go(m_h[4 + i])
        hacc[4 + i] = dot_nn(turned_k, g_own) + dot_nt(turned_k, g_own) + dot_nt(sxt[1, i], g_off)

    def finish(i):
        m_h[i].wait_recv()
        ht_out[pl.ds(i * 128, 128), :] = (hacc[i] + hrecv[i].astype(F32)).astype(BF16)

    m_ho = [
        remote(ht_out.at[pl.ds(pl.multiple_of(other * 512 + j * 128, 128), 128)], ho.at[j], mate)
        for j in range(4)
    ]

    first_y = [True, False, True, True]

    def chunk(j):
        m_ho[j].wait_recv()
        mine = ht_out[pl.ds(pl.multiple_of(core * 512 + j * 128, 128), 128), :]
        theirs = ho[j]
        for k in range(4):
            part = dot_nn(mine, xb[core, :, k * 1024:(k + 1) * 1024])
            part = part + dot_nn(theirs, xb[other, :, k * 1024:(k + 1) * 1024])
            part = part.astype(BF16)
            for m in range(4):
                piece = part[:, m * 256:(m + 1) * 256]
                if first_y[j]:
                    gb[j, m, k] = piece
                else:
                    gb[j, k, m] = piece

    class Ring:
        def __init__(self, j, along_y, unit, bufs, halves):
            self.me = y if along_y else zl
            up = on_y(1) if along_y else on_z(1)
            down = on_y(3) if along_y else on_z(7)
            self.unit, self.halves = unit, halves
            self.b1p, self.b1m, self.bdp, self.bdm, self.b2p, self.b2m = [b.at[j] for b in bufs]
            lo, hi = halves
            self.s1p = remote(self.at(2, lo), self.b1p, up)
            self.s1m = remote(self.at(2, hi), self.b1m, down)
            self.dp = remote(self.at(1, hi), self.bdp, up)
            self.dm = remote(self.at(3, lo), self.bdm, down)
            self.s2p = remote(self.b1p, self.b2p, up)
            self.s2m = remote(self.b1m, self.b2m, down)

        def at(self, k, half):
            return self.unit.at[(self.me + k) % 4].at[half]

        def open(self):
            go(self.s1p); go(self.s1m); go(self.dp); go(self.dm)

        def middle(self):
            lo, hi = self.halves
            self.s1p.wait_recv()
            self.b1p[...] = (
                self.b1p[...].astype(F32) + self.at(1, lo)[...].astype(F32)
            ).astype(BF16)
            go(self.s2p)
            self.s1m.wait_recv()
            self.b1m[...] = (
                self.b1m[...].astype(F32) + self.at(3, hi)[...].astype(F32)
            ).astype(BF16)
            go(self.s2m)

        def close(self, dst):
            lo, hi = self.halves
            self.s2p.wait_recv()
            self.dm.wait_recv()
            dst.at[lo][...] = (
                self.at(0, lo)[...].astype(F32) + self.b2p[...].astype(F32)
                + self.bdm[...].astype(F32)
            ).astype(BF16)
            self.s2m.wait_recv()
            self.dp.wait_recv()
            dst.at[hi][...] = (
                self.at(0, hi)[...].astype(F32) + self.b2m[...].astype(F32)
                + self.bdp[...].astype(F32)
            ).astype(BF16)

    p_ring = [
        Ring(j, first_y[j], gb.at[j], (p1p, p1m, pdp, pdm, p2p, p2m), (pl.ds(0, 2), pl.ds(2, 2)))
        for j in range(4)
    ]
    q_ring = [
        Ring(j, not first_y[j], qb.at[j], (q1p, q1m, qdp, qdm, q2p, q2m),
             (pl.ds(0, 64), pl.ds(64, 64)))
        for j in range(4)
    ]
    m_fin = [remote(fin.at[j], fin_r.at[j], on_z(4)) for j in range(4)]
    m_gf = [remote(gf.at[j], gf_r.at[j], mate) for j in range(4)]

    def to_q(j):
        p_ring[j].close(qb.at[j])
        q_ring[j].open()

    def to_pair(j):
        q_ring[j].close(fin.at[j])
        go(m_fin[j])

    def total(j):
        m_fin[j].wait_recv()
        gf[j] = fin[j].astype(F32) + fin_r[j].astype(F32)
        go(m_gf[j])

    def emit(j):
        m_gf[j].wait_recv()
        gt_out[pl.ds(pl.multiple_of(core * 512 + j * 128, 128), 128), :] = gf[j]
        gt_out[pl.ds(pl.multiple_of(other * 512 + j * 128, 128), 128), :] = gf_r[j]

    def spread(buf, me, where):
        return [go(remote(buf.at[me], buf.at[me], where(k))) for k in (1, 2, 3)]

    def gathered(copies, buf):
        for copy in copies:
            copy.wait_recv()
        return buf[0] + buf[1] + buf[2] + buf[3]

    for i in range(4):
        relate_a(i)
    m_sd.wait_recv()
    m_sn.wait_recv()
    relate_b(0)
    finish(0); finish(4); go(m_ho[0])
    relate_b(1)
    finish(1); finish(5); go(m_ho[1])
    chunk(0)
    p_ring[0].open()
    relate_b(2)
    finish(2); finish(6); go(m_ho[2])
    chunk(1)
    p_ring[1].open()
    relate_b(3)
    finish(3); finish(7); go(m_ho[3])
    p_ring[0].middle()
    chunk(2)
    p_ring[2].open()
    loss = losses[0]
    for part in losses[1:]:
        loss = loss + part
    loss = jnp.sum(loss, keepdims=True) * (1.0 / HEADS)
    lx[x] = jnp.broadcast_to(loss, (8, 128))
    c_x = spread(lx, x, on_x)
    p_ring[1].middle()
    chunk(3)
    p_ring[3].open()
    to_q(0)
    p_ring[2].middle()
    ly[y] = gathered(c_x, lx)
    c_y = spread(ly, y, on_y)
    to_q(1)
    q_ring[0].middle()
    p_ring[3].middle()
    to_q(2)
    q_ring[1].middle()
    lz[zl] = gathered(c_y, ly)
    c_z = spread(lz, zl, on_zl)
    to_pair(0)
    to_q(3)
    q_ring[2].middle()
    to_pair(1)
    total(0)
    q_ring[3].middle()
    to_pair(2)
    total(1)
    emit(0)
    to_pair(3)
    loss_out[...] = gathered(c_z, lz)
    total(2)
    emit(1)
    total(3)
    emit(2)
    emit(3)
    for copy in pending:
        copy.wait_send()


def per_device(teacher_part, student_in, out_proj, segment_ids, valid_count):
    anywhere = pl.BlockSpec(memory_space=pl.ANY)
    vmem = pl.BlockSpec(memory_space=pltpu.VMEM)

    def b(*shape):
        return pltpu.VMEM(shape, BF16)

    def f(*shape):
        return pltpu.VMEM(shape, F32)

    scratch = [b(2, 256, 4096), b(16, 256, 512), f(512, 512)]
    scratch += [b(8, 256, 256)] + [b(4, 256, 256)] * 8 + [b(8, 256, 256), b(2, 4, 256, 256)]
    scratch += [b(8, 256, 128), b(4, 256, 128), b(2, 4, 256, 128), b(8, 128, 256), b(2, 4, 128, 256)]
    scratch += [f(256, 256)] * 3 + [f(8, 2, 256, 256), f(8, 256), f(4, 2, 256, 256)]
    scratch += [f(16, 256)] * 4
    scratch += [f(8, 128, 256), b(8, 128, 256), b(8, 128, 256), b(4, 128, 256)]
    scratch += [b(4, 4, 4, 128, 256)] + [b(4, 2, 128, 256)] * 6
    scratch += [b(4, 4, 128, 256)] + [b(4, 64, 256)] * 6
    scratch += [b(4, 128, 256)] * 2 + [f(4, 128, 256)] * 2
    scratch += [f(4, 8, 128)] * 3
    scratch += [
        pltpu.SemaphoreType.DMA((N_SEM,)), pltpu.SemaphoreType.DMA((N_SEM,)),
        pltpu.SemaphoreType.DMA((24,)),
    ]
    ht, gt, loss = pl.pallas_call(
        kernel,
        out_shape=(
            jax.ShapeDtypeStruct((1024, 256), BF16),
            jax.ShapeDtypeStruct((1024, 256), F32),
            jax.ShapeDtypeStruct((8, 128), F32),
        ),
        in_specs=[anywhere, anywhere, anywhere, vmem, pl.BlockSpec(memory_space=pltpu.SMEM)],
        out_specs=(vmem, vmem, vmem),
        scratch_shapes=scratch,
        name="relation_step",
        compiler_params=pltpu.CompilerParams(
            collective_id=0, has_side_effects=True, vmem_limit_bytes=60 * 2**20
        ),
    )(teacher_part[0, 0], student_in[0], out_proj, segment_ids, valid_count)
    state_grad = (ht.T.astype(F32) * UNSCALE)[None]
    return (loss[0, :1], gt.T, state_grad)


def solution(mesh):
    return jax.shard_map(
        per_device,
        mesh=mesh,
        in_specs=(
            P("dp", "tp", "ctx", None),
            P("dp", "ctx", None),
            P("ctx", "tp"),
            P("dp", None),
            P("dp"),
        ),
        out_specs=(P("dp"), P("ctx", "tp"), P("dp", "ctx", "tp")),
        check_vma=False,
    )
```

```python
import math

import jax
import jax.numpy as jnp
from jax import lax
from jax.experimental import pallas as pl
from jax.experimental.pallas import tpu as pltpu
from jax.sharding import PartitionSpec as P

DS = 4096
HEADS = 32
MESH = pl.DeviceIdType.MESH
F32 = jnp.float32
BF16 = jnp.bfloat16
NEG = -1e30
UNSCALE = HEADS * math.sqrt(DS // HEADS)
T_SCALE = 1.0 / math.sqrt(256)
S_SCALE = 1.0 / math.sqrt(128)
G_SCALE = S_SCALE / HEADS
N_SEM = 224


def dot_nn(a, b):
    return lax.dot_general(a, b, (((1,), (0,)), ((), ())), preferred_element_type=F32)


def dot_nt(a, b):
    return lax.dot_general(a, b, (((1,), (1,)), ((), ())), preferred_element_type=F32)


def turned(a):
    return jnp.transpose(a.astype(F32)).astype(BF16)


def kernel(
    tpart, xin, win, seg_ref, valid_ref,
    h_out, gt_out, loss_out,
    xb, wb, acc,
    t_own, t_fp, t_fm, r1p, r1m, rdp, rdm, r2p, r2m, tt, tx,
    ss, so, sx, st, sxt,
    mo, mp, mn, zt, lt, zs, st_d, st_n, rs_d, rs_n,
    hacc, hsend, hrecv, ht, ho,
    gb, p1p, p1m, pdp, pdm, p2p, p2m, qb, q1p, q1m, qdp, qdm, q2p, q2m, fin, fin_m, fin_r, gf, gf_r,
    lx, ly, lz,
    send_sem, recv_sem, loc_sem,
):
    dp, ctx, x = lax.axis_index("dp"), lax.axis_index("ctx"), lax.axis_index("tp")
    core, zh, zl, y = dp % 2, dp // 2, ctx // 4, ctx % 4
    z = zh * 4 + zl
    other = 1 - core

    def dev(x_, y_, z_, c_):
        return ((z_ // 4) * 2 + c_, (z_ % 4) * 4 + y_, x_)

    def on_x(k):
        return dev((x + k) % 4, y, z, core)

    def on_y(k):
        return dev(x, (y + k) % 4, z, core)

    def on_z(k):
        return dev(x, y, (z + k) % 8, core)

    def on_zl(k):
        return dev(x, y, zh * 4 + (zl + k) % 4, core)

    mate = dev(x, y, z, other)
    nxt = dev(x, (y + 1) % 4, (z + (y + 1) // 4) % 8, core)
    prv = dev(x, (y + 3) % 4, (z + 7 + (y + 3) // 4) % 8, core)

    partners = [on_x(1), on_x(3), on_y(1), on_y(3), on_z(1), on_z(7), mate]

    sems = [0]
    pending = []

    def remote(src, dst, where):
        k = sems[0]
        sems[0] += 1
        return pltpu.make_async_remote_copy(
            src_ref=src, dst_ref=dst, send_sem=send_sem.at[k], recv_sem=recv_sem.at[k],
            device_id=where, device_id_type=MESH,
        )

    def go(copy):
        copy.start()
        pending.append(copy)
        return copy

    locs = [0]

    def local(src, dst):
        k = locs[0]
        locs[0] += 1
        copy = pltpu.make_async_copy(src, dst, loc_sem.at[k])
        copy.start()
        return copy

    x_loc = local(xin, xb.at[core])
    col0 = pl.multiple_of(core * 512, 512)
    w_loc = local(win.at[:, pl.ds(col0, 512)], wb.at[ctx])

    def tcol(block, head):
        return tpart.at[:, pl.ds(pl.multiple_of(block * 2048 + head * 256, 256), 256)]

    fp_loc = [local(tcol((x + 1) % 4, i), t_fp.at[i]) for i in range(4)]
    fm_loc = [local(tcol((x + 3) % 4, 4 + i), t_fm.at[i]) for i in range(4)]
    own_loc = [local(tcol(x, i), t_own.at[i]) for i in range(8)]

    barrier = pltpu.get_barrier_semaphore()
    for where in partners:
        pl.semaphore_signal(barrier, inc=1, device_id=where, device_id_type=MESH)
    pl.semaphore_wait(barrier, len(partners))

    m_s1p = [remote(tcol((x + 2) % 4, i), r1p.at[i], on_x(1)) for i in range(4)]
    m_s1m = [remote(tcol((x + 2) % 4, 4 + i), r1m.at[i], on_x(3)) for i in range(4)]
    m_dp = [remote(tcol((x + 1) % 4, 4 + i), rdp.at[i], on_x(1)) for i in range(4)]
    m_dm = [remote(tcol((x + 3) % 4, i), rdm.at[i], on_x(3)) for i in range(4)]
    m_s2p = [remote(r1p.at[i], r2p.at[i], on_x(1)) for i in range(4)]
    m_s2m = [remote(r1m.at[i], r2m.at[i], on_x(3)) for i in range(4)]
    m_ta = [remote(tt.at[i], tx.at[0, i], nxt) for i in range(4)]
    m_tb = [remote(tt.at[4 + i], tx.at[1, i], prv) for i in range(4)]
    m_x = remote(xin, xb.at[core], mate)

    def block(dy, dz):
        return ((zl + dz) % 4) * 4 + (y + dy) % 4

    def gather_messages(kind):
        base = kind * 128

        def at(dp_, dq_):
            return block(dq_, dp_) if kind == 0 else block(dp_, dq_)

        def to(which, sign):
            on_z_axis = (kind == 0) == (which == "p")
            k = 1 if sign > 0 else -1
            return on_z(k % 8) if on_z_axis else on_y(k % 4)

        def piece(dp_, dq_, part):
            start, size = {"all": (0, 128), "lo": (0, 64), "hi": (64, 64)}[part]
            b = at(dp_, dq_)
            return wb.at[b, pl.ds(base + start, size)]

        def message(dp_, dq_, part, which, sign):
            ref = piece(dp_, dq_, part)
            return remote(ref, ref, to(which, sign))

        own = win.at[pl.ds(base, 128), pl.ds(col0, 512)]

        def first(which, sign):
            return remote(own, piece(0, 0, "all"), to(which, sign))

        return [
            first("p", 1), first("p", -1), first("q", 1), first("q", -1),
            message(-1, 0, "lo", "p", 1), message(1, 0, "hi", "p", -1),
            message(-1, 0, "all", "q", 1), message(-1, 0, "all", "q", -1),
            message(1, 0, "all", "q", 1), message(1, 0, "all", "q", -1),
            message(0, -1, "lo", "q", 1), message(0, 1, "hi", "q", -1),
            message(2, 0, "all", "q", 1), message(2, 0, "all", "q", -1),
            message(-1, -1, "lo", "q", 1), message(-1, 1, "hi", "q", -1),
            message(1, -1, "lo", "q", 1), message(1, 1, "hi", "q", -1),
            message(2, -1, "lo", "q", 1), message(2, 1, "hi", "q", -1),
        ]

    ag = [gather_messages(0), gather_messages(1)]

    def ag_start(*ids):
        for k in ids:
            for kind in (0, 1):
                go(ag[kind][k])

    def ag_wait(*ids):
        for k in ids:
            for kind in (0, 1):
                ag[kind][k].wait_recv()

    go(m_s1p[0]); go(m_s1m[0])
    ag_start(0, 1)
    go(m_s1p[1]); go(m_s1m[1]); go(m_dp[0]); go(m_dm[0])
    ag_start(2, 3)
    go(m_x)

    window = ctx
    valid = valid_ref[0]

    def seg_row(w):
        return seg_ref[:, pl.ds(pl.multiple_of(w * 256, 256), 256)].astype(F32)

    row_own = seg_row(window)
    row_next = seg_row((window + 1) % 16)
    col_own = jnp.transpose(jnp.broadcast_to(row_own, (256, 256)))
    col_prev = jnp.transpose(jnp.broadcast_to(seg_row((window + 15) % 16), (256, 256)))
    key_iota = lax.broadcasted_iota(jnp.int32, (256, 256), 0)
    query_iota = lax.broadcasted_iota(jnp.int32, (256, 256), 1)
    key_own = key_iota + window * 256
    key_prev = key_own - 256
    query_next = query_iota + (window + 1) * 256
    mo[...] = jnp.where((col_own == row_own) & (key_own < valid), 0.0, NEG)
    mp[...] = jnp.where((col_prev == row_own) & (key_prev >= 0) & (key_prev < valid), 0.0, NEG)
    mn[...] = jnp.where((col_own == row_next) & (key_own < valid) & (query_next < 4096), 0.0, NEG)
    lane = lax.broadcasted_iota(jnp.int32, (1, 256), 1)
    live_own = jnp.where(lane + window * 256 < valid, 1.0, 0.0).astype(F32)
    live_next = jnp.where(
        (lane + (window + 1) * 256 < valid) & (lane + (window + 1) * 256 < 4096), 1.0, 0.0
    ).astype(F32)

    acc[...] = jnp.zeros_like(acc)

    def feed(dy, dz):
        b = block(dy, dz)
        xs = xb[:, :, pl.ds(pl.multiple_of(b * 256, 256), 256)].reshape(512, 256)
        acc[...] += dot_nn(xs, wb[b])

    def relay(i):
        m_s1p[i].wait_recv()
        fp_loc[i].wait()
        r1p[i] = (r1p[i].astype(F32) + t_fp[i].astype(F32)).astype(BF16)
        go(m_s2p[i])
        m_s1m[i].wait_recv()
        fm_loc[i].wait()
        r1m[i] = (r1m[i].astype(F32) + t_fm[i].astype(F32)).astype(BF16)
        go(m_s2m[i])

    def settle(i):
        m_s2p[i].wait_recv()
        m_dm[i].wait_recv()
        own_loc[i].wait()
        tt[i] = (t_own[i].astype(F32) + r2p[i].astype(F32) + rdm[i].astype(F32)).astype(BF16)
        go(m_ta[i])
        m_s2m[i].wait_recv()
        m_dp[i].wait_recv()
        own_loc[4 + i].wait()
        tt[4 + i] = (
            t_own[4 + i].astype(F32) + r2m[i].astype(F32) + rdp[i].astype(F32)
        ).astype(BF16)
        go(m_tb[i])

    ag_wait(0, 1)
    ag_start(4, 5, 6, 7, 8, 9)
    relay(0)
    go(m_s1p[2]); go(m_s1m[2]); go(m_dp[1]); go(m_dm[1])
    ag_wait(2, 3)
    ag_start(10, 11)
    x_loc.wait()
    w_loc.wait()
    m_x.wait_recv()
    feed(0, 0)
    relay(1)
    go(m_s1p[3]); go(m_s1m[3]); go(m_dp[2]); go(m_dm[2])
    ag_wait(4, 5)
    ag_start(12, 13)
    feed(1, 0)
    feed(-1, 0)
    feed(0, 1)
    feed(0, -1)
    ag_wait(6, 7, 8, 9)
    ag_start(14, 15, 16, 17)
    settle(0)
    relay(2)
    go(m_dp[3]); go(m_dm[3])
    feed(1, 1)
    feed(-1, 1)
    feed(1, -1)
    feed(-1, -1)
    ag_wait(12, 13)
    ag_start(18, 19)
    ag_wait(10, 11)
    feed(2, 0)
    feed(0, 2)
    settle(1)
    ag_wait(14, 15, 16, 17)
    feed(2, 1)
    feed(2, -1)
    feed(1, 2)
    feed(-1, 2)
    relay(3)
    ag_wait(18, 19)
    feed(2, 2)

    m_so = remote(so, ss.at[pl.ds(core * 4, 4)], mate)

    def half_to(f):
        up = 1 - f
        y_ = (y + 1 + 2 * f) % 4
        z_ = (z + up * ((y + 1) // 4) + f * (7 + (y + 3) // 4)) % 8
        return dev(x, y_, z_, core)

    k_half = sems[0]
    sems[0] += 8

    def half_copy(f, j):
        k = k_half + f * 4 + j
        return pltpu.make_async_remote_copy(
            src_ref=ss.at[f * 4 + j], dst_ref=sx.at[f, j], send_sem=send_sem.at[k],
            recv_sem=recv_sem.at[k], device_id=half_to(f), device_id_type=MESH,
        )

    acc_own = acc[pl.ds(pl.multiple_of(core * 256, 256), 256), :].astype(BF16)
    acc_oth = acc[pl.ds(pl.multiple_of(other * 256, 256), 256), :].astype(BF16)
    for j in range(4):
        so[j] = acc_oth[:, j * 128:(j + 1) * 128]
    go(m_so)
    for j in range(4):
        ss[core * 4 + j] = acc_own[:, j * 128:(j + 1) * 128]
        go(half_copy(core, j))
    for j in range(4):
        st[core * 4 + j] = turned(acc_own[:, j * 128:(j + 1) * 128])
    m_so.wait_recv()
    for j in range(4):
        go(half_copy(other, j))

    def teacher_a(i):
        m_ta[i].wait_recv()
        q = tt[i]
        own = dot_nt(q, q) * T_SCALE + mo[...]
        off = dot_nt(tx[0, i], q) * T_SCALE + mp[...]
        top = jnp.maximum(jnp.max(own, 0, keepdims=True), jnp.max(off, 0, keepdims=True))
        own = own - top
        off = off - top
        zt[i, 0] = own
        zt[i, 1] = off
        total = jnp.sum(jnp.exp(own), 0, keepdims=True) + jnp.sum(jnp.exp(off), 0, keepdims=True)
        lt[i:i + 1] = jnp.log(total)

    def b_stats(own, off, i, row):
        top = jnp.max(own, 0, keepdims=True)
        own = own - top
        st_d[i, row:row + 1] = top
        st_d[i, row + 1:row + 2] = jnp.sum(jnp.exp(own), 0, keepdims=True)
        top = jnp.max(off, 0, keepdims=True)
        off = off - top
        st_n[i, row:row + 1] = top
        st_n[i, row + 1:row + 2] = jnp.sum(jnp.exp(off), 0, keepdims=True)
        return own, off

    def teacher_b(i):
        m_tb[i].wait_recv()
        k = tt[4 + i]
        own = dot_nt(k, k) * T_SCALE + mo[...]
        off = dot_nt(k, tx[1, i]) * T_SCALE + mn[...]
        zt[4 + i, 0], zt[4 + i, 1] = b_stats(own, off, i, 0)

    m_sd = [remote(st_d.at[i], rs_d.at[i], prv) for i in range(4)]
    m_sn = [remote(st_n.at[i], rs_n.at[i], nxt) for i in range(4)]

    def student_b(i):
        half_copy(1, i).wait_recv()
        k = ss[4 + i]
        own = dot_nt(k, k) * S_SCALE + mo[...]
        off = dot_nt(k, sx[1, i]) * S_SCALE + mn[...]
        zs[i, 0], zs[i, 1] = b_stats(own, off, i, 2)
        go(m_sd[i])
        go(m_sn[i])
        sxt[1, i] = turned(sx[1, i])

    def turn_own(j):
        st[other * 4 + j] = turned(ss[other * 4 + j])

    gain_own = live_own * G_SCALE
    gain_next = live_next * G_SCALE

    def grads(t_log, s_log, live, gain):
        t_prob = jnp.exp(t_log)
        s_prob = jnp.exp(s_log)
        loss = jnp.sum(t_prob * (t_log - s_log), 0, keepdims=True) * live
        return loss, ((s_prob - t_prob) * gain).astype(BF16)

    m_h = [remote(hsend.at[i], hrecv.at[i], prv if i < 4 else nxt) for i in range(8)]
    losses = []

    def relate_a(i):
        half_copy(0, i).wait_recv()
        sxt[0, i] = turned(sx[0, i])
        q = ss[i]
        own = dot_nt(q, q) * S_SCALE + mo[...]
        off = dot_nt(sx[0, i], q) * S_SCALE + mp[...]
        top = jnp.maximum(jnp.max(own, 0, keepdims=True), jnp.max(off, 0, keepdims=True))
        own = own - top
        off = off - top
        total = jnp.sum(jnp.exp(own), 0, keepdims=True) + jnp.sum(jnp.exp(off), 0, keepdims=True)
        s_sum = jnp.log(total)
        t_sum = lt[i:i + 1]
        loss_o, g_own = grads(zt[i, 0] - t_sum, own - s_sum, live_own, gain_own)
        loss_p, g_off = grads(zt[i, 1] - t_sum, off - s_sum, live_own, gain_own)
        losses.append(loss_o + loss_p)
        turned_q = st[i]
        hsend[i] = dot_nt(turned_q, g_off).astype(BF16)
        go(m_h[i])
        hacc[i] = dot_nn(sxt[0, i], g_off) + dot_nn(turned_q, g_own) + dot_nt(turned_q, g_own)

    def shifts(m_here, l_here, m_there, l_there):
        top = jnp.maximum(m_here, m_there)
        total = l_here * jnp.exp(m_here - top) + l_there * jnp.exp(m_there - top)
        return (m_here - top) - jnp.log(total)

    def relate_b(i):
        m_sd[i].wait_recv()
        m_sn[i].wait_recv()

        def row(ref, r):
            return ref[i, r:r + 1]

        t_own = shifts(row(st_d, 0), row(st_d, 1), row(rs_n, 0), row(rs_n, 1))
        s_own = shifts(row(st_d, 2), row(st_d, 3), row(rs_n, 2), row(rs_n, 3))
        t_off = shifts(row(st_n, 0), row(st_n, 1), row(rs_d, 0), row(rs_d, 1))
        s_off = shifts(row(st_n, 2), row(st_n, 3), row(rs_d, 2), row(rs_d, 3))
        loss_o, g_own = grads(zt[4 + i, 0] + t_own, zs[i, 0] + s_own, live_own, gain_own)
        loss_n, g_off = grads(zt[4 + i, 1] + t_off, zs[i, 1] + s_off, live_next, gain_next)
        losses.append(loss_o + loss_n)
        turned_k = st[4 + i]
        hsend[4 + i] = dot_nn(turned_k, g_off).astype(BF16)
        go(m_h[4 + i])
        hacc[4 + i] = dot_nn(turned_k, g_own) + dot_nt(turned_k, g_own) + dot_nt(sxt[1, i], g_off)

    def finish_one(i):
        m_h[i].wait_recv()
        full = (hacc[i] + hrecv[i].astype(F32)).astype(BF16)
        ht[i] = full
        return full

    m_ho = [remote(ht.at[other * 4 + j], ho.at[j], mate) for j in range(4)]

    def finish(j):
        low = finish_one(j)
        high = finish_one(4 + j)
        go(m_ho[j])
        h_out[:, j * 128:(j + 1) * 128] = turned(low)
        h_out[:, (4 + j) * 128:(5 + j) * 128] = turned(high)

    first_y = [True, False, True, True]

    def chunk(j):
        m_ho[j].wait_recv()
        mine = ht[core * 4 + j]
        theirs = ho[j]
        for k in range(4):
            part = dot_nn(mine, xb[core, :, k * 1024:(k + 1) * 1024])
            part = part + dot_nn(theirs, xb[other, :, k * 1024:(k + 1) * 1024])
            part = part.astype(BF16)
            for m in range(4):
                piece = part[:, m * 256:(m + 1) * 256]
                if first_y[j]:
                    gb[j, m, k] = piece
                else:
                    gb[j, k, m] = piece

    class Ring:
        def __init__(self, j, along_y, unit, bufs, halves):
            self.me = y if along_y else zl
            up = on_y(1) if along_y else on_z(1)
            down = on_y(3) if along_y else on_z(7)
            self.unit, self.halves = unit, halves
            self.b1p, self.b1m, self.bdp, self.bdm, self.b2p, self.b2m = [b.at[j] for b in bufs]
            lo, hi = halves
            self.s1p = remote(self.at(2, lo), self.b1p, up)
            self.s1m = remote(self.at(2, hi), self.b1m, down)
            self.dp = remote(self.at(1, hi), self.bdp, up)
            self.dm = remote(self.at(3, lo), self.bdm, down)
            self.s2p = remote(self.b1p, self.b2p, up)
            self.s2m = remote(self.b1m, self.b2m, down)

        def at(self, k, half):
            return self.unit.at[(self.me + k) % 4].at[half]

        def open(self):
            go(self.s1p); go(self.s1m); go(self.dp); go(self.dm)

        def middle(self):
            lo, hi = self.halves
            self.s1p.wait_recv()
            self.b1p[...] = (
                self.b1p[...].astype(F32) + self.at(1, lo)[...].astype(F32)
            ).astype(BF16)
            go(self.s2p)
            self.s1m.wait_recv()
            self.b1m[...] = (
                self.b1m[...].astype(F32) + self.at(3, hi)[...].astype(F32)
            ).astype(BF16)
            go(self.s2m)

        def close(self, dst):
            lo, hi = self.halves
            self.s2p.wait_recv()
            self.dm.wait_recv()
            dst.at[lo][...] = (
                self.at(0, lo)[...].astype(F32) + self.b2p[...].astype(F32)
                + self.bdm[...].astype(F32)
            ).astype(BF16)
            self.s2m.wait_recv()
            self.dp.wait_recv()
            dst.at[hi][...] = (
                self.at(0, hi)[...].astype(F32) + self.b2m[...].astype(F32)
                + self.bdp[...].astype(F32)
            ).astype(BF16)

    p_ring = [
        Ring(j, first_y[j], gb.at[j], (p1p, p1m, pdp, pdm, p2p, p2m), (pl.ds(0, 2), pl.ds(2, 2)))
        for j in range(4)
    ]
    q_ring = [
        Ring(j, not first_y[j], qb.at[j], (q1p, q1m, qdp, qdm, q2p, q2m),
             (pl.ds(0, 64), pl.ds(64, 64)))
        for j in range(4)
    ]
    low, high = pl.ds(0, 64), pl.ds(64, 64)
    m_f1 = [
        (remote(fin.at[j, low], fin_m.at[j, low], on_z(2)),
         remote(fin.at[j, high], fin_m.at[j, high], on_z(6)))
        for j in range(4)
    ]
    m_f2 = [
        (remote(fin_m.at[j, low], fin_r.at[j, low], on_z(2)),
         remote(fin_m.at[j, high], fin_r.at[j, high], on_z(6)))
        for j in range(4)
    ]
    m_gf = [remote(gf.at[j], gf_r.at[j], mate) for j in range(4)]

    def to_q(j):
        p_ring[j].close(qb.at[j])
        q_ring[j].open()

    def to_pair(j):
        q_ring[j].close(fin.at[j])
        for copy in m_f1[j]:
            go(copy)

    def pass_on(j):
        for come, leave in zip(m_f1[j], m_f2[j]):
            come.wait_recv()
            go(leave)

    def total(j):
        for copy in m_f2[j]:
            copy.wait_recv()
        gf[j] = fin[j].astype(F32) + fin_r[j].astype(F32)
        go(m_gf[j])
        gt_out[:, pl.ds(pl.multiple_of(core * 512 + j * 128, 128), 128)] = jnp.transpose(gf[j])

    def emit(j):
        m_gf[j].wait_recv()
        gt_out[:, pl.ds(pl.multiple_of(other * 512 + j * 128, 128), 128)] = jnp.transpose(gf_r[j])

    def spread(buf, me, where):
        return [go(remote(buf.at[me], buf.at[me], where(k))) for k in (1, 2, 3)]

    def gathered(copies, buf):
        for copy in copies:
            copy.wait_recv()
        return buf[0] + buf[1] + buf[2] + buf[3]

    teacher_a(0)
    teacher_b(0)
    student_b(0)
    for j in range(4):
        turn_own(j)
    relate_a(0)
    settle(2)
    teacher_b(1)
    student_b(1)
    relate_b(0)
    finish(0)
    teacher_a(1)
    relate_a(1)
    chunk(0)
    p_ring[0].open()
    settle(3)
    relate_b(1)
    finish(1)
    teacher_b(2)
    student_b(2)
    p_ring[0].middle()
    teacher_a(2)
    relate_a(2)
    chunk(1)
    p_ring[1].open()
    relate_b(2)
    finish(2)
    teacher_b(3)
    student_b(3)
    to_q(0)
    teacher_a(3)
    relate_a(3)
    chunk(2)
    p_ring[2].open()
    p_ring[1].middle()
    q_ring[0].middle()
    relate_b(3)
    finish(3)
    to_pair(0)
    p_ring[2].middle()
    to_q(1)
    chunk(3)
    p_ring[3].open()
    pass_on(0)
    loss = losses[0]
    for part in losses[1:]:
        loss = loss + part
    loss = jnp.sum(loss, keepdims=True) * (1.0 / HEADS)
    lx[x] = jnp.broadcast_to(loss, (8, 128))
    c_x = spread(lx, x, on_x)
    q_ring[1].middle()
    to_q(2)
    p_ring[3].middle()
    to_pair(1)
    q_ring[2].middle()
    pass_on(1)
    to_q(3)
    ly[y] = gathered(c_x, lx)
    c_y = spread(ly, y, on_y)
    to_pair(2)
    total(0)
    pass_on(2)
    q_ring[3].middle()
    lz[zl] = gathered(c_y, ly)
    c_z = spread(lz, zl, on_zl)
    total(1)
    emit(0)
    to_pair(3)
    pass_on(3)
    loss_out[...] = gathered(c_z, lz)
    total(2)
    emit(1)
    total(3)
    emit(2)
    emit(3)
    for copy in pending:
        copy.wait_send()


def per_device(teacher_part, student_in, out_proj, segment_ids, valid_count):
    anywhere = pl.BlockSpec(memory_space=pl.ANY)
    vmem = pl.BlockSpec(memory_space=pltpu.VMEM)

    def b(*shape):
        return pltpu.VMEM(shape, BF16)

    def f(*shape):
        return pltpu.VMEM(shape, F32)

    scratch = [b(2, 256, 4096), b(16, 256, 512), f(512, 512)]
    scratch += [b(8, 256, 256)] + [b(4, 256, 256)] * 8 + [b(8, 256, 256), b(2, 4, 256, 256)]
    scratch += [b(8, 256, 128), b(4, 256, 128), b(2, 4, 256, 128), b(8, 128, 256), b(2, 4, 128, 256)]
    scratch += [f(256, 256)] * 3 + [f(8, 2, 256, 256), f(8, 256), f(4, 2, 256, 256)]
    scratch += [f(4, 4, 256)] * 4
    scratch += [f(8, 128, 256)] + [b(8, 128, 256)] * 3 + [b(4, 128, 256)]
    scratch += [b(4, 4, 4, 128, 256)] + [b(4, 2, 128, 256)] * 6
    scratch += [b(4, 4, 128, 256)] + [b(4, 64, 256)] * 6
    scratch += [b(4, 128, 256)] * 3 + [f(4, 128, 256)] * 2
    scratch += [f(4, 8, 128)] * 3
    scratch += [
        pltpu.SemaphoreType.DMA((N_SEM,)), pltpu.SemaphoreType.DMA((N_SEM,)),
        pltpu.SemaphoreType.DMA((24,)),
    ]
    hidden_grad, wo_grad, loss = pl.pallas_call(
        kernel,
        out_shape=(
            jax.ShapeDtypeStruct((256, 1024), BF16),
            jax.ShapeDtypeStruct((256, 1024), F32),
            jax.ShapeDtypeStruct((8, 128), F32),
        ),
        in_specs=[anywhere, anywhere, anywhere, vmem, pl.BlockSpec(memory_space=pltpu.SMEM)],
        out_specs=(vmem, vmem, vmem),
        scratch_shapes=scratch,
        name="relation_step",
        compiler_params=pltpu.CompilerParams(
            collective_id=0, has_side_effects=True, vmem_limit_bytes=60 * 2**20
        ),
    )(teacher_part[0, 0], student_in[0], out_proj, segment_ids, valid_count)
    state_grad = (hidden_grad.astype(F32) * UNSCALE)[None]
    return (loss[0, :1], wo_grad, state_grad)


def solution(mesh):
    return jax.shard_map(
        per_device,
        mesh=mesh,
        in_specs=(
            P("dp", "tp", "ctx", None),
            P("dp", "ctx", None),
            P("ctx", "tp"),
            P("dp", None),
            P("dp"),
        ),
        out_specs=(P("dp"), P("ctx", "tp"), P("dp", "ctx", "tp")),
        check_vma=False,
    )
```

```python
import math

import jax
import jax.numpy as jnp
from jax import lax
from jax.experimental import pallas as pl
from jax.experimental.pallas import tpu as pltpu
from jax.sharding import PartitionSpec as P

DS = 4096
HEADS = 32
MESH = pl.DeviceIdType.MESH
F32 = jnp.float32
BF16 = jnp.bfloat16
NEG = -1e30
UNSCALE = HEADS * math.sqrt(DS // HEADS)
T_SCALE = 1.0 / math.sqrt(256)
S_SCALE = 1.0 / math.sqrt(128)
G_SCALE = S_SCALE / HEADS
N_SEM = 224


def dot_nn(a, b):
    return lax.dot_general(a, b, (((1,), (0,)), ((), ())), preferred_element_type=F32)


def dot_nt(a, b):
    return lax.dot_general(a, b, (((1,), (1,)), ((), ())), preferred_element_type=F32)


def turned(a):
    return jnp.transpose(a.astype(F32)).astype(BF16)


def kernel(
    tpart, xin, win, seg_ref, valid_ref,
    h_out, gt_out, loss_out,
    xb, wb, acc,
    t_own, t_fp, t_fm, r1p, r1m, rdp, rdm, r2p, r2m, tt, tx,
    ss, so, sx, st, sxt,
    mo, mp, mn, zt, lt, zs, st_d, st_n, rs_d, rs_n,
    hacc, hsend, hrecv, ht, ho,
    gb, p1p, p1m, pdp, pdm, p2p, p2m, qb, q1p, q1m, qdp, qdm, q2p, q2m, fin, fin_m, fin_r, gf, gf_r,
    lx, ly, lz,
    send_sem, recv_sem, loc_sem,
):
    dp, ctx, x = lax.axis_index("dp"), lax.axis_index("ctx"), lax.axis_index("tp")
    core, zh, zl, y = dp % 2, dp // 2, ctx // 4, ctx % 4
    z = zh * 4 + zl
    other = 1 - core

    def dev(x_, y_, z_, c_):
        return ((z_ // 4) * 2 + c_, (z_ % 4) * 4 + y_, x_)

    def on_x(k):
        return dev((x + k) % 4, y, z, core)

    def on_y(k):
        return dev(x, (y + k) % 4, z, core)

    def on_z(k):
        return dev(x, y, (z + k) % 8, core)

    def on_zl(k):
        return dev(x, y, zh * 4 + (zl + k) % 4, core)

    mate = dev(x, y, z, other)
    nxt = dev(x, (y + 1) % 4, (z + (y + 1) // 4) % 8, core)
    prv = dev(x, (y + 3) % 4, (z + 7 + (y + 3) // 4) % 8, core)

    partners = [on_x(1), on_x(3), on_y(1), on_y(3), on_z(1), on_z(7), mate]

    sems = [0]
    pending = []

    def remote(src, dst, where):
        k = sems[0]
        sems[0] += 1
        return pltpu.make_async_remote_copy(
            src_ref=src, dst_ref=dst, send_sem=send_sem.at[k], recv_sem=recv_sem.at[k],
            device_id=where, device_id_type=MESH,
        )

    def go(copy):
        copy.start()
        pending.append(copy)
        return copy

    locs = [0]

    def local(src, dst):
        k = locs[0]
        locs[0] += 1
        copy = pltpu.make_async_copy(src, dst, loc_sem.at[k])
        copy.start()
        return copy

    x_loc = local(xin, xb.at[core])
    col0 = pl.multiple_of(core * 512, 512)
    w_loc = local(win.at[:, pl.ds(col0, 512)], wb.at[ctx])

    def tcol(block, head):
        return tpart.at[:, pl.ds(pl.multiple_of(block * 2048 + head * 256, 256), 256)]

    fp_loc = [local(tcol((x + 1) % 4, i), t_fp.at[i]) for i in range(4)]
    fm_loc = [local(tcol((x + 3) % 4, 4 + i), t_fm.at[i]) for i in range(4)]
    own_loc = [local(tcol(x, i), t_own.at[i]) for i in range(8)]

    barrier = pltpu.get_barrier_semaphore()
    for where in partners:
        pl.semaphore_signal(barrier, inc=1, device_id=where, device_id_type=MESH)
    pl.semaphore_wait(barrier, len(partners))

    m_s1p = [remote(tcol((x + 2) % 4, i), r1p.at[i], on_x(1)) for i in range(4)]
    m_s1m = [remote(tcol((x + 2) % 4, 4 + i), r1m.at[i], on_x(3)) for i in range(4)]
    m_dp = [remote(tcol((x + 1) % 4, 4 + i), rdp.at[i], on_x(1)) for i in range(4)]
    m_dm = [remote(tcol((x + 3) % 4, i), rdm.at[i], on_x(3)) for i in range(4)]
    m_s2p = [remote(r1p.at[i], r2p.at[i], on_x(1)) for i in range(4)]
    m_s2m = [remote(r1m.at[i], r2m.at[i], on_x(3)) for i in range(4)]
    m_ta = [remote(tt.at[i], tx.at[0, i], nxt) for i in range(4)]
    m_tb = [remote(tt.at[4 + i], tx.at[1, i], prv) for i in range(4)]
    m_x = remote(xin, xb.at[core], mate)

    def block(dy, dz):
        return ((zl + dz) % 4) * 4 + (y + dy) % 4

    def gather_messages(kind):
        base = kind * 128

        def at(dp_, dq_):
            return block(dq_, dp_) if kind == 0 else block(dp_, dq_)

        def to(which, sign):
            on_z_axis = (kind == 0) == (which == "p")
            k = 1 if sign > 0 else -1
            return on_z(k % 8) if on_z_axis else on_y(k % 4)

        def piece(dp_, dq_, part):
            start, size = {"all": (0, 128), "lo": (0, 64), "hi": (64, 64)}[part]
            b = at(dp_, dq_)
            return wb.at[b, pl.ds(base + start, size)]

        def message(dp_, dq_, part, which, sign):
            ref = piece(dp_, dq_, part)
            return remote(ref, ref, to(which, sign))

        own = win.at[pl.ds(base, 128), pl.ds(col0, 512)]

        def first(which, sign):
            return remote(own, piece(0, 0, "all"), to(which, sign))

        return [
            first("p", 1), first("p", -1), first("q", 1), first("q", -1),
            message(-1, 0, "lo", "p", 1), message(1, 0, "hi", "p", -1),
            message(-1, 0, "all", "q", 1), message(-1, 0, "all", "q", -1),
            message(1, 0, "all", "q", 1), message(1, 0, "all", "q", -1),
            message(0, -1, "lo", "q", 1), message(0, 1, "hi", "q", -1),
            message(2, 0, "all", "q", 1), message(2, 0, "all", "q", -1),
            message(-1, -1, "lo", "q", 1), message(-1, 1, "hi", "q", -1),
            message(1, -1, "lo", "q", 1), message(1, 1, "hi", "q", -1),
            message(2, -1, "lo", "q", 1), message(2, 1, "hi", "q", -1),
        ]

    ag = [gather_messages(0), gather_messages(1)]

    def ag_start(*ids):
        for k in ids:
            for kind in (0, 1):
                go(ag[kind][k])

    def ag_wait(*ids):
        for k in ids:
            for kind in (0, 1):
                ag[kind][k].wait_recv()

    go(m_s1p[0]); go(m_s1m[0])
    ag_start(0, 1)
    go(m_s1p[1]); go(m_s1m[1]); go(m_dp[0]); go(m_dm[0])
    ag_start(2, 3)
    go(m_x)

    window = ctx
    valid = valid_ref[0]

    def seg_row(w):
        return seg_ref[:, pl.ds(pl.multiple_of(w * 256, 256), 256)].astype(F32)

    row_own = seg_row(window)
    row_next = seg_row((window + 1) % 16)
    col_own = jnp.transpose(jnp.broadcast_to(row_own, (256, 256)))
    col_prev = jnp.transpose(jnp.broadcast_to(seg_row((window + 15) % 16), (256, 256)))
    key_iota = lax.broadcasted_iota(jnp.int32, (256, 256), 0)
    query_iota = lax.broadcasted_iota(jnp.int32, (256, 256), 1)
    key_own = key_iota + window * 256
    key_prev = key_own - 256
    query_next = query_iota + (window + 1) * 256
    mo[...] = jnp.where((col_own == row_own) & (key_own < valid), 0.0, NEG)
    mp[...] = jnp.where((col_prev == row_own) & (key_prev >= 0) & (key_prev < valid), 0.0, NEG)
    mn[...] = jnp.where((col_own == row_next) & (key_own < valid) & (query_next < 4096), 0.0, NEG)
    lane = lax.broadcasted_iota(jnp.int32, (1, 256), 1)
    live_own = jnp.where(lane + window * 256 < valid, 1.0, 0.0).astype(F32)
    live_next = jnp.where(
        (lane + (window + 1) * 256 < valid) & (lane + (window + 1) * 256 < 4096), 1.0, 0.0
    ).astype(F32)

    acc[...] = jnp.zeros_like(acc)

    def feed(dy, dz):
        b = block(dy, dz)
        xs = xb[:, :, pl.ds(pl.multiple_of(b * 256, 256), 256)].reshape(512, 256)
        acc[...] += dot_nn(xs, wb[b])

    def relay(i):
        m_s1p[i].wait_recv()
        fp_loc[i].wait()
        r1p[i] = (r1p[i].astype(F32) + t_fp[i].astype(F32)).astype(BF16)
        go(m_s2p[i])
        m_s1m[i].wait_recv()
        fm_loc[i].wait()
        r1m[i] = (r1m[i].astype(F32) + t_fm[i].astype(F32)).astype(BF16)
        go(m_s2m[i])

    def settle(i):
        m_s2p[i].wait_recv()
        m_dm[i].wait_recv()
        own_loc[i].wait()
        tt[i] = (t_own[i].astype(F32) + r2p[i].astype(F32) + rdm[i].astype(F32)).astype(BF16)
        go(m_ta[i])
        m_s2m[i].wait_recv()
        m_dp[i].wait_recv()
        own_loc[4 + i].wait()
        tt[4 + i] = (
            t_own[4 + i].astype(F32) + r2m[i].astype(F32) + rdp[i].astype(F32)
        ).astype(BF16)
        go(m_tb[i])

    ag_wait(0, 1)
    ag_start(4, 5, 6, 7, 8, 9)
    relay(0)
    go(m_s1p[2]); go(m_s1m[2]); go(m_dp[1]); go(m_dm[1])
    ag_wait(2, 3)
    ag_start(10, 11)
    x_loc.wait()
    w_loc.wait()
    m_x.wait_recv()
    feed(0, 0)
    relay(1)
    go(m_s1p[3]); go(m_s1m[3]); go(m_dp[2]); go(m_dm[2])
    ag_wait(4, 5)
    ag_start(12, 13)
    feed(1, 0)
    feed(-1, 0)
    feed(0, 1)
    feed(0, -1)
    ag_wait(6, 7, 8, 9)
    ag_start(14, 15, 16, 17)
    settle(0)
    relay(2)
    go(m_dp[3]); go(m_dm[3])
    feed(1, 1)
    feed(-1, 1)
    feed(1, -1)
    feed(-1, -1)
    ag_wait(12, 13)
    ag_start(18, 19)
    ag_wait(10, 11)
    feed(2, 0)
    feed(0, 2)
    settle(1)
    ag_wait(14, 15, 16, 17)
    feed(2, 1)
    feed(2, -1)
    feed(1, 2)
    feed(-1, 2)
    relay(3)
    ag_wait(18, 19)
    feed(2, 2)

    m_so = remote(so, ss.at[pl.ds(core * 4, 4)], mate)

    def half_to(f):
        up = 1 - f
        y_ = (y + 1 + 2 * f) % 4
        z_ = (z + up * ((y + 1) // 4) + f * (7 + (y + 3) // 4)) % 8
        return dev(x, y_, z_, core)

    k_half = sems[0]
    sems[0] += 8

    def half_copy(f, j):
        k = k_half + f * 4 + j
        return pltpu.make_async_remote_copy(
            src_ref=ss.at[f * 4 + j], dst_ref=sx.at[f, j], send_sem=send_sem.at[k],
            recv_sem=recv_sem.at[k], device_id=half_to(f), device_id_type=MESH,
        )

    acc_own = acc[pl.ds(pl.multiple_of(core * 256, 256), 256), :].astype(BF16)
    acc_oth = acc[pl.ds(pl.multiple_of(other * 256, 256), 256), :].astype(BF16)
    for j in range(4):
        so[j] = acc_oth[:, j * 128:(j + 1) * 128]
    go(m_so)
    for j in range(4):
        ss[core * 4 + j] = acc_own[:, j * 128:(j + 1) * 128]
        go(half_copy(core, j))
    for j in range(4):
        st[core * 4 + j] = turned(acc_own[:, j * 128:(j + 1) * 128])
    m_so.wait_recv()
    for j in range(4):
        go(half_copy(other, j))

    def teacher_a(i):
        m_ta[i].wait_recv()
        q = tt[i]
        own = dot_nt(q, q) * T_SCALE + mo[...]
        off = dot_nt(tx[0, i], q) * T_SCALE + mp[...]
        top = jnp.maximum(jnp.max(own, 0, keepdims=True), jnp.max(off, 0, keepdims=True))
        own = own - top
        off = off - top
        zt[i, 0] = own
        zt[i, 1] = off
        total = jnp.sum(jnp.exp(own), 0, keepdims=True) + jnp.sum(jnp.exp(off), 0, keepdims=True)
        lt[i:i + 1] = jnp.log(total)

    def b_stats(own, off, i, row):
        top = jnp.max(own, 0, keepdims=True)
        own = own - top
        st_d[i, row:row + 1] = top
        st_d[i, row + 1:row + 2] = jnp.sum(jnp.exp(own), 0, keepdims=True)
        top = jnp.max(off, 0, keepdims=True)
        off = off - top
        st_n[i, row:row + 1] = top
        st_n[i, row + 1:row + 2] = jnp.sum(jnp.exp(off), 0, keepdims=True)
        return own, off

    def teacher_b(i):
        m_tb[i].wait_recv()
        k = tt[4 + i]
        own = dot_nt(k, k) * T_SCALE + mo[...]
        off = dot_nt(k, tx[1, i]) * T_SCALE + mn[...]
        zt[4 + i, 0], zt[4 + i, 1] = b_stats(own, off, i, 0)

    m_sd = [remote(st_d.at[i], rs_d.at[i], prv) for i in range(4)]
    m_sn = [remote(st_n.at[i], rs_n.at[i], nxt) for i in range(4)]

    def student_b(i):
        half_copy(1, i).wait_recv()
        k = ss[4 + i]
        own = dot_nt(k, k) * S_SCALE + mo[...]
        off = dot_nt(k, sx[1, i]) * S_SCALE + mn[...]
        zs[i, 0], zs[i, 1] = b_stats(own, off, i, 2)
        go(m_sd[i])
        go(m_sn[i])
        sxt[1, i] = turned(sx[1, i])

    def turn_own(j):
        st[other * 4 + j] = turned(ss[other * 4 + j])

    gain_own = live_own * G_SCALE
    gain_next = live_next * G_SCALE

    def grads(t_log, s_log, live, gain):
        t_prob = jnp.exp(t_log)
        s_prob = jnp.exp(s_log)
        loss = jnp.sum(t_prob * (t_log - s_log), 0, keepdims=True) * live
        return loss, ((s_prob - t_prob) * gain).astype(BF16)

    m_h = [remote(hsend.at[i], hrecv.at[i], prv if i < 4 else nxt) for i in range(8)]
    losses = []

    def relate_a(i):
        half_copy(0, i).wait_recv()
        sxt[0, i] = turned(sx[0, i])
        q = ss[i]
        own = dot_nt(q, q) * S_SCALE + mo[...]
        off = dot_nt(sx[0, i], q) * S_SCALE + mp[...]
        top = jnp.maximum(jnp.max(own, 0, keepdims=True), jnp.max(off, 0, keepdims=True))
        own = own - top
        off = off - top
        total = jnp.sum(jnp.exp(own), 0, keepdims=True) + jnp.sum(jnp.exp(off), 0, keepdims=True)
        s_sum = jnp.log(total)
        t_sum = lt[i:i + 1]
        loss_o, g_own = grads(zt[i, 0] - t_sum, own - s_sum, live_own, gain_own)
        loss_p, g_off = grads(zt[i, 1] - t_sum, off - s_sum, live_own, gain_own)
        losses.append(loss_o + loss_p)
        turned_q = st[i]
        hsend[i] = dot_nt(turned_q, g_off).astype(BF16)
        go(m_h[i])
        hacc[i] = dot_nn(sxt[0, i], g_off) + dot_nn(turned_q, g_own) + dot_nt(turned_q, g_own)

    def shifts(m_here, l_here, m_there, l_there):
        top = jnp.maximum(m_here, m_there)
        total = l_here * jnp.exp(m_here - top) + l_there * jnp.exp(m_there - top)
        return (m_here - top) - jnp.log(total)

    def relate_b(i):
        m_sd[i].wait_recv()
        m_sn[i].wait_recv()

        def row(ref, r):
            return ref[i, r:r + 1]

        t_own = shifts(row(st_d, 0), row(st_d, 1), row(rs_n, 0), row(rs_n, 1))
        s_own = shifts(row(st_d, 2), row(st_d, 3), row(rs_n, 2), row(rs_n, 3))
        t_off = shifts(row(st_n, 0), row(st_n, 1), row(rs_d, 0), row(rs_d, 1))
        s_off = shifts(row(st_n, 2), row(st_n, 3), row(rs_d, 2), row(rs_d, 3))
        loss_o, g_own = grads(zt[4 + i, 0] + t_own, zs[i, 0] + s_own, live_own, gain_own)
        loss_n, g_off = grads(zt[4 + i, 1] + t_off, zs[i, 1] + s_off, live_next, gain_next)
        losses.append(loss_o + loss_n)
        turned_k = st[4 + i]
        hsend[4 + i] = dot_nn(turned_k, g_off).astype(BF16)
        go(m_h[4 + i])
        hacc[4 + i] = dot_nn(turned_k, g_own) + dot_nt(turned_k, g_own) + dot_nt(sxt[1, i], g_off)

    def finish_one(i):
        m_h[i].wait_recv()
        full = (hacc[i] + hrecv[i].astype(F32)).astype(BF16)
        ht[i] = full
        return full

    m_ho = [remote(ht.at[other * 4 + j], ho.at[j], mate) for j in range(4)]

    def finish(j):
        low = finish_one(j)
        high = finish_one(4 + j)
        go(m_ho[j])
        h_out[:, j * 128:(j + 1) * 128] = turned(low)
        h_out[:, (4 + j) * 128:(5 + j) * 128] = turned(high)

    first_y = [True, False, True, True]

    def chunk(j):
        m_ho[j].wait_recv()
        mine = ht[core * 4 + j]
        theirs = ho[j]
        for k in range(4):
            part = dot_nn(mine, xb[core, :, k * 1024:(k + 1) * 1024])
            part = part + dot_nn(theirs, xb[other, :, k * 1024:(k + 1) * 1024])
            part = part.astype(BF16)
            for m in range(4):
                piece = part[:, m * 256:(m + 1) * 256]
                if first_y[j]:
                    gb[j, m, k] = piece
                else:
                    gb[j, k, m] = piece

    class Ring:
        def __init__(self, j, along_y, unit, bufs, halves):
            self.me = y if along_y else zl
            up = on_y(1) if along_y else on_z(1)
            down = on_y(3) if along_y else on_z(7)
            self.unit, self.halves = unit, halves
            self.b1p, self.b1m, self.bdp, self.bdm, self.b2p, self.b2m = [b.at[j] for b in bufs]
            lo, hi = halves
            self.s1p = remote(self.at(2, lo), self.b1p, up)
            self.s1m = remote(self.at(2, hi), self.b1m, down)
            self.dp = remote(self.at(1, hi), self.bdp, up)
            self.dm = remote(self.at(3, lo), self.bdm, down)
            self.s2p = remote(self.b1p, self.b2p, up)
            self.s2m = remote(self.b1m, self.b2m, down)

        def at(self, k, half):
            return self.unit.at[(self.me + k) % 4].at[half]

        def far(self):
            go(self.s1p); go(self.s1m)

        def near(self):
            go(self.dp); go(self.dm)

        def middle(self):
            lo, hi = self.halves
            self.s1p.wait_recv()
            self.b1p[...] = (
                self.b1p[...].astype(F32) + self.at(1, lo)[...].astype(F32)
            ).astype(BF16)
            go(self.s2p)
            self.s1m.wait_recv()
            self.b1m[...] = (
                self.b1m[...].astype(F32) + self.at(3, hi)[...].astype(F32)
            ).astype(BF16)
            go(self.s2m)

        def close(self, dst):
            lo, hi = self.halves
            self.s2p.wait_recv()
            self.dm.wait_recv()
            dst.at[lo][...] = (
                self.at(0, lo)[...].astype(F32) + self.b2p[...].astype(F32)
                + self.bdm[...].astype(F32)
            ).astype(BF16)
            self.s2m.wait_recv()
            self.dp.wait_recv()
            dst.at[hi][...] = (
                self.at(0, hi)[...].astype(F32) + self.b2m[...].astype(F32)
                + self.bdp[...].astype(F32)
            ).astype(BF16)

    p_ring = [
        Ring(j, first_y[j], gb.at[j], (p1p, p1m, pdp, pdm, p2p, p2m), (pl.ds(0, 2), pl.ds(2, 2)))
        for j in range(4)
    ]
    q_ring = [
        Ring(j, not first_y[j], qb.at[j], (q1p, q1m, qdp, qdm, q2p, q2m),
             (pl.ds(0, 64), pl.ds(64, 64)))
        for j in range(4)
    ]
    low, high = pl.ds(0, 64), pl.ds(64, 64)
    m_f1 = [
        (remote(fin.at[j, low], fin_m.at[j, low], on_z(2)),
         remote(fin.at[j, high], fin_m.at[j, high], on_z(6)))
        for j in range(4)
    ]
    m_f2 = [
        (remote(fin_m.at[j, low], fin_r.at[j, low], on_z(2)),
         remote(fin_m.at[j, high], fin_r.at[j, high], on_z(6)))
        for j in range(4)
    ]
    m_gf = [remote(gf.at[j], gf_r.at[j], mate) for j in range(4)]

    def to_q(j):
        p_ring[j].close(qb.at[j])
        q_ring[j].far()
        q_ring[j].near()

    def to_pair(j):
        q_ring[j].close(fin.at[j])
        for copy in m_f1[j]:
            go(copy)

    def pass_on(j):
        for come, leave in zip(m_f1[j], m_f2[j]):
            come.wait_recv()
            go(leave)

    def total(j):
        for copy in m_f2[j]:
            copy.wait_recv()
        gf[j] = fin[j].astype(F32) + fin_r[j].astype(F32)
        go(m_gf[j])
        gt_out[:, pl.ds(pl.multiple_of(core * 512 + j * 128, 128), 128)] = jnp.transpose(gf[j])

    def emit(j):
        m_gf[j].wait_recv()
        gt_out[:, pl.ds(pl.multiple_of(other * 512 + j * 128, 128), 128)] = jnp.transpose(gf_r[j])

    def spread(buf, me, where):
        return [go(remote(buf.at[me], buf.at[me], where(k))) for k in (1, 2, 3)]

    def gathered(copies, buf):
        for copy in copies:
            copy.wait_recv()
        return buf[0] + buf[1] + buf[2] + buf[3]

    settle(2)
    teacher_a(0)
    teacher_b(0)
    student_b(0)
    teacher_b(1)
    student_b(1)
    for j in range(4):
        turn_own(j)
    relate_a(0)
    teacher_a(1)
    relate_a(1)
    relate_b(0)
    relate_b(1)
    teacher_b(2)
    student_b(2)
    settle(3)
    teacher_a(2)
    relate_a(2)
    finish(0)
    relate_b(2)
    finish(1)
    teacher_b(3)
    student_b(3)
    teacher_a(3)
    relate_a(3)
    chunk(0)
    p_ring[0].far()
    finish(2)
    chunk(1)
    p_ring[1].far()
    p_ring[1].near()
    relate_b(3)
    p_ring[0].near()
    chunk(2)
    p_ring[2].far()
    loss = losses[0]
    for part in losses[1:]:
        loss = loss + part
    loss = jnp.sum(loss, keepdims=True) * (1.0 / HEADS)
    lx[x] = jnp.broadcast_to(loss, (8, 128))
    c_x = spread(lx, x, on_x)
    p_ring[0].middle()
    p_ring[2].near()
    finish(3)
    chunk(3)
    p_ring[3].far()
    p_ring[1].middle()
    p_ring[2].middle()
    p_ring[3].near()
    to_q(0)
    to_q(1)
    p_ring[3].middle()
    ly[y] = gathered(c_x, lx)
    c_y = spread(ly, y, on_y)
    q_ring[0].middle()
    q_ring[1].middle()
    to_q(2)
    to_pair(0)
    to_pair(1)
    q_ring[2].middle()
    pass_on(0)
    pass_on(1)
    to_q(3)
    to_pair(2)
    lz[zl] = gathered(c_y, ly)
    c_z = spread(lz, zl, on_zl)
    q_ring[3].middle()
    pass_on(2)
    total(0)
    total(1)
    emit(0)
    to_pair(3)
    emit(1)
    total(2)
    pass_on(3)
    emit(2)
    loss_out[...] = gathered(c_z, lz)
    total(3)
    emit(3)
    for copy in pending:
        copy.wait_send()


def results(h_ref, g_ref, l_ref, loss_ref, wo_ref, state_ref):
    loss_ref[0] = jnp.max(l_ref[0:1, 0:1])
    wo_ref[...] = g_ref[...]
    state_ref[...] = h_ref[...].astype(F32) * UNSCALE


def per_device(teacher_part, student_in, out_proj, segment_ids, valid_count):
    anywhere = pl.BlockSpec(memory_space=pltpu.HBM)
    vmem = pl.BlockSpec(memory_space=pltpu.VMEM)

    def b(*shape):
        return pltpu.VMEM(shape, BF16)

    def f(*shape):
        return pltpu.VMEM(shape, F32)

    scratch = [b(2, 256, 4096), b(16, 256, 512), f(512, 512)]
    scratch += [b(8, 256, 256)] + [b(4, 256, 256)] * 8 + [b(8, 256, 256), b(2, 4, 256, 256)]
    scratch += [b(8, 256, 128), b(4, 256, 128), b(2, 4, 256, 128), b(8, 128, 256), b(2, 4, 128, 256)]
    scratch += [f(256, 256)] * 3 + [f(8, 2, 256, 256), f(8, 256), f(4, 2, 256, 256)]
    scratch += [f(4, 4, 256)] * 4
    scratch += [f(8, 128, 256)] + [b(8, 128, 256)] * 3 + [b(4, 128, 256)]
    scratch += [b(4, 4, 4, 128, 256)] + [b(4, 2, 128, 256)] * 6
    scratch += [b(4, 4, 128, 256)] + [b(4, 64, 256)] * 6
    scratch += [b(4, 128, 256)] * 3 + [f(4, 128, 256)] * 2
    scratch += [f(4, 8, 128)] * 3
    scratch += [
        pltpu.SemaphoreType.DMA((N_SEM,)), pltpu.SemaphoreType.DMA((N_SEM,)),
        pltpu.SemaphoreType.DMA((24,)),
    ]
    hidden_grad, wo_grad, loss = pl.pallas_call(
        kernel,
        out_shape=(
            jax.ShapeDtypeStruct((256, 1024), BF16),
            jax.ShapeDtypeStruct((256, 1024), F32),
            jax.ShapeDtypeStruct((8, 128), F32),
        ),
        in_specs=[anywhere, anywhere, anywhere, vmem, pl.BlockSpec(memory_space=pltpu.SMEM)],
        out_specs=(vmem, vmem, vmem),
        scratch_shapes=scratch,
        name="relation_step",
        compiler_params=pltpu.CompilerParams(
            collective_id=0, has_side_effects=True, vmem_limit_bytes=60 * 2**20
        ),
    )(teacher_part[0, 0], student_in[0], out_proj, segment_ids, valid_count)
    doc_loss, wo_grad, state_grad = pl.pallas_call(
        results,
        out_shape=(
            jax.ShapeDtypeStruct((1,), F32),
            jax.ShapeDtypeStruct((256, 1024), F32),
            jax.ShapeDtypeStruct((256, 1024), F32),
        ),
        in_specs=[vmem, vmem, vmem],
        out_specs=(pl.BlockSpec(memory_space=pltpu.SMEM), vmem, vmem),
        name="results",
        compiler_params=pltpu.CompilerParams(vmem_limit_bytes=16 * 2**20),
    )(hidden_grad, wo_grad, loss)
    return (doc_loss, wo_grad, state_grad[None])


def solution(mesh):
    return jax.shard_map(
        per_device,
        mesh=mesh,
        in_specs=(
            P("dp", "tp", "ctx", None),
            P("dp", "ctx", None),
            P("ctx", "tp"),
            P("dp", None),
            P("dp"),
        ),
        out_specs=(P("dp"), P("ctx", "tp"), P("dp", "ctx", "tp")),
        check_vma=False,
    )
```

```python
import math

import jax
import jax.numpy as jnp
from jax import lax
from jax.experimental import pallas as pl
from jax.experimental.pallas import tpu as pltpu
from jax.sharding import PartitionSpec as P

DS = 4096
HEADS = 32
MESH = pl.DeviceIdType.MESH
F32 = jnp.float32
BF16 = jnp.bfloat16
NEG = -1e30
UNSCALE = HEADS * math.sqrt(DS // HEADS)
T_SCALE = 1.0 / math.sqrt(256)
S_SCALE = 1.0 / math.sqrt(128)
G_SCALE = S_SCALE / HEADS
N_SEM = 224


def dot_nn(a, b):
    return lax.dot_general(a, b, (((1,), (0,)), ((), ())), preferred_element_type=F32)


def dot_nt(a, b):
    return lax.dot_general(a, b, (((1,), (1,)), ((), ())), preferred_element_type=F32)


def turned(a):
    return jnp.transpose(a.astype(F32)).astype(BF16)


def kernel(
    tpart, xin, win, seg_ref, valid_ref,
    h_out, gt_out, loss_out,
    xb, wb, acc,
    t_own, t_fp, t_fm, r1p, r1m, rdp, rdm, r2p, r2m, tt, tx,
    ss, so, sx, st, sxt,
    mo, mp, mn, zt, lt, zs, st_d, st_n, rs_d, rs_n,
    hacc, hsend, hrecv, ht, ho,
    gb, p1p, p1m, pdp, pdm, p2p, p2m, qb, q1p, q1m, qdp, qdm, q2p, q2m, fin, fin_m, fin_r, gf, gf_r,
    lx, ly, lz,
    send_sem, recv_sem, loc_sem,
):
    dp, ctx, x = lax.axis_index("dp"), lax.axis_index("ctx"), lax.axis_index("tp")
    core, zh, zl, y = dp % 2, dp // 2, ctx // 4, ctx % 4
    z = zh * 4 + zl
    other = 1 - core

    def dev(x_, y_, z_, c_):
        return ((z_ // 4) * 2 + c_, (z_ % 4) * 4 + y_, x_)

    def on_x(k):
        return dev((x + k) % 4, y, z, core)

    def on_y(k):
        return dev(x, (y + k) % 4, z, core)

    def on_z(k):
        return dev(x, y, (z + k) % 8, core)

    def on_zl(k):
        return dev(x, y, zh * 4 + (zl + k) % 4, core)

    mate = dev(x, y, z, other)
    nxt = dev(x, (y + 1) % 4, (z + (y + 1) // 4) % 8, core)
    prv = dev(x, (y + 3) % 4, (z + 7 + (y + 3) // 4) % 8, core)

    partners = [on_x(1), on_x(3), on_y(1), on_y(3), on_z(1), on_z(7), mate]

    sems = [0]
    pending = []

    def remote(src, dst, where):
        k = sems[0]
        sems[0] += 1
        return pltpu.make_async_remote_copy(
            src_ref=src, dst_ref=dst, send_sem=send_sem.at[k], recv_sem=recv_sem.at[k],
            device_id=where, device_id_type=MESH,
        )

    def go(copy):
        copy.start()
        pending.append(copy)
        return copy

    locs = [0]

    def local(src, dst):
        k = locs[0]
        locs[0] += 1
        copy = pltpu.make_async_copy(src, dst, loc_sem.at[k])
        copy.start()
        return copy

    x_loc = local(xin, xb.at[core])
    col0 = pl.multiple_of(core * 512, 512)
    w_loc = local(win.at[:, pl.ds(col0, 512)], wb.at[ctx])

    def tcol(block, head):
        return tpart.at[:, pl.ds(pl.multiple_of(block * 2048 + head * 256, 256), 256)]

    fp_loc = [local(tcol((x + 1) % 4, i), t_fp.at[i]) for i in range(4)]
    fm_loc = [local(tcol((x + 3) % 4, 4 + i), t_fm.at[i]) for i in range(4)]
    own_loc = [local(tcol(x, i), t_own.at[i]) for i in range(8)]

    barrier = pltpu.get_barrier_semaphore()
    for where in partners:
        pl.semaphore_signal(barrier, inc=1, device_id=where, device_id_type=MESH)
    pl.semaphore_wait(barrier, len(partners))

    m_s1p = [remote(tcol((x + 2) % 4, i), r1p.at[i], on_x(1)) for i in range(4)]
    m_s1m = [remote(tcol((x + 2) % 4, 4 + i), r1m.at[i], on_x(3)) for i in range(4)]
    m_dp = [remote(tcol((x + 1) % 4, 4 + i), rdp.at[i], on_x(1)) for i in range(4)]
    m_dm = [remote(tcol((x + 3) % 4, i), rdm.at[i], on_x(3)) for i in range(4)]
    m_s2p = [remote(r1p.at[i], r2p.at[i], on_x(1)) for i in range(4)]
    m_s2m = [remote(r1m.at[i], r2m.at[i], on_x(3)) for i in range(4)]
    m_ta = [remote(tt.at[i], tx.at[0, i], nxt) for i in range(4)]
    m_tb = [remote(tt.at[4 + i], tx.at[1, i], prv) for i in range(4)]
    m_x = remote(xin, xb.at[core], mate)

    def block(dy, dz):
        return ((zl + dz) % 4) * 4 + (y + dy) % 4

    def gather_messages(kind):
        base = kind * 128

        def at(dp_, dq_):
            return block(dq_, dp_) if kind == 0 else block(dp_, dq_)

        def to(which, sign):
            on_z_axis = (kind == 0) == (which == "p")
            k = 1 if sign > 0 else -1
            return on_z(k % 8) if on_z_axis else on_y(k % 4)

        def piece(dp_, dq_, part):
            start, size = {"all": (0, 128), "lo": (0, 64), "hi": (64, 64)}[part]
            b = at(dp_, dq_)
            return wb.at[b, pl.ds(base + start, size)]

        def message(dp_, dq_, part, which, sign):
            ref = piece(dp_, dq_, part)
            return remote(ref, ref, to(which, sign))

        own = win.at[pl.ds(base, 128), pl.ds(col0, 512)]

        def first(which, sign):
            return remote(own, piece(0, 0, "all"), to(which, sign))

        return [
            first("p", 1), first("p", -1), first("q", 1), first("q", -1),
            message(-1, 0, "lo", "p", 1), message(1, 0, "hi", "p", -1),
            message(-1, 0, "all", "q", 1), message(-1, 0, "all", "q", -1),
            message(1, 0, "all", "q", 1), message(1, 0, "all", "q", -1),
            message(0, -1, "lo", "q", 1), message(0, 1, "hi", "q", -1),
            message(2, 0, "all", "q", 1), message(2, 0, "all", "q", -1),
            message(-1, -1, "lo", "q", 1), message(-1, 1, "hi", "q", -1),
            message(1, -1, "lo", "q", 1), message(1, 1, "hi", "q", -1),
            message(2, -1, "lo", "q", 1), message(2, 1, "hi", "q", -1),
        ]

    ag = [gather_messages(0), gather_messages(1)]

    def ag_start(*ids):
        for k in ids:
            for kind in (0, 1):
                go(ag[kind][k])

    def ag_wait(*ids):
        for k in ids:
            for kind in (0, 1):
                ag[kind][k].wait_recv()

    go(m_s1p[0]); go(m_s1m[0])
    ag_start(0, 1)
    go(m_s1p[1]); go(m_s1m[1]); go(m_dp[0]); go(m_dm[0])
    ag_start(2, 3)
    go(m_x)

    window = ctx
    valid = valid_ref[0]

    def seg_row(w):
        return seg_ref[:, pl.ds(pl.multiple_of(w * 256, 256), 256)].astype(F32)

    row_own = seg_row(window)
    row_next = seg_row((window + 1) % 16)
    col_own = jnp.transpose(jnp.broadcast_to(row_own, (256, 256)))
    col_prev = jnp.transpose(jnp.broadcast_to(seg_row((window + 15) % 16), (256, 256)))
    key_iota = lax.broadcasted_iota(jnp.int32, (256, 256), 0)
    query_iota = lax.broadcasted_iota(jnp.int32, (256, 256), 1)
    key_own = key_iota + window * 256
    key_prev = key_own - 256
    query_next = query_iota + (window + 1) * 256
    mo[...] = jnp.where((col_own == row_own) & (key_own < valid), 0.0, NEG)
    mp[...] = jnp.where((col_prev == row_own) & (key_prev >= 0) & (key_prev < valid), 0.0, NEG)
    mn[...] = jnp.where((col_own == row_next) & (key_own < valid) & (query_next < 4096), 0.0, NEG)
    lane = lax.broadcasted_iota(jnp.int32, (1, 256), 1)
    live_own = jnp.where(lane + window * 256 < valid, 1.0, 0.0).astype(F32)
    live_next = jnp.where(
        (lane + (window + 1) * 256 < valid) & (lane + (window + 1) * 256 < 4096), 1.0, 0.0
    ).astype(F32)

    acc[...] = jnp.zeros_like(acc)

    def feed(dy, dz):
        b = block(dy, dz)
        xs = xb[:, :, pl.ds(pl.multiple_of(b * 256, 256), 256)].reshape(512, 256)
        acc[...] += dot_nn(xs, wb[b])

    def relay(i):
        m_s1p[i].wait_recv()
        fp_loc[i].wait()
        r1p[i] = (r1p[i].astype(F32) + t_fp[i].astype(F32)).astype(BF16)
        go(m_s2p[i])
        m_s1m[i].wait_recv()
        fm_loc[i].wait()
        r1m[i] = (r1m[i].astype(F32) + t_fm[i].astype(F32)).astype(BF16)
        go(m_s2m[i])

    def settle(i):
        m_s2p[i].wait_recv()
        m_dm[i].wait_recv()
        own_loc[i].wait()
        tt[i] = (t_own[i].astype(F32) + r2p[i].astype(F32) + rdm[i].astype(F32)).astype(BF16)
        go(m_ta[i])
        m_s2m[i].wait_recv()
        m_dp[i].wait_recv()
        own_loc[4 + i].wait()
        tt[4 + i] = (
            t_own[4 + i].astype(F32) + r2m[i].astype(F32) + rdp[i].astype(F32)
        ).astype(BF16)
        go(m_tb[i])

    ag_wait(0, 1)
    ag_start(4, 5, 6, 7, 8, 9)
    relay(0)
    go(m_s1p[2]); go(m_s1m[2]); go(m_dp[1]); go(m_dm[1])
    ag_wait(2, 3)
    ag_start(10, 11)
    x_loc.wait()
    w_loc.wait()
    m_x.wait_recv()
    feed(0, 0)
    relay(1)
    go(m_s1p[3]); go(m_s1m[3]); go(m_dp[2]); go(m_dm[2])
    ag_wait(4, 5)
    ag_start(12, 13)
    feed(1, 0)
    feed(-1, 0)
    feed(0, 1)
    feed(0, -1)
    ag_wait(6, 7, 8, 9)
    ag_start(14, 15, 16, 17)
    settle(0)
    relay(2)
    go(m_dp[3]); go(m_dm[3])
    feed(1, 1)
    feed(-1, 1)
    feed(1, -1)
    feed(-1, -1)
    ag_wait(12, 13)
    ag_start(18, 19)
    ag_wait(10, 11)
    feed(2, 0)
    feed(0, 2)
    settle(1)
    ag_wait(14, 15, 16, 17)
    feed(2, 1)
    feed(2, -1)
    feed(1, 2)
    feed(-1, 2)
    relay(3)
    ag_wait(18, 19)
    feed(2, 2)

    m_so = remote(so, ss.at[pl.ds(core * 4, 4)], mate)

    def half_to(f):
        up = 1 - f
        y_ = (y + 1 + 2 * f) % 4
        z_ = (z + up * ((y + 1) // 4) + f * (7 + (y + 3) // 4)) % 8
        return dev(x, y_, z_, core)

    k_half = sems[0]
    sems[0] += 8

    def half_copy(f, j):
        k = k_half + f * 4 + j
        return pltpu.make_async_remote_copy(
            src_ref=ss.at[f * 4 + j], dst_ref=sx.at[f, j], send_sem=send_sem.at[k],
            recv_sem=recv_sem.at[k], device_id=half_to(f), device_id_type=MESH,
        )

    acc_own = acc[pl.ds(pl.multiple_of(core * 256, 256), 256), :].astype(BF16)
    acc_oth = acc[pl.ds(pl.multiple_of(other * 256, 256), 256), :].astype(BF16)
    for j in range(4):
        so[j] = acc_oth[:, j * 128:(j + 1) * 128]
    go(m_so)
    for j in range(4):
        ss[core * 4 + j] = acc_own[:, j * 128:(j + 1) * 128]
        go(half_copy(core, j))
    for j in range(4):
        st[core * 4 + j] = turned(acc_own[:, j * 128:(j + 1) * 128])
    m_so.wait_recv()
    for j in range(4):
        go(half_copy(other, j))

    def teacher_a(i):
        m_ta[i].wait_recv()
        q = tt[i]
        own = dot_nt(q, q) * T_SCALE + mo[...]
        off = dot_nt(tx[0, i], q) * T_SCALE + mp[...]
        top = jnp.maximum(jnp.max(own, 0, keepdims=True), jnp.max(off, 0, keepdims=True))
        own = own - top
        off = off - top
        zt[i, 0] = own
        zt[i, 1] = off
        total = jnp.sum(jnp.exp(own), 0, keepdims=True) + jnp.sum(jnp.exp(off), 0, keepdims=True)
        lt[i:i + 1] = jnp.log(total)

    def b_stats(own, off, i, row):
        top = jnp.max(own, 0, keepdims=True)
        own = own - top
        st_d[i, row:row + 1] = top
        st_d[i, row + 1:row + 2] = jnp.sum(jnp.exp(own), 0, keepdims=True)
        top = jnp.max(off, 0, keepdims=True)
        off = off - top
        st_n[i, row:row + 1] = top
        st_n[i, row + 1:row + 2] = jnp.sum(jnp.exp(off), 0, keepdims=True)
        return own, off

    def teacher_b(i):
        m_tb[i].wait_recv()
        k = tt[4 + i]
        own = dot_nt(k, k) * T_SCALE + mo[...]
        off = dot_nt(k, tx[1, i]) * T_SCALE + mn[...]
        zt[4 + i, 0], zt[4 + i, 1] = b_stats(own, off, i, 0)

    m_sd = [remote(st_d.at[i], rs_d.at[i], prv) for i in range(4)]
    m_sn = [remote(st_n.at[i], rs_n.at[i], nxt) for i in range(4)]

    def student_b(i):
        half_copy(1, i).wait_recv()
        k = ss[4 + i]
        own = dot_nt(k, k) * S_SCALE + mo[...]
        off = dot_nt(k, sx[1, i]) * S_SCALE + mn[...]
        zs[i, 0], zs[i, 1] = b_stats(own, off, i, 2)
        go(m_sd[i])
        go(m_sn[i])
        sxt[1, i] = turned(sx[1, i])

    def turn_own(j):
        st[other * 4 + j] = turned(ss[other * 4 + j])

    gain_own = live_own * G_SCALE
    gain_next = live_next * G_SCALE

    def grads(t_log, s_log, live, gain):
        t_prob = jnp.exp(t_log)
        s_prob = jnp.exp(s_log)
        loss = jnp.sum(t_prob * (t_log - s_log), 0, keepdims=True) * live
        return loss, ((s_prob - t_prob) * gain).astype(BF16)

    m_h = [remote(hsend.at[i], hrecv.at[i], prv if i < 4 else nxt) for i in range(8)]
    losses = []

    def relate_a(i):
        half_copy(0, i).wait_recv()
        sxt[0, i] = turned(sx[0, i])
        q = ss[i]
        own = dot_nt(q, q) * S_SCALE + mo[...]
        off = dot_nt(sx[0, i], q) * S_SCALE + mp[...]
        top = jnp.maximum(jnp.max(own, 0, keepdims=True), jnp.max(off, 0, keepdims=True))
        own = own - top
        off = off - top
        total = jnp.sum(jnp.exp(own), 0, keepdims=True) + jnp.sum(jnp.exp(off), 0, keepdims=True)
        s_sum = jnp.log(total)
        t_sum = lt[i:i + 1]
        loss_o, g_own = grads(zt[i, 0] - t_sum, own - s_sum, live_own, gain_own)
        loss_p, g_off = grads(zt[i, 1] - t_sum, off - s_sum, live_own, gain_own)
        losses.append(loss_o + loss_p)
        turned_q = st[i]
        hsend[i] = dot_nt(turned_q, g_off).astype(BF16)
        go(m_h[i])
        hacc[i] = dot_nn(sxt[0, i], g_off) + dot_nn(turned_q, g_own) + dot_nt(turned_q, g_own)

    def shifts(m_here, l_here, m_there, l_there):
        top = jnp.maximum(m_here, m_there)
        total = l_here * jnp.exp(m_here - top) + l_there * jnp.exp(m_there - top)
        return (m_here - top) - jnp.log(total)

    def relate_b(i):
        m_sd[i].wait_recv()
        m_sn[i].wait_recv()

        def row(ref, r):
            return ref[i, r:r + 1]

        t_own = shifts(row(st_d, 0), row(st_d, 1), row(rs_n, 0), row(rs_n, 1))
        s_own = shifts(row(st_d, 2), row(st_d, 3), row(rs_n, 2), row(rs_n, 3))
        t_off = shifts(row(st_n, 0), row(st_n, 1), row(rs_d, 0), row(rs_d, 1))
        s_off = shifts(row(st_n, 2), row(st_n, 3), row(rs_d, 2), row(rs_d, 3))
        loss_o, g_own = grads(zt[4 + i, 0] + t_own, zs[i, 0] + s_own, live_own, gain_own)
        loss_n, g_off = grads(zt[4 + i, 1] + t_off, zs[i, 1] + s_off, live_next, gain_next)
        losses.append(loss_o + loss_n)
        turned_k = st[4 + i]
        hsend[4 + i] = dot_nn(turned_k, g_off).astype(BF16)
        go(m_h[4 + i])
        hacc[4 + i] = dot_nn(turned_k, g_own) + dot_nt(turned_k, g_own) + dot_nt(sxt[1, i], g_off)

    def finish_one(i):
        m_h[i].wait_recv()
        full = (hacc[i] + hrecv[i].astype(F32)).astype(BF16)
        ht[i] = full
        return full

    m_ho = [remote(ht.at[other * 4 + j], ho.at[j], mate) for j in range(4)]

    def finish(j):
        low = finish_one(j)
        high = finish_one(4 + j)
        go(m_ho[j])
        h_out[:, j * 128:(j + 1) * 128] = turned(low)
        h_out[:, (4 + j) * 128:(5 + j) * 128] = turned(high)

    first_y = [False, True, True, True]

    def chunk(j):
        m_ho[j].wait_recv()
        mine = ht[core * 4 + j]
        theirs = ho[j]
        for k in range(4):
            part = dot_nn(mine, xb[core, :, k * 1024:(k + 1) * 1024])
            part = part + dot_nn(theirs, xb[other, :, k * 1024:(k + 1) * 1024])
            part = part.astype(BF16)
            for m in range(4):
                piece = part[:, m * 256:(m + 1) * 256]
                if first_y[j]:
                    gb[j, m, k] = piece
                else:
                    gb[j, k, m] = piece

    class Ring:
        def __init__(self, j, along_y, unit, bufs, halves):
            self.me = y if along_y else zl
            up = on_y(1) if along_y else on_z(1)
            down = on_y(3) if along_y else on_z(7)
            self.unit, self.halves = unit, halves
            self.b1p, self.b1m, self.bdp, self.bdm, self.b2p, self.b2m = [b.at[j] for b in bufs]
            lo, hi = halves
            self.s1p = remote(self.at(2, lo), self.b1p, up)
            self.s1m = remote(self.at(2, hi), self.b1m, down)
            self.dp = remote(self.at(1, hi), self.bdp, up)
            self.dm = remote(self.at(3, lo), self.bdm, down)
            self.s2p = remote(self.b1p, self.b2p, up)
            self.s2m = remote(self.b1m, self.b2m, down)

        def at(self, k, half):
            return self.unit.at[(self.me + k) % 4].at[half]

        def far(self):
            go(self.s1p); go(self.s1m)

        def near(self):
            go(self.dp); go(self.dm)

        def middle(self):
            lo, hi = self.halves
            self.s1p.wait_recv()
            self.b1p[...] = (
                self.b1p[...].astype(F32) + self.at(1, lo)[...].astype(F32)
            ).astype(BF16)
            go(self.s2p)
            self.s1m.wait_recv()
            self.b1m[...] = (
                self.b1m[...].astype(F32) + self.at(3, hi)[...].astype(F32)
            ).astype(BF16)
            go(self.s2m)

        def close(self, dst):
            lo, hi = self.halves
            self.s2p.wait_recv()
            self.dm.wait_recv()
            dst.at[lo][...] = (
                self.at(0, lo)[...].astype(F32) + self.b2p[...].astype(F32)
                + self.bdm[...].astype(F32)
            ).astype(BF16)
            self.s2m.wait_recv()
            self.dp.wait_recv()
            dst.at[hi][...] = (
                self.at(0, hi)[...].astype(F32) + self.b2m[...].astype(F32)
                + self.bdp[...].astype(F32)
            ).astype(BF16)

    p_ring = [
        Ring(j, first_y[j], gb.at[j], (p1p, p1m, pdp, pdm, p2p, p2m), (pl.ds(0, 2), pl.ds(2, 2)))
        for j in range(4)
    ]
    q_ring = [
        Ring(j, not first_y[j], qb.at[j], (q1p, q1m, qdp, qdm, q2p, q2m),
             (pl.ds(0, 64), pl.ds(64, 64)))
        for j in range(4)
    ]
    low, high = pl.ds(0, 64), pl.ds(64, 64)
    m_f1 = [
        (remote(fin.at[j, low], fin_m.at[j, low], on_z(2)),
         remote(fin.at[j, high], fin_m.at[j, high], on_z(6)))
        for j in range(4)
    ]
    m_f2 = [
        (remote(fin_m.at[j, low], fin_r.at[j, low], on_z(2)),
         remote(fin_m.at[j, high], fin_r.at[j, high], on_z(6)))
        for j in range(4)
    ]
    m_gf = [remote(gf.at[j], gf_r.at[j], mate) for j in range(4)]

    def to_q(j):
        p_ring[j].close(qb.at[j])
        q_ring[j].far()
        q_ring[j].near()

    def to_pair(j):
        q_ring[j].close(fin.at[j])
        for copy in m_f1[j]:
            go(copy)

    def pass_on(j):
        for come, leave in zip(m_f1[j], m_f2[j]):
            come.wait_recv()
            go(leave)

    def total(j):
        for copy in m_f2[j]:
            copy.wait_recv()
        gf[j] = fin[j].astype(F32) + fin_r[j].astype(F32)
        go(m_gf[j])
        gt_out[:, pl.ds(pl.multiple_of(core * 512 + j * 128, 128), 128)] = jnp.transpose(gf[j])

    def emit(j):
        m_gf[j].wait_recv()
        gt_out[:, pl.ds(pl.multiple_of(other * 512 + j * 128, 128), 128)] = jnp.transpose(gf_r[j])

    def spread(buf, me, where):
        return [go(remote(buf.at[me], buf.at[me], where(k))) for k in (1, 2, 3)]

    def gathered(copies, buf):
        for copy in copies:
            copy.wait_recv()
        return buf[0] + buf[1] + buf[2] + buf[3]

    settle(2)
    teacher_a(0)
    teacher_b(0)
    student_b(0)
    teacher_b(1)
    student_b(1)
    for j in range(4):
        turn_own(j)
    relate_a(0)
    teacher_a(1)
    relate_a(1)
    relate_b(0)
    relate_b(1)
    teacher_b(2)
    student_b(2)
    finish(0)
    settle(3)
    teacher_a(2)
    relate_a(2)
    relate_b(2)
    chunk(0)
    p_ring[0].far()
    p_ring[0].near()
    finish(1)
    teacher_b(3)
    student_b(3)
    teacher_a(3)
    relate_a(3)
    chunk(1)
    p_ring[1].far()
    finish(2)
    p_ring[0].middle()
    relate_b(3)
    p_ring[1].near()
    chunk(2)
    p_ring[2].far()
    loss = losses[0]
    for part in losses[1:]:
        loss = loss + part
    loss = jnp.sum(loss, keepdims=True) * (1.0 / HEADS)
    lx[x] = jnp.broadcast_to(loss, (8, 128))
    c_x = spread(lx, x, on_x)
    p_ring[1].middle()
    p_ring[2].near()
    finish(3)
    chunk(3)
    p_ring[3].far()
    to_q(0)
    p_ring[2].middle()
    p_ring[3].near()
    to_q(1)
    ly[y] = gathered(c_x, lx)
    c_y = spread(ly, y, on_y)
    q_ring[0].middle()
    p_ring[3].middle()
    q_ring[1].middle()
    to_pair(0)
    to_pair(1)
    to_q(2)
    pass_on(0)
    lz[zl] = gathered(c_y, ly)
    c_z = spread(lz, zl, on_zl)
    q_ring[2].middle()
    pass_on(1)
    to_q(3)
    to_pair(2)
    total(0)
    q_ring[3].middle()
    pass_on(2)
    total(1)
    emit(0)
    to_pair(3)
    emit(1)
    loss_out[...] = gathered(c_z, lz)
    total(2)
    pass_on(3)
    emit(2)
    total(3)
    emit(3)
    for copy in pending:
        copy.wait_send()


def results(h_ref, g_ref, l_ref, loss_ref, wo_ref, state_ref):
    loss_ref[0] = jnp.max(l_ref[0:1, 0:1])
    wo_ref[...] = g_ref[...]
    state_ref[...] = h_ref[...].astype(F32) * UNSCALE


def per_device(teacher_part, student_in, out_proj, segment_ids, valid_count):
    anywhere = pl.BlockSpec(memory_space=pltpu.HBM)
    vmem = pl.BlockSpec(memory_space=pltpu.VMEM)

    def b(*shape):
        return pltpu.VMEM(shape, BF16)

    def f(*shape):
        return pltpu.VMEM(shape, F32)

    scratch = [b(2, 256, 4096), b(16, 256, 512), f(512, 512)]
    scratch += [b(8, 256, 256)] + [b(4, 256, 256)] * 8 + [b(8, 256, 256), b(2, 4, 256, 256)]
    scratch += [b(8, 256, 128), b(4, 256, 128), b(2, 4, 256, 128), b(8, 128, 256), b(2, 4, 128, 256)]
    scratch += [f(256, 256)] * 3 + [f(8, 2, 256, 256), f(8, 256), f(4, 2, 256, 256)]
    scratch += [f(4, 4, 256)] * 4
    scratch += [f(8, 128, 256)] + [b(8, 128, 256)] * 3 + [b(4, 128, 256)]
    scratch += [b(4, 4, 4, 128, 256)] + [b(4, 2, 128, 256)] * 6
    scratch += [b(4, 4, 128, 256)] + [b(4, 64, 256)] * 6
    scratch += [b(4, 128, 256)] * 3 + [f(4, 128, 256)] * 2
    scratch += [f(4, 8, 128)] * 3
    scratch += [
        pltpu.SemaphoreType.DMA((N_SEM,)), pltpu.SemaphoreType.DMA((N_SEM,)),
        pltpu.SemaphoreType.DMA((24,)),
    ]
    hidden_grad, wo_grad, loss = pl.pallas_call(
        kernel,
        out_shape=(
            jax.ShapeDtypeStruct((256, 1024), BF16),
            jax.ShapeDtypeStruct((256, 1024), F32),
            jax.ShapeDtypeStruct((8, 128), F32),
        ),
        in_specs=[anywhere, anywhere, anywhere, vmem, pl.BlockSpec(memory_space=pltpu.SMEM)],
        out_specs=(vmem, vmem, vmem),
        scratch_shapes=scratch,
        name="relation_step",
        compiler_params=pltpu.CompilerParams(
            collective_id=0, has_side_effects=True, vmem_limit_bytes=60 * 2**20
        ),
    )(teacher_part[0, 0], student_in[0], out_proj, segment_ids, valid_count)
    doc_loss, wo_grad, state_grad = pl.pallas_call(
        results,
        out_shape=(
            jax.ShapeDtypeStruct((1,), F32),
            jax.ShapeDtypeStruct((256, 1024), F32),
            jax.ShapeDtypeStruct((256, 1024), F32),
        ),
        in_specs=[vmem, vmem, vmem],
        out_specs=(pl.BlockSpec(memory_space=pltpu.SMEM), vmem, vmem),
        name="results",
        compiler_params=pltpu.CompilerParams(vmem_limit_bytes=16 * 2**20),
    )(hidden_grad, wo_grad, loss)
    return (doc_loss, wo_grad, state_grad[None])


def solution(mesh):
    return jax.shard_map(
        per_device,
        mesh=mesh,
        in_specs=(
            P("dp", "tp", "ctx", None),
            P("dp", "ctx", None),
            P("ctx", "tp"),
            P("dp", None),
            P("dp"),
        ),
        out_specs=(P("dp"), P("ctx", "tp"), P("dp", "ctx", "tp")),
        check_vma=False,
    )
```

```python
import math

import jax
import jax.numpy as jnp
from jax import lax
from jax.experimental import pallas as pl
from jax.experimental.pallas import tpu as pltpu
from jax.sharding import PartitionSpec as P

DS = 4096
HEADS = 32
MESH = pl.DeviceIdType.MESH
F32 = jnp.float32
BF16 = jnp.bfloat16
NEG = -1e30
UNSCALE = HEADS * math.sqrt(DS // HEADS)
T_SCALE = 1.0 / math.sqrt(256)
S_SCALE = 1.0 / math.sqrt(128)
G_SCALE = S_SCALE / HEADS
N_SEM = 224


def dot_nn(a, b):
    return lax.dot_general(a, b, (((1,), (0,)), ((), ())), preferred_element_type=F32)


def dot_nt(a, b):
    return lax.dot_general(a, b, (((1,), (1,)), ((), ())), preferred_element_type=F32)


def turned(a):
    return jnp.transpose(a.astype(F32)).astype(BF16)


def neutral_rows():
    return jnp.where(lax.broadcasted_iota(jnp.int32, (4, 256), 0) % 2 == 0, NEG, 0.0).astype(F32)


def kernel(
    tpart, xin, win, seg_ref, valid_ref,
    h_out, gt_out, loss_out,
    xb, wb, acc,
    t_own, t_fp, t_fm, r1p, r1m, rdp, rdm, r2p, r2m, tt, tx,
    ss, so, sx, st, sxt,
    mo, mp, mn, zt, lt, zs, st_d, st_n, rs_d, rs_n,
    hacc, hsend, hrecv, ht, ho,
    gb, p1p, p1m, pdp, pdm, p2p, p2m, qb, q1p, q1m, qdp, qdm, q2p, q2m, fin, fin_r, gf, gf_r,
    lx, ly, lz,
    send_sem, recv_sem, loc_sem,
):
    dp, ctx, x = lax.axis_index("dp"), lax.axis_index("ctx"), lax.axis_index("tp")
    core, zh, zl, y = dp % 2, dp // 2, ctx // 4, ctx % 4
    z = zh * 4 + zl
    other = 1 - core

    def dev(x_, y_, z_, c_):
        return ((z_ // 4) * 2 + c_, (z_ % 4) * 4 + y_, x_)

    def on_x(k):
        return dev((x + k) % 4, y, z, core)

    def on_y(k):
        return dev(x, (y + k) % 4, z, core)

    def on_z(k):
        return dev(x, y, (z + k) % 8, core)

    def on_zl(k):
        return dev(x, y, zh * 4 + (zl + k) % 4, core)

    mate = dev(x, y, z, other)
    nxt = dev(x, (y + 1) % 4, (z + (y + 1) // 4) % 8, core)
    prv = dev(x, (y + 3) % 4, (z + 7 + (y + 3) // 4) % 8, core)

    partners = [on_x(1), on_x(3), on_y(1), on_y(3), on_z(1), on_z(7), mate]

    sems = [0]
    pending = []

    def remote(src, dst, where):
        k = sems[0]
        sems[0] += 1
        return pltpu.make_async_remote_copy(
            src_ref=src, dst_ref=dst, send_sem=send_sem.at[k], recv_sem=recv_sem.at[k],
            device_id=where, device_id_type=MESH,
        )

    def go(copy):
        copy.start()
        pending.append(copy)
        return copy

    has_next, has_prev = ctx < 15, ctx > 0
    guarded = []

    def go_if(cond, copy):
        guarded.append((cond, copy))

        @pl.when(cond)
        def _():
            copy.start()

    def recv_if(cond, copy):
        @pl.when(cond)
        def _():
            copy.wait_recv()

    @pl.when(ctx == 0)
    def _():
        tx[0] = jnp.zeros_like(tx[0])
        sx[0] = jnp.zeros_like(sx[0])
        for i in range(4):
            rs_n[i] = neutral_rows()
            hrecv[4 + i] = jnp.zeros_like(hrecv[4 + i])

    @pl.when(ctx == 15)
    def _():
        tx[1] = jnp.zeros_like(tx[1])
        sx[1] = jnp.zeros_like(sx[1])
        for i in range(4):
            rs_d[i] = neutral_rows()
            hrecv[i] = jnp.zeros_like(hrecv[i])

    locs = [0]

    def local(src, dst):
        k = locs[0]
        locs[0] += 1
        copy = pltpu.make_async_copy(src, dst, loc_sem.at[k])
        copy.start()
        return copy

    x_loc = local(xin, xb.at[core])
    col0 = pl.multiple_of(core * 512, 512)
    w_loc = local(win.at[:, pl.ds(col0, 512)], wb.at[ctx])

    def tcol(block, head):
        return tpart.at[:, pl.ds(pl.multiple_of(block * 2048 + head * 256, 256), 256)]

    fp_loc = [local(tcol((x + 1) % 4, i), t_fp.at[i]) for i in range(4)]
    fm_loc = [local(tcol((x + 3) % 4, 4 + i), t_fm.at[i]) for i in range(4)]
    own_loc = [local(tcol(x, i), t_own.at[i]) for i in range(8)]

    barrier = pltpu.get_barrier_semaphore()
    for where in partners:
        pl.semaphore_signal(barrier, inc=1, device_id=where, device_id_type=MESH)
    pl.semaphore_wait(barrier, len(partners))

    m_s1p = [remote(tcol((x + 2) % 4, i), r1p.at[i], on_x(1)) for i in range(4)]
    m_s1m = [remote(tcol((x + 2) % 4, 4 + i), r1m.at[i], on_x(3)) for i in range(4)]
    m_dp = [remote(tcol((x + 1) % 4, 4 + i), rdp.at[i], on_x(1)) for i in range(4)]
    m_dm = [remote(tcol((x + 3) % 4, i), rdm.at[i], on_x(3)) for i in range(4)]
    m_s2p = [remote(r1p.at[i], r2p.at[i], on_x(1)) for i in range(4)]
    m_s2m = [remote(r1m.at[i], r2m.at[i], on_x(3)) for i in range(4)]
    m_ta = [remote(tt.at[i], tx.at[0, i], nxt) for i in range(4)]
    m_tb = [remote(tt.at[4 + i], tx.at[1, i], prv) for i in range(4)]
    m_x = remote(xin, xb.at[core], mate)

    def block(dy, dz):
        return ((zl + dz) % 4) * 4 + (y + dy) % 4

    def gather_messages(kind):
        base = kind * 128

        def at(dp_, dq_):
            return block(dq_, dp_) if kind == 0 else block(dp_, dq_)

        def to(which, sign):
            on_z_axis = (kind == 0) == (which == "p")
            k = 1 if sign > 0 else -1
            return on_z(k % 8) if on_z_axis else on_y(k % 4)

        def piece(dp_, dq_, part):
            start, size = {"all": (0, 128), "lo": (0, 64), "hi": (64, 64)}[part]
            b = at(dp_, dq_)
            return wb.at[b, pl.ds(base + start, size)]

        def message(dp_, dq_, part, which, sign):
            ref = piece(dp_, dq_, part)
            return remote(ref, ref, to(which, sign))

        own = win.at[pl.ds(base, 128), pl.ds(col0, 512)]

        def first(which, sign):
            return remote(own, piece(0, 0, "all"), to(which, sign))

        return [
            first("p", 1), first("p", -1), first("q", 1), first("q", -1),
            message(-1, 0, "lo", "p", 1), message(1, 0, "hi", "p", -1),
            message(-1, 0, "all", "q", 1), message(-1, 0, "all", "q", -1),
            message(1, 0, "all", "q", 1), message(1, 0, "all", "q", -1),
            message(0, -1, "lo", "q", 1), message(0, 1, "hi", "q", -1),
            message(2, 0, "all", "q", 1), message(2, 0, "all", "q", -1),
            message(-1, -1, "lo", "q", 1), message(-1, 1, "hi", "q", -1),
            message(1, -1, "lo", "q", 1), message(1, 1, "hi", "q", -1),
            message(2, -1, "lo", "q", 1), message(2, 1, "hi", "q", -1),
        ]

    ag = [gather_messages(0), gather_messages(1)]

    def ag_start(*ids):
        for k in ids:
            for kind in (0, 1):
                go(ag[kind][k])

    def ag_wait(*ids):
        for k in ids:
            for kind in (0, 1):
                ag[kind][k].wait_recv()

    go(m_s1p[0]); go(m_s1m[0])
    ag_start(0, 1)
    go(m_s1p[1]); go(m_s1m[1]); go(m_dp[0]); go(m_dm[0])
    ag_start(2, 3)
    go(m_x)

    window = ctx
    valid = valid_ref[0]

    def seg_row(w):
        return seg_ref[:, pl.ds(pl.multiple_of(w * 256, 256), 256)].astype(F32)

    row_own = seg_row(window)
    row_next = seg_row((window + 1) % 16)
    col_own = jnp.transpose(jnp.broadcast_to(row_own, (256, 256)))
    col_prev = jnp.transpose(jnp.broadcast_to(seg_row((window + 15) % 16), (256, 256)))
    key_iota = lax.broadcasted_iota(jnp.int32, (256, 256), 0)
    query_iota = lax.broadcasted_iota(jnp.int32, (256, 256), 1)
    key_own = key_iota + window * 256
    key_prev = key_own - 256
    query_next = query_iota + (window + 1) * 256
    mo[...] = jnp.where((col_own == row_own) & (key_own < valid), 0.0, NEG)
    mp[...] = jnp.where((col_prev == row_own) & (key_prev >= 0) & (key_prev < valid), 0.0, NEG)
    mn[...] = jnp.where((col_own == row_next) & (key_own < valid) & (query_next < 4096), 0.0, NEG)
    lane = lax.broadcasted_iota(jnp.int32, (1, 256), 1)
    live_own = jnp.where(lane + window * 256 < valid, 1.0, 0.0).astype(F32)
    live_next = jnp.where(
        (lane + (window + 1) * 256 < valid) & (lane + (window + 1) * 256 < 4096), 1.0, 0.0
    ).astype(F32)

    acc[...] = jnp.zeros_like(acc)

    def feed(dy, dz):
        b = block(dy, dz)
        xs = xb[:, :, pl.ds(pl.multiple_of(b * 256, 256), 256)].reshape(512, 256)
        acc[...] += dot_nn(xs, wb[b])

    def relay(i):
        m_s1p[i].wait_recv()
        fp_loc[i].wait()
        r1p[i] = (r1p[i].astype(F32) + t_fp[i].astype(F32)).astype(BF16)
        go(m_s2p[i])
        m_s1m[i].wait_recv()
        fm_loc[i].wait()
        r1m[i] = (r1m[i].astype(F32) + t_fm[i].astype(F32)).astype(BF16)
        go(m_s2m[i])

    def settle(i):
        m_s2p[i].wait_recv()
        m_dm[i].wait_recv()
        own_loc[i].wait()
        tt[i] = (t_own[i].astype(F32) + r2p[i].astype(F32) + rdm[i].astype(F32)).astype(BF16)
        go_if(has_next, m_ta[i])
        m_s2m[i].wait_recv()
        m_dp[i].wait_recv()
        own_loc[4 + i].wait()
        tt[4 + i] = (
            t_own[4 + i].astype(F32) + r2m[i].astype(F32) + rdp[i].astype(F32)
        ).astype(BF16)
        go_if(has_prev, m_tb[i])

    ag_wait(0, 1)
    ag_start(4, 5, 6, 7, 8, 9)
    relay(0)
    go(m_s1p[2]); go(m_s1m[2]); go(m_dp[1]); go(m_dm[1])
    ag_wait(2, 3)
    ag_start(10, 11)
    x_loc.wait()
    w_loc.wait()
    m_x.wait_recv()
    feed(0, 0)
    relay(1)
    go(m_s1p[3]); go(m_s1m[3]); go(m_dp[2]); go(m_dm[2])
    ag_wait(4, 5)
    ag_start(12, 13)
    feed(1, 0)
    feed(-1, 0)
    feed(0, 1)
    feed(0, -1)
    ag_wait(6, 7, 8, 9)
    ag_start(14, 15, 16, 17)
    settle(0)
    relay(2)
    go(m_dp[3]); go(m_dm[3])
    feed(1, 1)
    feed(-1, 1)
    feed(1, -1)
    feed(-1, -1)
    ag_wait(12, 13)
    ag_start(18, 19)
    ag_wait(10, 11)
    feed(2, 0)
    feed(0, 2)
    settle(1)
    ag_wait(14, 15, 16, 17)
    feed(2, 1)
    feed(2, -1)
    feed(1, 2)
    feed(-1, 2)
    relay(3)
    ag_wait(18, 19)
    feed(2, 2)

    m_so = remote(so, ss.at[pl.ds(core * 4, 4)], mate)

    def half_to(f):
        up = 1 - f
        y_ = (y + 1 + 2 * f) % 4
        z_ = (z + up * ((y + 1) // 4) + f * (7 + (y + 3) // 4)) % 8
        return dev(x, y_, z_, core)

    k_half = sems[0]
    sems[0] += 8

    def half_copy(f, j):
        k = k_half + f * 4 + j
        return pltpu.make_async_remote_copy(
            src_ref=ss.at[f * 4 + j], dst_ref=sx.at[f, j], send_sem=send_sem.at[k],
            recv_sem=recv_sem.at[k], device_id=half_to(f), device_id_type=MESH,
        )

    acc_own = acc[pl.ds(pl.multiple_of(core * 256, 256), 256), :].astype(BF16)
    acc_oth = acc[pl.ds(pl.multiple_of(other * 256, 256), 256), :].astype(BF16)
    for j in range(4):
        so[j] = acc_oth[:, j * 128:(j + 1) * 128]
    go(m_so)
    for j in range(4):
        ss[core * 4 + j] = acc_own[:, j * 128:(j + 1) * 128]
        go_if(core * ctx + other * (15 - ctx) > 0, half_copy(core, j))
    for j in range(4):
        st[core * 4 + j] = turned(acc_own[:, j * 128:(j + 1) * 128])
    m_so.wait_recv()
    for j in range(4):
        go_if(other * ctx + core * (15 - ctx) > 0, half_copy(other, j))

    def teacher_a(i):
        recv_if(has_prev, m_ta[i])
        q = tt[i]
        own = dot_nt(q, q) * T_SCALE + mo[...]
        off = dot_nt(tx[0, i], q) * T_SCALE + mp[...]
        top = jnp.maximum(jnp.max(own, 0, keepdims=True), jnp.max(off, 0, keepdims=True))
        own = own - top
        off = off - top
        zt[i, 0] = own
        zt[i, 1] = off
        total = jnp.sum(jnp.exp(own), 0, keepdims=True) + jnp.sum(jnp.exp(off), 0, keepdims=True)
        lt[i:i + 1] = jnp.log(total)

    def b_stats(own, off, i, row):
        top = jnp.max(own, 0, keepdims=True)
        own = own - top
        st_d[i, row:row + 1] = top
        st_d[i, row + 1:row + 2] = jnp.sum(jnp.exp(own), 0, keepdims=True)
        top = jnp.max(off, 0, keepdims=True)
        off = off - top
        st_n[i, row:row + 1] = top
        st_n[i, row + 1:row + 2] = jnp.sum(jnp.exp(off), 0, keepdims=True)
        return own, off

    def teacher_b(i):
        recv_if(has_next, m_tb[i])
        k = tt[4 + i]
        own = dot_nt(k, k) * T_SCALE + mo[...]
        off = dot_nt(k, tx[1, i]) * T_SCALE + mn[...]
        zt[4 + i, 0], zt[4 + i, 1] = b_stats(own, off, i, 0)

    m_sd = [remote(st_d.at[i], rs_d.at[i], prv) for i in range(4)]
    m_sn = [remote(st_n.at[i], rs_n.at[i], nxt) for i in range(4)]

    def student_b(i):
        recv_if(has_next, half_copy(1, i))
        k = ss[4 + i]
        own = dot_nt(k, k) * S_SCALE + mo[...]
        off = dot_nt(k, sx[1, i]) * S_SCALE + mn[...]
        zs[i, 0], zs[i, 1] = b_stats(own, off, i, 2)
        go_if(has_prev, m_sd[i])
        go_if(has_next, m_sn[i])
        sxt[1, i] = turned(sx[1, i])

    def turn_own(j):
        st[other * 4 + j] = turned(ss[other * 4 + j])

    gain_own = live_own * G_SCALE
    gain_next = live_next * G_SCALE

    def grads(t_log, s_log, live, gain):
        t_prob = jnp.exp(t_log)
        s_prob = jnp.exp(s_log)
        loss = jnp.sum(t_prob * (t_log - s_log), 0, keepdims=True) * live
        return loss, ((s_prob - t_prob) * gain).astype(BF16)

    m_h = [remote(hsend.at[i], hrecv.at[i], prv if i < 4 else nxt) for i in range(8)]
    losses = []

    def relate_a(i):
        recv_if(has_prev, half_copy(0, i))
        sxt[0, i] = turned(sx[0, i])
        q = ss[i]
        own = dot_nt(q, q) * S_SCALE + mo[...]
        off = dot_nt(sx[0, i], q) * S_SCALE + mp[...]
        top = jnp.maximum(jnp.max(own, 0, keepdims=True), jnp.max(off, 0, keepdims=True))
        own = own - top
        off = off - top
        total = jnp.sum(jnp.exp(own), 0, keepdims=True) + jnp.sum(jnp.exp(off), 0, keepdims=True)
        s_sum = jnp.log(total)
        t_sum = lt[i:i + 1]
        loss_o, g_own = grads(zt[i, 0] - t_sum, own - s_sum, live_own, gain_own)
        loss_p, g_off = grads(zt[i, 1] - t_sum, off - s_sum, live_own, gain_own)
        losses.append(loss_o + loss_p)
        turned_q = st[i]
        hsend[i] = dot_nt(turned_q, g_off).astype(BF16)
        go_if(has_prev, m_h[i])
        hacc[i] = dot_nn(sxt[0, i], g_off) + dot_nn(turned_q, g_own) + dot_nt(turned_q, g_own)

    def shifts(m_here, l_here, m_there, l_there):
        top = jnp.maximum(m_here, m_there)
        total = l_here * jnp.exp(m_here - top) + l_there * jnp.exp(m_there - top)
        return (m_here - top) - jnp.log(total)

    def relate_b(i):
        recv_if(has_next, m_sd[i])
        recv_if(has_prev, m_sn[i])

        def row(ref, r):
            return ref[i, r:r + 1]

        t_own = shifts(row(st_d, 0), row(st_d, 1), row(rs_n, 0), row(rs_n, 1))
        s_own = shifts(row(st_d, 2), row(st_d, 3), row(rs_n, 2), row(rs_n, 3))
        t_off = shifts(row(st_n, 0), row(st_n, 1), row(rs_d, 0), row(rs_d, 1))
        s_off = shifts(row(st_n, 2), row(st_n, 3), row(rs_d, 2), row(rs_d, 3))
        loss_o, g_own = grads(zt[4 + i, 0] + t_own, zs[i, 0] + s_own, live_own, gain_own)
        loss_n, g_off = grads(zt[4 + i, 1] + t_off, zs[i, 1] + s_off, live_next, gain_next)
        losses.append(loss_o + loss_n)
        turned_k = st[4 + i]
        hsend[4 + i] = dot_nn(turned_k, g_off).astype(BF16)
        go_if(has_next, m_h[4 + i])
        hacc[4 + i] = dot_nn(turned_k, g_own) + dot_nt(turned_k, g_own) + dot_nt(sxt[1, i], g_off)

    def finish_one(i):
        recv_if(has_next if i < 4 else has_prev, m_h[i])
        full = (hacc[i] + hrecv[i].astype(F32)).astype(BF16)
        ht[i] = full
        return full

    m_ho = [remote(ht.at[other * 4 + j], ho.at[j], mate) for j in range(4)]

    def finish(j):
        low = finish_one(j)
        high = finish_one(4 + j)
        go(m_ho[j])
        h_out[:, j * 128:(j + 1) * 128] = turned(low)
        h_out[:, (4 + j) * 128:(5 + j) * 128] = turned(high)

    first_y = [True, False, True, True]

    def chunk(j):
        m_ho[j].wait_recv()
        mine = ht[core * 4 + j]
        theirs = ho[j]
        for k in range(4):
            part = dot_nn(mine, xb[core, :, k * 1024:(k + 1) * 1024])
            part = part + dot_nn(theirs, xb[other, :, k * 1024:(k + 1) * 1024])
            part = part.astype(BF16)
            for m in range(4):
                piece = part[:, m * 256:(m + 1) * 256]
                if first_y[j]:
                    gb[j, m, k] = piece
                else:
                    gb[j, k, m] = piece

    class Ring:
        def __init__(self, j, along_y, unit, bufs, halves):
            self.me = y if along_y else zl
            up = on_y(1) if along_y else on_z(1)
            down = on_y(3) if along_y else on_z(7)
            self.unit, self.halves = unit, halves
            self.b1p, self.b1m, self.bdp, self.bdm, self.b2p, self.b2m = [b.at[j] for b in bufs]
            lo, hi = halves
            self.s1p = remote(self.at(2, lo), self.b1p, up)
            self.s1m = remote(self.at(2, hi), self.b1m, down)
            self.dp = remote(self.at(1, hi), self.bdp, up)
            self.dm = remote(self.at(3, lo), self.bdm, down)
            self.s2p = remote(self.b1p, self.b2p, up)
            self.s2m = remote(self.b1m, self.b2m, down)

        def at(self, k, half):
            return self.unit.at[(self.me + k) % 4].at[half]

        def far(self):
            go(self.s1p); go(self.s1m)

        def near(self):
            go(self.dp); go(self.dm)

        def middle(self):
            lo, hi = self.halves
            self.s1p.wait_recv()
            self.b1p[...] = (
                self.b1p[...].astype(F32) + self.at(1, lo)[...].astype(F32)
            ).astype(BF16)
            go(self.s2p)
            self.s1m.wait_recv()
            self.b1m[...] = (
                self.b1m[...].astype(F32) + self.at(3, hi)[...].astype(F32)
            ).astype(BF16)
            go(self.s2m)

        def close(self, dst):
            lo, hi = self.halves
            self.s2p.wait_recv()
            self.dm.wait_recv()
            dst.at[lo][...] = (
                self.at(0, lo)[...].astype(F32) + self.b2p[...].astype(F32)
                + self.bdm[...].astype(F32)
            ).astype(BF16)
            self.s2m.wait_recv()
            self.dp.wait_recv()
            dst.at[hi][...] = (
                self.at(0, hi)[...].astype(F32) + self.b2m[...].astype(F32)
                + self.bdp[...].astype(F32)
            ).astype(BF16)

    p_ring = [
        Ring(j, first_y[j], gb.at[j], (p1p, p1m, pdp, pdm, p2p, p2m), (pl.ds(0, 2), pl.ds(2, 2)))
        for j in range(4)
    ]
    q_ring = [
        Ring(j, not first_y[j], qb.at[j], (q1p, q1m, qdp, qdm, q2p, q2m),
             (pl.ds(0, 64), pl.ds(64, 64)))
        for j in range(4)
    ]
    m_fin = [remote(fin.at[j], fin_r.at[j], on_z(4)) for j in range(4)]
    m_gf = [remote(gf.at[j], gf_r.at[j], mate) for j in range(4)]

    def to_q(j):
        p_ring[j].close(qb.at[j])
        q_ring[j].far()
        q_ring[j].near()

    def to_pair(j):
        q_ring[j].close(fin.at[j])
        go(m_fin[j])

    def total(j):
        m_fin[j].wait_recv()
        gf[j] = fin[j].astype(F32) + fin_r[j].astype(F32)
        go(m_gf[j])
        gt_out[:, pl.ds(pl.multiple_of(core * 512 + j * 128, 128), 128)] = jnp.transpose(gf[j])

    def emit(j):
        m_gf[j].wait_recv()
        gt_out[:, pl.ds(pl.multiple_of(other * 512 + j * 128, 128), 128)] = jnp.transpose(gf_r[j])

    def spread(buf, me, where):
        return [go(remote(buf.at[me], buf.at[me], where(k))) for k in (1, 2, 3)]

    def gathered(copies, buf):
        for copy in copies:
            copy.wait_recv()
        return buf[0] + buf[1] + buf[2] + buf[3]

    settle(2)
    teacher_a(0)
    teacher_b(0)
    student_b(0)
    teacher_b(1)
    student_b(1)
    for j in range(4):
        turn_own(j)
    relate_a(0)
    teacher_a(1)
    relate_a(1)
    relate_b(0)
    relate_b(1)
    teacher_b(2)
    student_b(2)
    settle(3)
    teacher_a(2)
    relate_a(2)
    finish(0)
    relate_b(2)
    finish(1)
    teacher_b(3)
    student_b(3)
    teacher_a(3)
    relate_a(3)
    chunk(0)
    p_ring[0].far()
    finish(2)
    chunk(1)
    p_ring[1].far()
    p_ring[1].near()
    relate_b(3)
    p_ring[0].near()
    chunk(2)
    p_ring[2].far()
    loss = losses[0]
    for part in losses[1:]:
        loss = loss + part
    loss = jnp.sum(loss, keepdims=True) * (1.0 / HEADS)
    lx[x] = jnp.broadcast_to(loss, (8, 128))
    c_x = spread(lx, x, on_x)
    p_ring[0].middle()
    p_ring[2].near()
    finish(3)
    chunk(3)
    p_ring[3].far()
    p_ring[1].middle()
    p_ring[2].middle()
    p_ring[3].near()
    to_q(0)
    to_q(1)
    p_ring[3].middle()
    ly[y] = gathered(c_x, lx)
    c_y = spread(ly, y, on_y)
    q_ring[0].middle()
    q_ring[1].middle()
    to_q(2)
    to_pair(0)
    to_pair(1)
    q_ring[2].middle()
    to_q(3)
    to_pair(2)
    lz[zl] = gathered(c_y, ly)
    c_z = spread(lz, zl, on_zl)
    q_ring[3].middle()
    total(0)
    total(1)
    emit(0)
    to_pair(3)
    emit(1)
    total(2)
    emit(2)
    loss_out[...] = gathered(c_z, lz)
    total(3)
    emit(3)
    for copy in pending:
        copy.wait_send()
    for cond, copy in guarded:

        @pl.when(cond)
        def _():
            copy.wait_send()


def results(h_ref, g_ref, l_ref, loss_ref, wo_ref, state_ref):
    loss_ref[0] = jnp.max(l_ref[0:1, 0:1])
    wo_ref[...] = g_ref[...]
    state_ref[...] = h_ref[...].astype(F32) * UNSCALE


def per_device(teacher_part, student_in, out_proj, segment_ids, valid_count):
    anywhere = pl.BlockSpec(memory_space=pltpu.HBM)
    vmem = pl.BlockSpec(memory_space=pltpu.VMEM)

    def b(*shape):
        return pltpu.VMEM(shape, BF16)

    def f(*shape):
        return pltpu.VMEM(shape, F32)

    scratch = [b(2, 256, 4096), b(16, 256, 512), f(512, 512)]
    scratch += [b(8, 256, 256)] + [b(4, 256, 256)] * 8 + [b(8, 256, 256), b(2, 4, 256, 256)]
    scratch += [b(8, 256, 128), b(4, 256, 128), b(2, 4, 256, 128), b(8, 128, 256), b(2, 4, 128, 256)]
    scratch += [f(256, 256)] * 3 + [f(8, 2, 256, 256), f(8, 256), f(4, 2, 256, 256)]
    scratch += [f(4, 4, 256)] * 4
    scratch += [f(8, 128, 256)] + [b(8, 128, 256)] * 3 + [b(4, 128, 256)]
    scratch += [b(4, 4, 4, 128, 256)] + [b(4, 2, 128, 256)] * 6
    scratch += [b(4, 4, 128, 256)] + [b(4, 64, 256)] * 6
    scratch += [b(4, 128, 256)] * 2 + [f(4, 128, 256)] * 2
    scratch += [f(4, 8, 128)] * 3
    scratch += [
        pltpu.SemaphoreType.DMA((N_SEM,)), pltpu.SemaphoreType.DMA((N_SEM,)),
        pltpu.SemaphoreType.DMA((24,)),
    ]
    hidden_grad, wo_grad, loss = pl.pallas_call(
        kernel,
        out_shape=(
            jax.ShapeDtypeStruct((256, 1024), BF16),
            jax.ShapeDtypeStruct((256, 1024), F32),
            jax.ShapeDtypeStruct((8, 128), F32),
        ),
        in_specs=[anywhere, anywhere, anywhere, vmem, pl.BlockSpec(memory_space=pltpu.SMEM)],
        out_specs=(vmem, vmem, vmem),
        scratch_shapes=scratch,
        name="relation_step",
        compiler_params=pltpu.CompilerParams(
            collective_id=0, has_side_effects=True, vmem_limit_bytes=60 * 2**20
        ),
    )(teacher_part[0, 0], student_in[0], out_proj, segment_ids, valid_count)
    doc_loss, wo_grad, state_grad = pl.pallas_call(
        results,
        out_shape=(
            jax.ShapeDtypeStruct((1,), F32),
            jax.ShapeDtypeStruct((256, 1024), F32),
            jax.ShapeDtypeStruct((256, 1024), F32),
        ),
        in_specs=[vmem, vmem, vmem],
        out_specs=(pl.BlockSpec(memory_space=pltpu.SMEM), vmem, vmem),
        name="results",
        compiler_params=pltpu.CompilerParams(vmem_limit_bytes=16 * 2**20),
    )(hidden_grad, wo_grad, loss)
    return (doc_loss, wo_grad, state_grad[None])


def solution(mesh):
    return jax.shard_map(
        per_device,
        mesh=mesh,
        in_specs=(
            P("dp", "tp", "ctx", None),
            P("dp", "ctx", None),
            P("ctx", "tp"),
            P("dp", None),
            P("dp"),
        ),
        out_specs=(P("dp"), P("ctx", "tp"), P("dp", "ctx", "tp")),
        check_vma=False,
    )
```

```python
import math

import jax
import jax.numpy as jnp
from jax import lax
from jax.experimental import pallas as pl
from jax.experimental.pallas import tpu as pltpu
from jax.sharding import PartitionSpec as P

DS = 4096
HEADS = 32
MESH = pl.DeviceIdType.MESH
F32 = jnp.float32
BF16 = jnp.bfloat16
NEG = -1e30
UNSCALE = HEADS * math.sqrt(DS // HEADS)
T_SCALE = 1.0 / math.sqrt(256)
S_SCALE = 1.0 / math.sqrt(128)
G_SCALE = S_SCALE / HEADS
N_SEM = 224


def dot_nn(a, b):
    return lax.dot_general(a, b, (((1,), (0,)), ((), ())), preferred_element_type=F32)


def dot_nt(a, b):
    return lax.dot_general(a, b, (((1,), (1,)), ((), ())), preferred_element_type=F32)


def turned(a):
    return jnp.transpose(a.astype(F32)).astype(BF16)


def neutral_rows():
    return jnp.where(lax.broadcasted_iota(jnp.int32, (4, 256), 0) % 2 == 0, NEG, 0.0).astype(F32)


def kernel(
    tpart, xin, win, seg_ref, valid_ref,
    h_out, gt_out, loss_out,
    xb, wb, acc,
    t_own, t_fp, t_fm, r1p, r1m, rdp, rdm, r2p, r2m, tt, tx,
    ss, so, sx, st, sxt,
    mo, mp, mn, zt, lt, zs, st_d, st_n, rs_d, rs_n,
    hacc, hsend, hrecv, ht, ho,
    gb, p1p, p1m, pdp, pdm, p2p, p2m, qb, q1p, q1m, qdp, qdm, q2p, q2m, fin, fin_r, gf, gf_r,
    lx, ly, lz,
    send_sem, recv_sem, loc_sem,
):
    dp, ctx, x = lax.axis_index("dp"), lax.axis_index("ctx"), lax.axis_index("tp")
    core, zh, zl, y = dp % 2, dp // 2, ctx // 4, ctx % 4
    z = zh * 4 + zl
    other = 1 - core

    def dev(x_, y_, z_, c_):
        return ((z_ // 4) * 2 + c_, (z_ % 4) * 4 + y_, x_)

    def on_x(k):
        return dev((x + k) % 4, y, z, core)

    def on_y(k):
        return dev(x, (y + k) % 4, z, core)

    def on_z(k):
        return dev(x, y, (z + k) % 8, core)

    def on_zl(k):
        return dev(x, y, zh * 4 + (zl + k) % 4, core)

    mate = dev(x, y, z, other)
    nxt = dev(x, (y + 1) % 4, (z + (y + 1) // 4) % 8, core)
    prv = dev(x, (y + 3) % 4, (z + 7 + (y + 3) // 4) % 8, core)

    partners = [on_x(1), on_x(3), on_y(1), on_y(3), on_z(1), on_z(7), mate]

    sems = [0]
    pending = []

    def remote(src, dst, where):
        k = sems[0]
        sems[0] += 1
        return pltpu.make_async_remote_copy(
            src_ref=src, dst_ref=dst, send_sem=send_sem.at[k], recv_sem=recv_sem.at[k],
            device_id=where, device_id_type=MESH,
        )

    def go(copy):
        copy.start()
        pending.append(copy)
        return copy

    has_next, has_prev = ctx < 15, ctx > 0
    guarded = []

    def go_if(cond, copy):
        guarded.append((cond, copy))

        @pl.when(cond)
        def _():
            copy.start()

    def recv_if(cond, copy):
        @pl.when(cond)
        def _():
            copy.wait_recv()

    @pl.when(ctx == 0)
    def _():
        tx[0] = jnp.zeros_like(tx[0])
        sx[0] = jnp.zeros_like(sx[0])
        for i in range(4):
            rs_n[i] = neutral_rows()
            hrecv[4 + i] = jnp.zeros_like(hrecv[4 + i])

    @pl.when(ctx == 15)
    def _():
        tx[1] = jnp.zeros_like(tx[1])
        sx[1] = jnp.zeros_like(sx[1])
        for i in range(4):
            rs_d[i] = neutral_rows()
            hrecv[i] = jnp.zeros_like(hrecv[i])

    locs = [0]

    def local(src, dst):
        k = locs[0]
        locs[0] += 1
        copy = pltpu.make_async_copy(src, dst, loc_sem.at[k])
        copy.start()
        return copy

    x_loc = local(xin, xb.at[core])
    col0 = pl.multiple_of(core * 512, 512)
    w_loc = local(win.at[:, pl.ds(col0, 512)], wb.at[ctx])

    def tcol(block, head):
        return tpart.at[:, pl.ds(pl.multiple_of(block * 2048 + head * 256, 256), 256)]

    fp_loc = [local(tcol((x + 1) % 4, i), t_fp.at[i]) for i in range(4)]
    fm_loc = [local(tcol((x + 3) % 4, 4 + i), t_fm.at[i]) for i in range(4)]
    own_loc = [local(tcol(x, i), t_own.at[i]) for i in range(8)]

    barrier = pltpu.get_barrier_semaphore()
    for where in partners:
        pl.semaphore_signal(barrier, inc=1, device_id=where, device_id_type=MESH)
    pl.semaphore_wait(barrier, len(partners))

    m_s1p = [remote(tcol((x + 2) % 4, i), r1p.at[i], on_x(1)) for i in range(4)]
    m_s1m = [remote(tcol((x + 2) % 4, 4 + i), r1m.at[i], on_x(3)) for i in range(4)]
    m_dp = [remote(tcol((x + 1) % 4, 4 + i), rdp.at[i], on_x(1)) for i in range(4)]
    m_dm = [remote(tcol((x + 3) % 4, i), rdm.at[i], on_x(3)) for i in range(4)]
    m_s2p = [remote(r1p.at[i], r2p.at[i], on_x(1)) for i in range(4)]
    m_s2m = [remote(r1m.at[i], r2m.at[i], on_x(3)) for i in range(4)]
    m_ta = [remote(tt.at[i], tx.at[0, i], nxt) for i in range(4)]
    m_tb = [remote(tt.at[4 + i], tx.at[1, i], prv) for i in range(4)]
    m_x = remote(xin, xb.at[core], mate)

    def block(dy, dz):
        return ((zl + dz) % 4) * 4 + (y + dy) % 4

    def gather_messages(kind):
        base, rows = ((0, 96), (96, 160))[kind]

        def at(dp_, dq_):
            return block(dq_, dp_) if kind == 0 else block(dp_, dq_)

        def to(which, sign):
            on_z_axis = (kind == 0) == (which == "p")
            k = 1 if sign > 0 else -1
            return on_z(k % 8) if on_z_axis else on_y(k % 4)

        def piece(dp_, dq_, part):
            start, size = {"all": (0, rows), "lo": (0, rows // 2), "hi": (rows // 2, rows // 2)}[part]
            b = at(dp_, dq_)
            return wb.at[b, pl.ds(base + start, size)]

        def message(dp_, dq_, part, which, sign):
            ref = piece(dp_, dq_, part)
            return remote(ref, ref, to(which, sign))

        own = win.at[pl.ds(base, rows), pl.ds(col0, 512)]

        def first(which, sign):
            return remote(own, piece(0, 0, "all"), to(which, sign))

        return [
            first("p", 1), first("p", -1), first("q", 1), first("q", -1),
            message(-1, 0, "lo", "p", 1), message(1, 0, "hi", "p", -1),
            message(-1, 0, "all", "q", 1), message(-1, 0, "all", "q", -1),
            message(1, 0, "all", "q", 1), message(1, 0, "all", "q", -1),
            message(0, -1, "lo", "q", 1), message(0, 1, "hi", "q", -1),
            message(2, 0, "all", "q", 1), message(2, 0, "all", "q", -1),
            message(-1, -1, "lo", "q", 1), message(-1, 1, "hi", "q", -1),
            message(1, -1, "lo", "q", 1), message(1, 1, "hi", "q", -1),
            message(2, -1, "lo", "q", 1), message(2, 1, "hi", "q", -1),
        ]

    ag = [gather_messages(0), gather_messages(1)]

    def ag_start(*ids):
        for k in ids:
            for kind in (0, 1):
                go(ag[kind][k])

    def ag_wait(*ids):
        for k in ids:
            for kind in (0, 1):
                ag[kind][k].wait_recv()

    go(m_s1p[0]); go(m_s1m[0])
    ag_start(0, 1)
    go(m_s1p[1]); go(m_s1m[1]); go(m_dp[0]); go(m_dm[0])
    ag_start(2, 3)
    go(m_x)

    window = ctx
    valid = valid_ref[0]

    def seg_row(w):
        return seg_ref[:, pl.ds(pl.multiple_of(w * 256, 256), 256)].astype(F32)

    row_own = seg_row(window)
    row_next = seg_row((window + 1) % 16)
    col_own = jnp.transpose(jnp.broadcast_to(row_own, (256, 256)))
    col_prev = jnp.transpose(jnp.broadcast_to(seg_row((window + 15) % 16), (256, 256)))
    key_iota = lax.broadcasted_iota(jnp.int32, (256, 256), 0)
    query_iota = lax.broadcasted_iota(jnp.int32, (256, 256), 1)
    key_own = key_iota + window * 256
    key_prev = key_own - 256
    query_next = query_iota + (window + 1) * 256
    mo[...] = jnp.where((col_own == row_own) & (key_own < valid), 0.0, NEG)
    mp[...] = jnp.where((col_prev == row_own) & (key_prev >= 0) & (key_prev < valid), 0.0, NEG)
    mn[...] = jnp.where((col_own == row_next) & (key_own < valid) & (query_next < 4096), 0.0, NEG)
    lane = lax.broadcasted_iota(jnp.int32, (1, 256), 1)
    live_own = jnp.where(lane + window * 256 < valid, 1.0, 0.0).astype(F32)
    live_next = jnp.where(
        (lane + (window + 1) * 256 < valid) & (lane + (window + 1) * 256 < 4096), 1.0, 0.0
    ).astype(F32)

    acc[...] = jnp.zeros_like(acc)

    def feed(dy, dz):
        b = block(dy, dz)
        xs = xb[:, :, pl.ds(pl.multiple_of(b * 256, 256), 256)].reshape(512, 256)
        acc[...] += dot_nn(xs, wb[b])

    def relay(i):
        m_s1p[i].wait_recv()
        fp_loc[i].wait()
        r1p[i] = (r1p[i].astype(F32) + t_fp[i].astype(F32)).astype(BF16)
        go(m_s2p[i])
        m_s1m[i].wait_recv()
        fm_loc[i].wait()
        r1m[i] = (r1m[i].astype(F32) + t_fm[i].astype(F32)).astype(BF16)
        go(m_s2m[i])

    def settle(i):
        m_s2p[i].wait_recv()
        m_dm[i].wait_recv()
        own_loc[i].wait()
        tt[i] = (t_own[i].astype(F32) + r2p[i].astype(F32) + rdm[i].astype(F32)).astype(BF16)
        go_if(has_next, m_ta[i])
        m_s2m[i].wait_recv()
        m_dp[i].wait_recv()
        own_loc[4 + i].wait()
        tt[4 + i] = (
            t_own[4 + i].astype(F32) + r2m[i].astype(F32) + rdp[i].astype(F32)
        ).astype(BF16)
        go_if(has_prev, m_tb[i])

    ag_wait(0, 1)
    ag_start(4, 5, 6, 7, 8, 9)
    relay(0)
    go(m_s1p[2]); go(m_s1m[2]); go(m_dp[1]); go(m_dm[1])
    ag_wait(2, 3)
    ag_start(10, 11)
    x_loc.wait()
    w_loc.wait()
    m_x.wait_recv()
    feed(0, 0)
    relay(1)
    go(m_s1p[3]); go(m_s1m[3]); go(m_dp[2]); go(m_dm[2])
    ag_wait(4, 5)
    ag_start(12, 13)
    feed(1, 0)
    feed(-1, 0)
    feed(0, 1)
    feed(0, -1)
    ag_wait(6, 7, 8, 9)
    ag_start(14, 15, 16, 17)
    settle(0)
    relay(2)
    go(m_dp[3]); go(m_dm[3])
    feed(1, 1)
    feed(-1, 1)
    feed(1, -1)
    feed(-1, -1)
    ag_wait(12, 13)
    ag_start(18, 19)
    ag_wait(10, 11)
    feed(2, 0)
    feed(0, 2)
    settle(1)
    ag_wait(14, 15, 16, 17)
    feed(2, 1)
    feed(2, -1)
    feed(1, 2)
    feed(-1, 2)
    relay(3)
    ag_wait(18, 19)
    feed(2, 2)

    m_so = remote(so, ss.at[pl.ds(core * 4, 4)], mate)

    def half_to(f):
        up = 1 - f
        y_ = (y + 1 + 2 * f) % 4
        z_ = (z + up * ((y + 1) // 4) + f * (7 + (y + 3) // 4)) % 8
        return dev(x, y_, z_, core)

    k_half = sems[0]
    sems[0] += 8

    def half_copy(f, j):
        k = k_half + f * 4 + j
        return pltpu.make_async_remote_copy(
            src_ref=ss.at[f * 4 + j], dst_ref=sx.at[f, j], send_sem=send_sem.at[k],
            recv_sem=recv_sem.at[k], device_id=half_to(f), device_id_type=MESH,
        )

    acc_own = acc[pl.ds(pl.multiple_of(core * 256, 256), 256), :].astype(BF16)
    acc_oth = acc[pl.ds(pl.multiple_of(other * 256, 256), 256), :].astype(BF16)
    for j in range(4):
        so[j] = acc_oth[:, j * 128:(j + 1) * 128]
    go(m_so)
    for j in range(4):
        ss[core * 4 + j] = acc_own[:, j * 128:(j + 1) * 128]
        go_if(core * ctx + other * (15 - ctx) > 0, half_copy(core, j))
    for j in range(4):
        st[core * 4 + j] = turned(acc_own[:, j * 128:(j + 1) * 128])
    m_so.wait_recv()
    for j in range(4):
        go_if(other * ctx + core * (15 - ctx) > 0, half_copy(other, j))

    def teacher_a(i):
        recv_if(has_prev, m_ta[i])
        q = tt[i]
        own = dot_nt(q, q) * T_SCALE + mo[...]
        off = dot_nt(tx[0, i], q) * T_SCALE + mp[...]
        top = jnp.maximum(jnp.max(own, 0, keepdims=True), jnp.max(off, 0, keepdims=True))
        own = own - top
        off = off - top
        zt[i, 0] = own
        zt[i, 1] = off
        total = jnp.sum(jnp.exp(own), 0, keepdims=True) + jnp.sum(jnp.exp(off), 0, keepdims=True)
        lt[i:i + 1] = jnp.log(total)

    def b_stats(own, off, i, row):
        top = jnp.max(own, 0, keepdims=True)
        own = own - top
        st_d[i, row:row + 1] = top
        st_d[i, row + 1:row + 2] = jnp.sum(jnp.exp(own), 0, keepdims=True)
        top = jnp.max(off, 0, keepdims=True)
        off = off - top
        st_n[i, row:row + 1] = top
        st_n[i, row + 1:row + 2] = jnp.sum(jnp.exp(off), 0, keepdims=True)
        return own, off

    def teacher_b(i):
        recv_if(has_next, m_tb[i])
        k = tt[4 + i]
        own = dot_nt(k, k) * T_SCALE + mo[...]
        off = dot_nt(k, tx[1, i]) * T_SCALE + mn[...]
        zt[4 + i, 0], zt[4 + i, 1] = b_stats(own, off, i, 0)

    m_sd = [remote(st_d.at[i], rs_d.at[i], prv) for i in range(4)]
    m_sn = [remote(st_n.at[i], rs_n.at[i], nxt) for i in range(4)]

    def student_b(i):
        recv_if(has_next, half_copy(1, i))
        k = ss[4 + i]
        own = dot_nt(k, k) * S_SCALE + mo[...]
        off = dot_nt(k, sx[1, i]) * S_SCALE + mn[...]
        zs[i, 0], zs[i, 1] = b_stats(own, off, i, 2)
        go_if(has_prev, m_sd[i])
        go_if(has_next, m_sn[i])
        sxt[1, i] = turned(sx[1, i])

    def turn_own(j):
        st[other * 4 + j] = turned(ss[other * 4 + j])

    gain_own = live_own * G_SCALE
    gain_next = live_next * G_SCALE

    def grads(t_log, s_log, live, gain):
        t_prob = jnp.exp(t_log)
        s_prob = jnp.exp(s_log)
        loss = jnp.sum(t_prob * (t_log - s_log), 0, keepdims=True) * live
        return loss, ((s_prob - t_prob) * gain).astype(BF16)

    m_h = [remote(hsend.at[i], hrecv.at[i], prv if i < 4 else nxt) for i in range(8)]
    losses = []

    def relate_a(i):
        recv_if(has_prev, half_copy(0, i))
        sxt[0, i] = turned(sx[0, i])
        q = ss[i]
        own = dot_nt(q, q) * S_SCALE + mo[...]
        off = dot_nt(sx[0, i], q) * S_SCALE + mp[...]
        top = jnp.maximum(jnp.max(own, 0, keepdims=True), jnp.max(off, 0, keepdims=True))
        own = own - top
        off = off - top
        total = jnp.sum(jnp.exp(own), 0, keepdims=True) + jnp.sum(jnp.exp(off), 0, keepdims=True)
        s_sum = jnp.log(total)
        t_sum = lt[i:i + 1]
        loss_o, g_own = grads(zt[i, 0] - t_sum, own - s_sum, live_own, gain_own)
        loss_p, g_off = grads(zt[i, 1] - t_sum, off - s_sum, live_own, gain_own)
        losses.append(loss_o + loss_p)
        turned_q = st[i]
        hsend[i] = dot_nt(turned_q, g_off).astype(BF16)
        go_if(has_prev, m_h[i])
        hacc[i] = dot_nn(sxt[0, i], g_off) + dot_nn(turned_q, g_own) + dot_nt(turned_q, g_own)

    def shifts(m_here, l_here, m_there, l_there):
        top = jnp.maximum(m_here, m_there)
        total = l_here * jnp.exp(m_here - top) + l_there * jnp.exp(m_there - top)
        return (m_here - top) - jnp.log(total)

    def relate_b(i):
        recv_if(has_next, m_sd[i])
        recv_if(has_prev, m_sn[i])

        def row(ref, r):
            return ref[i, r:r + 1]

        t_own = shifts(row(st_d, 0), row(st_d, 1), row(rs_n, 0), row(rs_n, 1))
        s_own = shifts(row(st_d, 2), row(st_d, 3), row(rs_n, 2), row(rs_n, 3))
        t_off = shifts(row(st_n, 0), row(st_n, 1), row(rs_d, 0), row(rs_d, 1))
        s_off = shifts(row(st_n, 2), row(st_n, 3), row(rs_d, 2), row(rs_d, 3))
        loss_o, g_own = grads(zt[4 + i, 0] + t_own, zs[i, 0] + s_own, live_own, gain_own)
        loss_n, g_off = grads(zt[4 + i, 1] + t_off, zs[i, 1] + s_off, live_next, gain_next)
        losses.append(loss_o + loss_n)
        turned_k = st[4 + i]
        hsend[4 + i] = dot_nn(turned_k, g_off).astype(BF16)
        go_if(has_next, m_h[4 + i])
        hacc[4 + i] = dot_nn(turned_k, g_own) + dot_nt(turned_k, g_own) + dot_nt(sxt[1, i], g_off)

    def finish_one(i):
        recv_if(has_next if i < 4 else has_prev, m_h[i])
        full = (hacc[i] + hrecv[i].astype(F32)).astype(BF16)
        ht[i] = full
        return full

    m_ho = [remote(ht.at[other * 4 + j], ho.at[j], mate) for j in range(4)]

    def finish(j):
        low = finish_one(j)
        high = finish_one(4 + j)
        go(m_ho[j])
        h_out[:, j * 128:(j + 1) * 128] = turned(low)
        h_out[:, (4 + j) * 128:(5 + j) * 128] = turned(high)

    first_y = [True, False, True, True]

    def chunk(j):
        m_ho[j].wait_recv()
        mine = ht[core * 4 + j]
        theirs = ho[j]
        for k in range(4):
            part = dot_nn(mine, xb[core, :, k * 1024:(k + 1) * 1024])
            part = part + dot_nn(theirs, xb[other, :, k * 1024:(k + 1) * 1024])
            part = part.astype(BF16)
            for m in range(4):
                piece = part[:, m * 256:(m + 1) * 256]
                if first_y[j]:
                    gb[j, m, k] = piece
                else:
                    gb[j, k, m] = piece

    class Ring:
        def __init__(self, j, along_y, unit, bufs, halves):
            self.me = y if along_y else zl
            up = on_y(1) if along_y else on_z(1)
            down = on_y(3) if along_y else on_z(7)
            self.unit, self.halves = unit, halves
            self.b1p, self.b1m, self.bdp, self.bdm, self.b2p, self.b2m = [b.at[j] for b in bufs]
            lo, hi = halves
            self.s1p = remote(self.at(2, lo), self.b1p, up)
            self.s1m = remote(self.at(2, hi), self.b1m, down)
            self.dp = remote(self.at(1, hi), self.bdp, up)
            self.dm = remote(self.at(3, lo), self.bdm, down)
            self.s2p = remote(self.b1p, self.b2p, up)
            self.s2m = remote(self.b1m, self.b2m, down)

        def at(self, k, half):
            return self.unit.at[(self.me + k) % 4].at[half]

        def far(self):
            go(self.s1p); go(self.s1m)

        def near(self):
            go(self.dp); go(self.dm)

        def middle(self):
            lo, hi = self.halves
            self.s1p.wait_recv()
            self.b1p[...] = (
                self.b1p[...].astype(F32) + self.at(1, lo)[...].astype(F32)
            ).astype(BF16)
            go(self.s2p)
            self.s1m.wait_recv()
            self.b1m[...] = (
                self.b1m[...].astype(F32) + self.at(3, hi)[...].astype(F32)
            ).astype(BF16)
            go(self.s2m)

        def close(self, dst):
            lo, hi = self.halves
            self.s2p.wait_recv()
            self.dm.wait_recv()
            dst.at[lo][...] = (
                self.at(0, lo)[...].astype(F32) + self.b2p[...].astype(F32)
                + self.bdm[...].astype(F32)
            ).astype(BF16)
            self.s2m.wait_recv()
            self.dp.wait_recv()
            dst.at[hi][...] = (
                self.at(0, hi)[...].astype(F32) + self.b2m[...].astype(F32)
                + self.bdp[...].astype(F32)
            ).astype(BF16)

    p_ring = [
        Ring(j, first_y[j], gb.at[j], (p1p, p1m, pdp, pdm, p2p, p2m), (pl.ds(0, 2), pl.ds(2, 2)))
        for j in range(4)
    ]
    q_ring = [
        Ring(j, not first_y[j], qb.at[j], (q1p, q1m, qdp, qdm, q2p, q2m),
             (pl.ds(0, 64), pl.ds(64, 64)))
        for j in range(4)
    ]
    m_fin = [remote(fin.at[j], fin_r.at[j], on_z(4)) for j in range(4)]
    m_gf = [remote(gf.at[j], gf_r.at[j], mate) for j in range(4)]

    def to_q(j):
        p_ring[j].close(qb.at[j])
        q_ring[j].far()
        q_ring[j].near()

    def to_pair(j):
        q_ring[j].close(fin.at[j])
        go(m_fin[j])

    def total(j):
        m_fin[j].wait_recv()
        gf[j] = fin[j].astype(F32) + fin_r[j].astype(F32)
        go(m_gf[j])
        gt_out[:, pl.ds(pl.multiple_of(core * 512 + j * 128, 128), 128)] = jnp.transpose(gf[j])

    def emit(j):
        m_gf[j].wait_recv()
        gt_out[:, pl.ds(pl.multiple_of(other * 512 + j * 128, 128), 128)] = jnp.transpose(gf_r[j])

    def spread(buf, me, where):
        return [go(remote(buf.at[me], buf.at[me], where(k))) for k in (1, 2, 3)]

    def gathered(copies, buf):
        for copy in copies:
            copy.wait_recv()
        return buf[0] + buf[1] + buf[2] + buf[3]

    settle(2)
    teacher_a(0)
    teacher_b(0)
    student_b(0)
    teacher_b(1)
    student_b(1)
    for j in range(4):
        turn_own(j)
    relate_a(0)
    teacher_a(1)
    relate_a(1)
    relate_b(0)
    relate_b(1)
    teacher_b(2)
    student_b(2)
    settle(3)
    teacher_a(2)
    relate_a(2)
    finish(0)
    relate_b(2)
    finish(1)
    teacher_b(3)
    student_b(3)
    teacher_a(3)
    relate_a(3)
    chunk(0)
    p_ring[0].far()
    finish(2)
    chunk(1)
    p_ring[1].far()
    p_ring[1].near()
    relate_b(3)
    p_ring[0].near()
    chunk(2)
    p_ring[2].far()
    loss = losses[0]
    for part in losses[1:]:
        loss = loss + part
    loss = jnp.sum(loss, keepdims=True) * (1.0 / HEADS)
    lx[x] = jnp.broadcast_to(loss, (8, 128))
    c_x = spread(lx, x, on_x)
    p_ring[0].middle()
    p_ring[2].near()
    finish(3)
    chunk(3)
    p_ring[3].far()
    p_ring[1].middle()
    p_ring[2].middle()
    p_ring[3].near()
    to_q(0)
    to_q(1)
    p_ring[3].middle()
    ly[y] = gathered(c_x, lx)
    c_y = spread(ly, y, on_y)
    q_ring[0].middle()
    q_ring[1].middle()
    to_q(2)
    to_pair(0)
    to_pair(1)
    q_ring[2].middle()
    to_q(3)
    to_pair(2)
    lz[zl] = gathered(c_y, ly)
    c_z = spread(lz, zl, on_zl)
    q_ring[3].middle()
    total(0)
    total(1)
    emit(0)
    to_pair(3)
    emit(1)
    total(2)
    emit(2)
    loss_out[...] = gathered(c_z, lz)
    total(3)
    emit(3)
    for copy in pending:
        copy.wait_send()
    for cond, copy in guarded:

        @pl.when(cond)
        def _():
            copy.wait_send()


def results(h_ref, g_ref, l_ref, loss_ref, wo_ref, state_ref):
    loss_ref[0] = jnp.max(l_ref[0:1, 0:1])
    wo_ref[...] = g_ref[...]
    state_ref[...] = h_ref[...].astype(F32) * UNSCALE


def per_device(teacher_part, student_in, out_proj, segment_ids, valid_count):
    anywhere = pl.BlockSpec(memory_space=pltpu.HBM)
    vmem = pl.BlockSpec(memory_space=pltpu.VMEM)

    def b(*shape):
        return pltpu.VMEM(shape, BF16)

    def f(*shape):
        return pltpu.VMEM(shape, F32)

    scratch = [b(2, 256, 4096), b(16, 256, 512), f(512, 512)]
    scratch += [b(8, 256, 256)] + [b(4, 256, 256)] * 8 + [b(8, 256, 256), b(2, 4, 256, 256)]
    scratch += [b(8, 256, 128), b(4, 256, 128), b(2, 4, 256, 128), b(8, 128, 256), b(2, 4, 128, 256)]
    scratch += [f(256, 256)] * 3 + [f(8, 2, 256, 256), f(8, 256), f(4, 2, 256, 256)]
    scratch += [f(4, 4, 256)] * 4
    scratch += [f(8, 128, 256)] + [b(8, 128, 256)] * 3 + [b(4, 128, 256)]
    scratch += [b(4, 4, 4, 128, 256)] + [b(4, 2, 128, 256)] * 6
    scratch += [b(4, 4, 128, 256)] + [b(4, 64, 256)] * 6
    scratch += [b(4, 128, 256)] * 2 + [f(4, 128, 256)] * 2
    scratch += [f(4, 8, 128)] * 3
    scratch += [
        pltpu.SemaphoreType.DMA((N_SEM,)), pltpu.SemaphoreType.DMA((N_SEM,)),
        pltpu.SemaphoreType.DMA((24,)),
    ]
    hidden_grad, wo_grad, loss = pl.pallas_call(
        kernel,
        out_shape=(
            jax.ShapeDtypeStruct((256, 1024), BF16),
            jax.ShapeDtypeStruct((256, 1024), F32),
            jax.ShapeDtypeStruct((8, 128), F32),
        ),
        in_specs=[anywhere, anywhere, anywhere, vmem, pl.BlockSpec(memory_space=pltpu.SMEM)],
        out_specs=(vmem, vmem, vmem),
        scratch_shapes=scratch,
        name="relation_step",
        compiler_params=pltpu.CompilerParams(
            collective_id=0, has_side_effects=True, vmem_limit_bytes=60 * 2**20
        ),
    )(teacher_part[0, 0], student_in[0], out_proj, segment_ids, valid_count)
    doc_loss, wo_grad, state_grad = pl.pallas_call(
        results,
        out_shape=(
            jax.ShapeDtypeStruct((1,), F32),
            jax.ShapeDtypeStruct((256, 1024), F32),
            jax.ShapeDtypeStruct((256, 1024), F32),
        ),
        in_specs=[vmem, vmem, vmem],
        out_specs=(pl.BlockSpec(memory_space=pltpu.SMEM), vmem, vmem),
        name="results",
        compiler_params=pltpu.CompilerParams(vmem_limit_bytes=16 * 2**20),
    )(hidden_grad, wo_grad, loss)
    return (doc_loss, wo_grad, state_grad[None])


def solution(mesh):
    return jax.shard_map(
        per_device,
        mesh=mesh,
        in_specs=(
            P("dp", "tp", "ctx", None),
            P("dp", "ctx", None),
            P("ctx", "tp"),
            P("dp", None),
            P("dp"),
        ),
        out_specs=(P("dp"), P("ctx", "tp"), P("dp", "ctx", "tp")),
        check_vma=False,
    )
```

```python
import math

import jax
import jax.numpy as jnp
from jax import lax
from jax.experimental import pallas as pl
from jax.experimental.pallas import tpu as pltpu
from jax.sharding import PartitionSpec as P

DS = 4096
HEADS = 32
MESH = pl.DeviceIdType.MESH
F32 = jnp.float32
BF16 = jnp.bfloat16
NEG = -1e30
UNSCALE = HEADS * math.sqrt(DS // HEADS)
T_SCALE = 1.0 / math.sqrt(256)
S_SCALE = 1.0 / math.sqrt(128)
G_SCALE = S_SCALE / HEADS
N_SEM = 224


def dot_nn(a, b):
    return lax.dot_general(a, b, (((1,), (0,)), ((), ())), preferred_element_type=F32)


def dot_nt(a, b):
    return lax.dot_general(a, b, (((1,), (1,)), ((), ())), preferred_element_type=F32)


def turned(a):
    return jnp.transpose(a.astype(F32)).astype(BF16)


def neutral_rows():
    return jnp.where(lax.broadcasted_iota(jnp.int32, (4, 256), 0) % 2 == 0, NEG, 0.0).astype(F32)


def kernel(
    tpart, xin, win, seg_ref, valid_ref,
    h_out, gt_out, loss_out,
    xb, wb, acc,
    t_own, t_fp, t_fm, r1p, r1m, rdp, rdm, r2p, r2m, tt, tx,
    ss, so, sx, st, sxt,
    mo, mp, mn, zt, lt, zs, st_d, st_n, rs_d, rs_n,
    hacc, hsend, hrecv, ht, ho,
    gb, p1p, p1m, pdp, pdm, p2p, p2m, qb, q1p, q1m, qdp, qdm, q2p, q2m, fin, fin_r, gf, gf_r,
    lx, ly, lz,
    send_sem, recv_sem, loc_sem,
):
    dp, ctx, x = lax.axis_index("dp"), lax.axis_index("ctx"), lax.axis_index("tp")
    core, zh, zl, y = dp % 2, dp // 2, ctx // 4, ctx % 4
    z = zh * 4 + zl
    other = 1 - core

    def dev(x_, y_, z_, c_):
        return ((z_ // 4) * 2 + c_, (z_ % 4) * 4 + y_, x_)

    def on_x(k):
        return dev((x + k) % 4, y, z, core)

    def on_y(k):
        return dev(x, (y + k) % 4, z, core)

    def on_z(k):
        return dev(x, y, (z + k) % 8, core)

    def on_zl(k):
        return dev(x, y, zh * 4 + (zl + k) % 4, core)

    mate = dev(x, y, z, other)
    nxt = dev(x, (y + 1) % 4, (z + (y + 1) // 4) % 8, core)
    prv = dev(x, (y + 3) % 4, (z + 7 + (y + 3) // 4) % 8, core)

    partners = [on_x(1), on_x(3), on_y(1), on_y(3), on_z(1), on_z(7), mate]

    sems = [0]
    pending = []

    def remote(src, dst, where):
        k = sems[0]
        sems[0] += 1
        return pltpu.make_async_remote_copy(
            src_ref=src, dst_ref=dst, send_sem=send_sem.at[k], recv_sem=recv_sem.at[k],
            device_id=where, device_id_type=MESH,
        )

    def go(copy):
        copy.start()
        pending.append(copy)
        return copy

    has_next, has_prev = ctx < 15, ctx > 0
    guarded = []

    def go_if(cond, copy):
        guarded.append((cond, copy))

        @pl.when(cond)
        def _():
            copy.start()

    def recv_if(cond, copy):
        @pl.when(cond)
        def _():
            copy.wait_recv()

    @pl.when(ctx == 0)
    def _():
        tx[0] = jnp.zeros_like(tx[0])
        sx[0] = jnp.zeros_like(sx[0])
        for i in range(4):
            rs_n[i] = neutral_rows()
            hrecv[4 + i] = jnp.zeros_like(hrecv[4 + i])

    @pl.when(ctx == 15)
    def _():
        tx[1] = jnp.zeros_like(tx[1])
        sx[1] = jnp.zeros_like(sx[1])
        for i in range(4):
            rs_d[i] = neutral_rows()
            hrecv[i] = jnp.zeros_like(hrecv[i])

    locs = [0]

    def local(src, dst):
        k = locs[0]
        locs[0] += 1
        copy = pltpu.make_async_copy(src, dst, loc_sem.at[k])
        copy.start()
        return copy

    x_loc = local(xin, xb.at[core])
    col0 = pl.multiple_of(core * 512, 512)
    w_loc = local(win.at[:, pl.ds(col0, 512)], wb.at[ctx])

    def tcol(block, head):
        return tpart.at[:, pl.ds(pl.multiple_of(block * 2048 + head * 256, 256), 256)]

    fp_loc = [local(tcol((x + 1) % 4, i), t_fp.at[i]) for i in range(4)]
    fm_loc = [local(tcol((x + 3) % 4, 4 + i), t_fm.at[i]) for i in range(4)]
    own_loc = [local(tcol(x, i), t_own.at[i]) for i in range(8)]

    barrier = pltpu.get_barrier_semaphore()
    for where in partners:
        pl.semaphore_signal(barrier, inc=1, device_id=where, device_id_type=MESH)
    pl.semaphore_wait(barrier, len(partners))

    m_s1p = [remote(tcol((x + 2) % 4, i), r1p.at[i], on_x(1)) for i in range(4)]
    m_s1m = [remote(tcol((x + 2) % 4, 4 + i), r1m.at[i], on_x(3)) for i in range(4)]
    m_dp = [remote(tcol((x + 1) % 4, 4 + i), rdp.at[i], on_x(1)) for i in range(4)]
    m_dm = [remote(tcol((x + 3) % 4, i), rdm.at[i], on_x(3)) for i in range(4)]
    m_s2p = [remote(r1p.at[i], r2p.at[i], on_x(1)) for i in range(4)]
    m_s2m = [remote(r1m.at[i], r2m.at[i], on_x(3)) for i in range(4)]
    m_ta = [remote(tt.at[i], tx.at[0, i], nxt) for i in range(4)]
    m_tb = [remote(tt.at[4 + i], tx.at[1, i], prv) for i in range(4)]
    m_x = remote(xin, xb.at[core], mate)

    def block(dy, dz):
        return ((zl + dz) % 4) * 4 + (y + dy) % 4

    def gather_messages(kind):
        base, rows = ((0, 96), (96, 160))[kind]

        def at(dp_, dq_):
            return block(dq_, dp_) if kind == 0 else block(dp_, dq_)

        def to(which, sign):
            on_z_axis = (kind == 0) == (which == "p")
            k = 1 if sign > 0 else -1
            return on_z(k % 8) if on_z_axis else on_y(k % 4)

        def piece(dp_, dq_, part):
            start, size = {"all": (0, rows), "lo": (0, rows // 2), "hi": (rows // 2, rows // 2)}[part]
            b = at(dp_, dq_)
            return wb.at[b, pl.ds(base + start, size)]

        def message(dp_, dq_, part, which, sign):
            ref = piece(dp_, dq_, part)
            return remote(ref, ref, to(which, sign))

        own = win.at[pl.ds(base, rows), pl.ds(col0, 512)]

        def first(which, sign):
            return remote(own, piece(0, 0, "all"), to(which, sign))

        return [
            first("p", 1), first("p", -1), first("q", 1), first("q", -1),
            message(-1, 0, "lo", "p", 1), message(1, 0, "hi", "p", -1),
            message(-1, 0, "all", "q", 1), message(-1, 0, "all", "q", -1),
            message(1, 0, "all", "q", 1), message(1, 0, "all", "q", -1),
            message(0, -1, "lo", "q", 1), message(0, 1, "hi", "q", -1),
            message(2, 0, "all", "q", 1), message(2, 0, "all", "q", -1),
            message(-1, -1, "lo", "q", 1), message(-1, 1, "hi", "q", -1),
            message(1, -1, "lo", "q", 1), message(1, 1, "hi", "q", -1),
            message(2, -1, "lo", "q", 1), message(2, 1, "hi", "q", -1),
        ]

    ag = [gather_messages(0), gather_messages(1)]

    def ag_start(*ids):
        for k in ids:
            for kind in (0, 1):
                go(ag[kind][k])

    def ag_wait(*ids):
        for k in ids:
            for kind in (0, 1):
                ag[kind][k].wait_recv()

    go(m_s1p[0]); go(m_s1m[0])
    ag_start(0, 1)
    go(m_s1p[1]); go(m_s1m[1]); go(m_dp[0]); go(m_dm[0])
    ag_start(2, 3)
    go(m_x)

    window = ctx
    valid = valid_ref[0]

    def seg_row(w):
        return seg_ref[:, pl.ds(pl.multiple_of(w * 256, 256), 256)].astype(F32)

    row_own = seg_row(window)
    row_next = seg_row((window + 1) % 16)
    col_own = jnp.transpose(jnp.broadcast_to(row_own, (256, 256)))
    col_prev = jnp.transpose(jnp.broadcast_to(seg_row((window + 15) % 16), (256, 256)))
    key_iota = lax.broadcasted_iota(jnp.int32, (256, 256), 0)
    query_iota = lax.broadcasted_iota(jnp.int32, (256, 256), 1)
    key_own = key_iota + window * 256
    key_prev = key_own - 256
    query_next = query_iota + (window + 1) * 256
    mo[...] = jnp.where((col_own == row_own) & (key_own < valid), 0.0, NEG)
    mp[...] = jnp.where((col_prev == row_own) & (key_prev >= 0) & (key_prev < valid), 0.0, NEG)
    mn[...] = jnp.where((col_own == row_next) & (key_own < valid) & (query_next < 4096), 0.0, NEG)
    lane = lax.broadcasted_iota(jnp.int32, (1, 256), 1)
    live_own = jnp.where(lane + window * 256 < valid, 1.0, 0.0).astype(F32)
    live_next = jnp.where(
        (lane + (window + 1) * 256 < valid) & (lane + (window + 1) * 256 < 4096), 1.0, 0.0
    ).astype(F32)

    acc[...] = jnp.zeros_like(acc)

    def feed(dy, dz):
        b = block(dy, dz)
        xs = xb[:, :, pl.ds(pl.multiple_of(b * 256, 256), 256)].reshape(512, 256)
        acc[...] += dot_nn(xs, wb[b])

    def relay(i):
        m_s1p[i].wait_recv()
        fp_loc[i].wait()
        r1p[i] = (r1p[i].astype(F32) + t_fp[i].astype(F32)).astype(BF16)
        go(m_s2p[i])
        m_s1m[i].wait_recv()
        fm_loc[i].wait()
        r1m[i] = (r1m[i].astype(F32) + t_fm[i].astype(F32)).astype(BF16)
        go(m_s2m[i])

    def settle(i):
        m_s2p[i].wait_recv()
        m_dm[i].wait_recv()
        own_loc[i].wait()
        tt[i] = (t_own[i].astype(F32) + r2p[i].astype(F32) + rdm[i].astype(F32)).astype(BF16)
        go_if(has_next, m_ta[i])
        m_s2m[i].wait_recv()
        m_dp[i].wait_recv()
        own_loc[4 + i].wait()
        tt[4 + i] = (
            t_own[4 + i].astype(F32) + r2m[i].astype(F32) + rdp[i].astype(F32)
        ).astype(BF16)
        go_if(has_prev, m_tb[i])

    ag_wait(0, 1)
    ag_start(4, 5, 6, 7, 8, 9)
    relay(0)
    go(m_s1p[2]); go(m_s1m[2]); go(m_dp[1]); go(m_dm[1])
    ag_wait(2, 3)
    ag_start(10, 11)
    x_loc.wait()
    w_loc.wait()
    m_x.wait_recv()
    feed(0, 0)
    relay(1)
    go(m_s1p[3]); go(m_s1m[3]); go(m_dp[2]); go(m_dm[2])
    ag_wait(4, 5)
    ag_start(12, 13)
    feed(1, 0)
    feed(-1, 0)
    feed(0, 1)
    feed(0, -1)
    ag_wait(6, 7, 8, 9)
    ag_start(14, 15, 16, 17)
    settle(0)
    relay(2)
    go(m_dp[3]); go(m_dm[3])
    feed(1, 1)
    feed(-1, 1)
    feed(1, -1)
    feed(-1, -1)
    ag_wait(12, 13)
    ag_start(18, 19)
    ag_wait(10, 11)
    feed(2, 0)
    feed(0, 2)
    settle(1)
    ag_wait(14, 15, 16, 17)
    feed(2, 1)
    feed(2, -1)
    feed(1, 2)
    feed(-1, 2)
    relay(3)
    ag_wait(18, 19)
    feed(2, 2)

    m_so = remote(so, ss.at[pl.ds(core * 4, 4)], mate)

    def half_to(f):
        up = 1 - f
        y_ = (y + 1 + 2 * f) % 4
        z_ = (z + up * ((y + 1) // 4) + f * (7 + (y + 3) // 4)) % 8
        return dev(x, y_, z_, core)

    k_half = sems[0]
    sems[0] += 8

    def half_copy(f, j):
        k = k_half + f * 4 + j
        return pltpu.make_async_remote_copy(
            src_ref=ss.at[f * 4 + j], dst_ref=sx.at[f, j], send_sem=send_sem.at[k],
            recv_sem=recv_sem.at[k], device_id=half_to(f), device_id_type=MESH,
        )

    acc_own = acc[pl.ds(pl.multiple_of(core * 256, 256), 256), :].astype(BF16)
    acc_oth = acc[pl.ds(pl.multiple_of(other * 256, 256), 256), :].astype(BF16)
    for j in range(4):
        so[j] = acc_oth[:, j * 128:(j + 1) * 128]
    go(m_so)
    for j in range(4):
        ss[core * 4 + j] = acc_own[:, j * 128:(j + 1) * 128]
        go_if(core * ctx + other * (15 - ctx) > 0, half_copy(core, j))
    for j in range(4):
        st[core * 4 + j] = turned(acc_own[:, j * 128:(j + 1) * 128])
    m_so.wait_recv()
    for j in range(4):
        go_if(other * ctx + core * (15 - ctx) > 0, half_copy(other, j))

    def teacher_a(i):
        recv_if(has_prev, m_ta[i])
        q = tt[i]
        own = dot_nt(q, q) * T_SCALE + mo[...]
        off = dot_nt(tx[0, i], q) * T_SCALE + mp[...]
        top = jnp.maximum(jnp.max(own, 0, keepdims=True), jnp.max(off, 0, keepdims=True))
        own = own - top
        off = off - top
        zt[i, 0] = own
        zt[i, 1] = off
        total = jnp.sum(jnp.exp(own), 0, keepdims=True) + jnp.sum(jnp.exp(off), 0, keepdims=True)
        lt[i:i + 1] = jnp.log(total)

    def b_stats(own, off, i, row):
        top = jnp.max(own, 0, keepdims=True)
        own = own - top
        st_d[i, row:row + 1] = top
        st_d[i, row + 1:row + 2] = jnp.sum(jnp.exp(own), 0, keepdims=True)
        top = jnp.max(off, 0, keepdims=True)
        off = off - top
        st_n[i, row:row + 1] = top
        st_n[i, row + 1:row + 2] = jnp.sum(jnp.exp(off), 0, keepdims=True)
        return own, off

    def teacher_b(i):
        recv_if(has_next, m_tb[i])
        k = tt[4 + i]
        own = dot_nt(k, k) * T_SCALE + mo[...]
        off = dot_nt(k, tx[1, i]) * T_SCALE + mn[...]
        zt[4 + i, 0], zt[4 + i, 1] = b_stats(own, off, i, 0)

    m_sd = [remote(st_d.at[i], rs_d.at[i], prv) for i in range(4)]
    m_sn = [remote(st_n.at[i], rs_n.at[i], nxt) for i in range(4)]

    def student_b(i):
        recv_if(has_next, half_copy(1, i))
        k = ss[4 + i]
        own = dot_nt(k, k) * S_SCALE + mo[...]
        off = dot_nt(k, sx[1, i]) * S_SCALE + mn[...]
        zs[i, 0], zs[i, 1] = b_stats(own, off, i, 2)
        go_if(has_prev, m_sd[i])
        go_if(has_next, m_sn[i])
        sxt[1, i] = turned(sx[1, i])

    def turn_own(j):
        st[other * 4 + j] = turned(ss[other * 4 + j])

    gain_own = live_own * G_SCALE
    gain_next = live_next * G_SCALE

    def grads(t_log, s_log, live, gain):
        t_prob = jnp.exp(t_log)
        s_prob = jnp.exp(s_log)
        loss = jnp.sum(t_prob * (t_log - s_log), 0, keepdims=True) * live
        return loss, ((s_prob - t_prob) * gain).astype(BF16)

    m_h = [remote(hsend.at[i], hrecv.at[i], prv if i < 4 else nxt) for i in range(8)]
    losses = []

    def relate_a(i):
        recv_if(has_prev, half_copy(0, i))
        sxt[0, i] = turned(sx[0, i])
        q = ss[i]
        own = dot_nt(q, q) * S_SCALE + mo[...]
        off = dot_nt(sx[0, i], q) * S_SCALE + mp[...]
        top = jnp.maximum(jnp.max(own, 0, keepdims=True), jnp.max(off, 0, keepdims=True))
        own = own - top
        off = off - top
        total = jnp.sum(jnp.exp(own), 0, keepdims=True) + jnp.sum(jnp.exp(off), 0, keepdims=True)
        s_sum = jnp.log(total)
        t_sum = lt[i:i + 1]
        loss_o, g_own = grads(zt[i, 0] - t_sum, own - s_sum, live_own, gain_own)
        loss_p, g_off = grads(zt[i, 1] - t_sum, off - s_sum, live_own, gain_own)
        losses.append(loss_o + loss_p)
        turned_q = st[i]
        hsend[i] = dot_nt(turned_q, g_off).astype(BF16)
        go_if(has_prev, m_h[i])
        hacc[i] = dot_nn(sxt[0, i], g_off) + dot_nn(turned_q, g_own) + dot_nt(turned_q, g_own)

    def shifts(m_here, l_here, m_there, l_there):
        top = jnp.maximum(m_here, m_there)
        total = l_here * jnp.exp(m_here - top) + l_there * jnp.exp(m_there - top)
        return (m_here - top) - jnp.log(total)

    def relate_b(i):
        recv_if(has_next, m_sd[i])
        recv_if(has_prev, m_sn[i])

        def row(ref, r):
            return ref[i, r:r + 1]

        t_own = shifts(row(st_d, 0), row(st_d, 1), row(rs_n, 0), row(rs_n, 1))
        s_own = shifts(row(st_d, 2), row(st_d, 3), row(rs_n, 2), row(rs_n, 3))
        t_off = shifts(row(st_n, 0), row(st_n, 1), row(rs_d, 0), row(rs_d, 1))
        s_off = shifts(row(st_n, 2), row(st_n, 3), row(rs_d, 2), row(rs_d, 3))
        loss_o, g_own = grads(zt[4 + i, 0] + t_own, zs[i, 0] + s_own, live_own, gain_own)
        loss_n, g_off = grads(zt[4 + i, 1] + t_off, zs[i, 1] + s_off, live_next, gain_next)
        losses.append(loss_o + loss_n)
        turned_k = st[4 + i]
        hsend[4 + i] = dot_nn(turned_k, g_off).astype(BF16)
        go_if(has_next, m_h[4 + i])
        hacc[4 + i] = dot_nn(turned_k, g_own) + dot_nt(turned_k, g_own) + dot_nt(sxt[1, i], g_off)

    def finish_one(i):
        recv_if(has_next if i < 4 else has_prev, m_h[i])
        full = (hacc[i] + hrecv[i].astype(F32)).astype(BF16)
        ht[i] = full
        return full

    m_ho = [remote(ht.at[other * 4 + j], ho.at[j], mate) for j in range(4)]

    def finish(j):
        low = finish_one(j)
        high = finish_one(4 + j)
        go(m_ho[j])
        h_out[:, j * 128:(j + 1) * 128] = turned(low)
        h_out[:, (4 + j) * 128:(5 + j) * 128] = turned(high)

    first_y = [True, False, True, True]

    def chunk(j):
        m_ho[j].wait_recv()
        mine = ht[core * 4 + j]
        theirs = ho[j]
        for k in range(4):
            part = dot_nn(mine, xb[core, :, k * 1024:(k + 1) * 1024])
            part = part + dot_nn(theirs, xb[other, :, k * 1024:(k + 1) * 1024])
            part = part.astype(BF16)
            for m in range(4):
                piece = part[:, m * 256:(m + 1) * 256]
                if first_y[j]:
                    gb[j, m, k] = piece
                else:
                    gb[j, k, m] = piece

    class Ring:
        def __init__(self, j, along_y, unit, bufs, halves):
            self.me = y if along_y else zl
            up = on_y(1) if along_y else on_z(1)
            down = on_y(3) if along_y else on_z(7)
            self.unit, self.halves = unit, halves
            self.b1p, self.b1m, self.bdp, self.bdm, self.b2p, self.b2m = [b.at[j] for b in bufs]
            lo, hi = halves
            self.s1p = remote(self.at(2, lo), self.b1p, up)
            self.s1m = remote(self.at(2, hi), self.b1m, down)
            self.dp = remote(self.at(1, hi), self.bdp, up)
            self.dm = remote(self.at(3, lo), self.bdm, down)
            self.s2p = remote(self.b1p, self.b2p, up)
            self.s2m = remote(self.b1m, self.b2m, down)

        def at(self, k, half):
            return self.unit.at[(self.me + k) % 4].at[half]

        def far(self):
            go(self.s1p); go(self.s1m)

        def near(self):
            go(self.dp); go(self.dm)

        def middle(self):
            lo, hi = self.halves
            self.s1p.wait_recv()
            self.b1p[...] = (
                self.b1p[...].astype(F32) + self.at(1, lo)[...].astype(F32)
            ).astype(BF16)
            go(self.s2p)
            self.s1m.wait_recv()
            self.b1m[...] = (
                self.b1m[...].astype(F32) + self.at(3, hi)[...].astype(F32)
            ).astype(BF16)
            go(self.s2m)

        def close(self, dst):
            lo, hi = self.halves
            self.s2p.wait_recv()
            self.dm.wait_recv()
            dst.at[lo][...] = (
                self.at(0, lo)[...].astype(F32) + self.b2p[...].astype(F32)
                + self.bdm[...].astype(F32)
            ).astype(BF16)
            self.s2m.wait_recv()
            self.dp.wait_recv()
            dst.at[hi][...] = (
                self.at(0, hi)[...].astype(F32) + self.b2m[...].astype(F32)
                + self.bdp[...].astype(F32)
            ).astype(BF16)

    p_ring = [
        Ring(j, first_y[j], gb.at[j], (p1p, p1m, pdp, pdm, p2p, p2m), (pl.ds(0, 2), pl.ds(2, 2)))
        for j in range(4)
    ]
    q_ring = [
        Ring(j, not first_y[j], qb.at[j], (q1p, q1m, qdp, qdm, q2p, q2m),
             (pl.ds(0, 64), pl.ds(64, 64)))
        for j in range(4)
    ]
    m_fin = [remote(fin.at[j], fin_r.at[j], on_z(4)) for j in range(4)]
    m_gf = [remote(gf.at[j], gf_r.at[j], mate) for j in range(4)]

    def to_q(j):
        p_ring[j].close(qb.at[j])
        q_ring[j].far()
        q_ring[j].near()

    def to_pair(j):
        q_ring[j].close(fin.at[j])
        go(m_fin[j])

    def total(j):
        m_fin[j].wait_recv()
        gf[j] = fin[j].astype(F32) + fin_r[j].astype(F32)
        go(m_gf[j])
        gt_out[:, pl.ds(pl.multiple_of(core * 512 + j * 128, 128), 128)] = jnp.transpose(gf[j])

    def emit(j):
        m_gf[j].wait_recv()
        gt_out[:, pl.ds(pl.multiple_of(other * 512 + j * 128, 128), 128)] = jnp.transpose(gf_r[j])

    def spread(buf, me, where):
        return [go(remote(buf.at[me], buf.at[me], where(k))) for k in (1, 2, 3)]

    def gathered(copies, buf):
        for copy in copies:
            copy.wait_recv()
        return buf[0] + buf[1] + buf[2] + buf[3]

    settle(2)
    teacher_a(0)
    teacher_b(0)
    student_b(0)
    teacher_b(1)
    student_b(1)
    for j in range(4):
        turn_own(j)
    relate_a(0)
    teacher_a(1)
    relate_a(1)
    relate_b(0)
    relate_b(1)
    teacher_b(2)
    student_b(2)
    settle(3)
    teacher_a(2)
    relate_a(2)
    finish(0)
    relate_b(2)
    chunk(0)
    p_ring[0].far()
    finish(1)
    teacher_b(3)
    student_b(3)
    teacher_a(3)
    relate_a(3)
    finish(2)
    chunk(1)
    p_ring[1].far()
    relate_b(3)
    p_ring[1].near()
    p_ring[0].near()
    chunk(2)
    p_ring[2].far()
    loss = losses[0]
    for part in losses[1:]:
        loss = loss + part
    loss = jnp.sum(loss, keepdims=True) * (1.0 / HEADS)
    lx[x] = jnp.broadcast_to(loss, (8, 128))
    c_x = spread(lx, x, on_x)
    p_ring[0].middle()
    p_ring[2].near()
    finish(3)
    chunk(3)
    p_ring[3].far()
    p_ring[1].middle()
    p_ring[2].middle()
    p_ring[3].near()
    to_q(0)
    to_q(1)
    p_ring[3].middle()
    ly[y] = gathered(c_x, lx)
    c_y = spread(ly, y, on_y)
    q_ring[0].middle()
    q_ring[1].middle()
    to_q(2)
    to_pair(0)
    to_pair(1)
    q_ring[2].middle()
    to_q(3)
    to_pair(2)
    lz[zl] = gathered(c_y, ly)
    c_z = spread(lz, zl, on_zl)
    q_ring[3].middle()
    total(0)
    total(1)
    emit(0)
    to_pair(3)
    emit(1)
    total(2)
    emit(2)
    loss_out[...] = gathered(c_z, lz)
    total(3)
    emit(3)
    for copy in pending:
        copy.wait_send()
    for cond, copy in guarded:

        @pl.when(cond)
        def _():
            copy.wait_send()


def results(h_ref, g_ref, l_ref, loss_ref, wo_ref, state_ref):
    loss_ref[0] = jnp.max(l_ref[0:1, 0:1])
    wo_ref[...] = g_ref[...]
    state_ref[...] = h_ref[...].astype(F32) * UNSCALE


def per_device(teacher_part, student_in, out_proj, segment_ids, valid_count):
    anywhere = pl.BlockSpec(memory_space=pltpu.HBM)
    vmem = pl.BlockSpec(memory_space=pltpu.VMEM)

    def b(*shape):
        return pltpu.VMEM(shape, BF16)

    def f(*shape):
        return pltpu.VMEM(shape, F32)

    scratch = [b(2, 256, 4096), b(16, 256, 512), f(512, 512)]
    scratch += [b(8, 256, 256)] + [b(4, 256, 256)] * 8 + [b(8, 256, 256), b(2, 4, 256, 256)]
    scratch += [b(8, 256, 128), b(4, 256, 128), b(2, 4, 256, 128), b(8, 128, 256), b(2, 4, 128, 256)]
    scratch += [f(256, 256)] * 3 + [f(8, 2, 256, 256), f(8, 256), f(4, 2, 256, 256)]
    scratch += [f(4, 4, 256)] * 4
    scratch += [f(8, 128, 256)] + [b(8, 128, 256)] * 3 + [b(4, 128, 256)]
    scratch += [b(4, 4, 4, 128, 256)] + [b(4, 2, 128, 256)] * 6
    scratch += [b(4, 4, 128, 256)] + [b(4, 64, 256)] * 6
    scratch += [b(4, 128, 256)] * 2 + [f(4, 128, 256)] * 2
    scratch += [f(4, 8, 128)] * 3
    scratch += [
        pltpu.SemaphoreType.DMA((N_SEM,)), pltpu.SemaphoreType.DMA((N_SEM,)),
        pltpu.SemaphoreType.DMA((24,)),
    ]
    hidden_grad, wo_grad, loss = pl.pallas_call(
        kernel,
        out_shape=(
            jax.ShapeDtypeStruct((256, 1024), BF16),
            jax.ShapeDtypeStruct((256, 1024), F32),
            jax.ShapeDtypeStruct((8, 128), F32),
        ),
        in_specs=[anywhere, anywhere, anywhere, vmem, pl.BlockSpec(memory_space=pltpu.SMEM)],
        out_specs=(vmem, vmem, vmem),
        scratch_shapes=scratch,
        name="relation_step",
        compiler_params=pltpu.CompilerParams(
            collective_id=0, has_side_effects=True, vmem_limit_bytes=60 * 2**20
        ),
    )(teacher_part[0, 0], student_in[0], out_proj, segment_ids, valid_count)
    doc_loss, wo_grad, state_grad = pl.pallas_call(
        results,
        out_shape=(
            jax.ShapeDtypeStruct((1,), F32),
            jax.ShapeDtypeStruct((256, 1024), F32),
            jax.ShapeDtypeStruct((256, 1024), F32),
        ),
        in_specs=[vmem, vmem, vmem],
        out_specs=(pl.BlockSpec(memory_space=pltpu.SMEM), vmem, vmem),
        name="results",
        compiler_params=pltpu.CompilerParams(vmem_limit_bytes=60 * 2**20),
    )(hidden_grad, wo_grad, loss)
    return (doc_loss, wo_grad, state_grad[None])


def solution(mesh):
    return jax.shard_map(
        per_device,
        mesh=mesh,
        in_specs=(
            P("dp", "tp", "ctx", None),
            P("dp", "ctx", None),
            P("ctx", "tp"),
            P("dp", None),
            P("dp"),
        ),
        out_specs=(P("dp"), P("ctx", "tp"), P("dp", "ctx", "tp")),
        check_vma=False,
    )
```
